32 devices in a mesh: member: 2 (over y), win: 4 (over z), seq: 4 (over x, core).
Axes of the slice: x: 2, y: 2, z: 4, core: 2. Of those that a mesh axis runs over, the one named last changes fastest.
Arguments:
- pixel_grid_input: bfloat16 [8, 8, 4, 64, 1536], P(('member', 'win'), None, 'seq'), parts along dimension 0, may hold values from -6 to 6
- mask_zone_labeling: int32 [8, 32, 64], P(('member', 'win')), parts along dimension 0, may hold values from 0 to 8, as said below
- standardize_multiplier: float32 [1536], replicated, may hold values from 0.25 to 1.75
- standardize_offset_vector: float32 [1536], replicated, may hold values from -3 to 3
- triple_projection_matrix: bfloat16 [3, 1536, 1536], P(None, None, 'seq'), may hold values from -0.15625 to 0.15625
- logit_scaling_per_part: float32 [16], P('seq'), may hold values from 1 to 45
- final_projection_matrix: bfloat16 [1536, 1536], P('seq'), may hold values from -0.15625 to 0.15625
Outputs:
- mixed: bfloat16 [8, 8, 4, 64, 1536], P(('member', 'win'), None, 'seq'), parts along dimension 0
The draws below stay inside these ranges and needn't reach their ends.
There are 2 independent parts, one for each index of `member`. The reference program is written for one: setup_inputs(seed, part) draws one part's arguments, and reference() takes and returns one part's arrays. A program takes and returns all parts, laid end to end along the dimension named above; an argument that names none is the same for every part. Nothing has to cross between parts.
Inputs may be any that keep to these rules, and one draw needn't show every extreme that they name: `mask_zone_labeling`: region is 3 * (row band) + (column band) of the pixel on the rolled grid: the row band is 0 in the first 32 rows, 1 in the next rows and 2 in the last few rows, whose count is drawn once for each member from 4 to 27; the column bands are cut the same way within the last 32 columns of the grid, with a count drawn apart. Only windows in the last window row or the last window column of the grid hold more than one region.
All inputs are finite; a program needn't handle non-finite values.
Results may differ from the reference program's by a relative error of at most 0.0065.
The reference program's roundings to bfloat16 on the way count: a program that leaves them out, or rounds other values in their place, can miss the bound.
Values may be sent and summed in bfloat16 or wider, within the bound.
No kernel may reach another device: no remote copies, remote signals or barrier semaphores. Data moves between devices by JAX's collectives and lax.ppermute only.
A program may use at most 64 MiB of HBM per device.

```python
import math
import jax
import jax.numpy as jnp
from jax import lax

D = 1536
HEADS = 16
CHANNEL_PER_PART = 96
WS = 32
WCD = 2
SHIFT = 16
LANES = 4
AROWS = 8
COLS = 64
N_WIN = 4


def draw_logit_scaling_per_part(key, part):
    logs = jax.random.uniform(key, (HEADS,), jnp.float32, 0.0, jnp.log(6.0))
    return jnp.exp(logs)


def draw_mask_zone_labeling(key, part):
    cuts = jax.random.randint(jax.random.fold_in(key, 17), (2,), 4, WS - 4)
    row_cut = cuts[0]
    col_cut = cuts[1]
    grid_rows = 2 * WS
    grid_width = N_WIN // 2 * COLS
    block_index = lax.broadcasted_iota(jnp.int32, (N_WIN, WS, COLS), 0)
    inner_row = lax.broadcasted_iota(jnp.int32, (N_WIN, WS, COLS), 1)
    inner_col = lax.broadcasted_iota(jnp.int32, (N_WIN, WS, COLS), 2)
    grid_row = block_index % 2 * WS + inner_row
    grid_col = block_index // 2 * COLS + inner_col
    row_band = jnp.where(grid_row < WS, 0, jnp.where(grid_row < grid_rows - row_cut, 1, 2))
    col_band = jnp.where(grid_col < grid_width - WS, 0, jnp.where(grid_col < grid_width - col_cut, 1, 2))
    return (3 * row_band + col_band).astype(jnp.int32)


def block_levels(own_key, shape, split, smallest, largest):
    loudness, own = 1.0, jax.random.fold_in(own_key, 6)
    for dim, blocks in split:
        heights = jnp.exp(jax.random.uniform(jax.random.fold_in(own, dim), (blocks,), jnp.float32, smallest / len(split), largest / len(split)))
        loudness = loudness * jnp.repeat(heights, shape[dim] // blocks).reshape([-1 if axis == dim else 1 for axis in range(len(shape))])
    return loudness


def scatter_about(key, shape, scale, bound, shards=(), kind=jnp.bfloat16):
    factor_of = block_levels(key, shape, shards, -0.22, 0.18) if shards else 1.0
    entries = jax.random.normal(key, shape, jnp.float32) * scale * factor_of
    return jnp.minimum(jnp.maximum(entries, -bound), bound).astype(kind)


def setup_inputs(seed: int = 0, part: int = 0) -> dict:
    key_list = jax.random.split(jax.random.key(seed), 8)
    own_keys = jax.random.split(jax.random.fold_in(key_list[7], part), 8)
    pixel_grid_input = scatter_about(own_keys[0], (N_WIN, AROWS, LANES, COLS, D), 1.0, 6.0, ((0, 4), (2, 4)))
    mask_zone_labeling = draw_mask_zone_labeling(jax.random.fold_in(jax.random.fold_in(key_list[7], part), 71), part)
    standardize_multiplier = jnp.clip(1.0 + 0.15 * jax.random.normal(key_list[2], (D,), jnp.float32), 0.25, 1.75)
    standardize_offset_vector = scatter_about(key_list[3], (D,), 0.5, 3.0, (), jnp.float32)
    triple_projection_matrix = scatter_about(key_list[4], (3, D, HEADS * CHANNEL_PER_PART), D ** -0.5, 0.15625, ((2, 4),))
    logit_scaling_per_part = draw_logit_scaling_per_part(jax.random.fold_in(key_list[7], 71), part)
    final_projection_matrix = scatter_about(key_list[6], (HEADS * CHANNEL_PER_PART, D), (HEADS * CHANNEL_PER_PART) ** -0.5, 0.15625, ((0, 4),))
    return dict(pixel_grid_input=pixel_grid_input, mask_zone_labeling=mask_zone_labeling, standardize_multiplier=standardize_multiplier, standardize_offset_vector=standardize_offset_vector, triple_projection_matrix=triple_projection_matrix, logit_scaling_per_part=logit_scaling_per_part, final_projection_matrix=final_projection_matrix)


def layer_norm(values_in, gain_vector, bias_vector):
    values = values_in.astype(jnp.float32)
    average = lax.optimization_barrier(jnp.mean(values, axis=-1, keepdims=True))
    centred = values - average
    variance = lax.optimization_barrier(jnp.mean(centred * centred, axis=-1, keepdims=True))
    return (centred * lax.rsqrt(variance + 1e-05) * gain_vector + bias_vector).astype(jnp.bfloat16)

def window_attend(triple, labels, logit_multiplier):
    queries = triple[0].astype(jnp.float32)
    keys_all = triple[1].astype(jnp.float32)
    values_all = triple[2].astype(jnp.float32)
    scores = jnp.einsum('hpe,hke->hpk', queries, keys_all) * logit_multiplier[:, None, None]
    same_region = labels[:, None] == labels[None, :]
    scores = jnp.where(same_region[None], scores, -1e+30)
    row_max = lax.optimization_barrier(jnp.max(scores, axis=-1, keepdims=True))
    numerators = jnp.exp(scores - row_max)
    probabilities = (numerators / lax.optimization_barrier(jnp.sum(numerators, axis=-1, keepdims=True))).astype(jnp.bfloat16)
    return jnp.einsum('hpk,hke->hpe', probabilities.astype(jnp.float32), values_all).astype(jnp.bfloat16)

def reference(pixel_grid_input, mask_zone_labeling, standardize_multiplier, standardize_offset_vector, triple_projection_matrix, logit_scaling_per_part, final_projection_matrix):
    grid_cols = N_WIN // 2
    blocks = pixel_grid_input.reshape(grid_cols, 2, WS, COLS, D)
    image = blocks.transpose(1, 2, 0, 3, 4).reshape(2 * WS, grid_cols * COLS, D)
    image = jnp.roll(image, (-SHIFT, -SHIFT), axis=(0, 1))
    blocks = image.reshape(2, WS, grid_cols, COLS, D).transpose(2, 0, 1, 3, 4).reshape(N_WIN, WS, COLS, D)
    windows = blocks.reshape(N_WIN, WS, WCD, WS, D).transpose(0, 2, 1, 3, 4).reshape(N_WIN * WCD, WS * WS, D)
    labels = mask_zone_labeling.reshape(N_WIN, WS, WCD, WS).transpose(0, 2, 1, 3).reshape(N_WIN * WCD, WS * WS)
    weights_qkv = triple_projection_matrix.astype(jnp.float32)
    logit_multiplier = logit_scaling_per_part / math.sqrt(CHANNEL_PER_PART)

    def one_window(pair):
        tokens, token_region_labels = pair
        normed = layer_norm(tokens, standardize_multiplier, standardize_offset_vector)
        triple = jnp.einsum('pd,tdc->tpc', normed.astype(jnp.float32), weights_qkv).astype(jnp.bfloat16)
        triple = triple.reshape(3, WS * WS, HEADS, CHANNEL_PER_PART).transpose(0, 2, 1, 3)
        heads_out = window_attend(triple, token_region_labels, logit_multiplier)
        joined = heads_out.transpose(1, 0, 2).reshape(WS * WS, HEADS * CHANNEL_PER_PART)
        attention_update = jnp.dot(joined, final_projection_matrix, preferred_element_type=jnp.float32)
        return (tokens.astype(jnp.float32) + attention_update).astype(jnp.bfloat16)
    result = lax.map(one_window, (windows, labels))
    result = result.reshape(N_WIN, WCD, WS, WS, D).transpose(0, 2, 1, 3, 4)
    return result.reshape(N_WIN, AROWS, LANES, COLS, D)
```

```python
import functools
import math

import jax
import jax.numpy as jnp
from jax import lax
from jax.experimental import pallas as pl
from jax.experimental.pallas import tpu as pltpu
from jax.sharding import PartitionSpec as P

CHANNEL_PER_PART = 96
WS = 32
REGIONS = 32
LANE = 128
FAR = -1e30
F32 = jnp.float32
BF16 = jnp.bfloat16


def permute_by(value, axis, move):
    count = lax.axis_size(axis)
    return lax.ppermute(value, axis, [(source, move(source, count)) for source in range(count)])


def exchange(value, mask, axis="seq"):
    return permute_by(value, axis, lambda source, count: source ^ mask)


def masks_of(count):
    masks = []
    while count > 1:
        count //= 2
        masks.append(count)
    return masks


def gather_pieces(piece):
    pieces = {0: piece}
    for mask in masks_of(lax.axis_size("seq")):
        for offset in list(pieces):
            pieces[offset ^ mask] = exchange(pieces[offset], mask)
    return [pieces[offset] for offset in range(len(pieces))]


def padded(width):
    return (width + LANE - 1) // LANE * LANE


def project_kernel(count, cuts, *refs):
    pieces = refs[:count]
    weight_ref, gain_ref, bias_ref = refs[count : count + 3]
    outs = refs[count + 3 : count + 3 + len(cuts)]
    normed_ref = refs[-1]
    rows, cols, width = pieces[0].shape
    gain = gain_ref[...]
    bias = bias_ref[...]

    starts, base = [], 0
    for lo, hi in cuts:
        starts.append(base)
        base += count * rows * (hi - lo)

    for offset in range(count):

        @pl.loop(0, rows)
        def _(row, offset=offset):
            values = pieces[offset][row].astype(F32)
            average = jnp.mean(values, axis=-1, keepdims=True)
            centred = values - average
            variance = jnp.mean(centred * centred, axis=-1, keepdims=True)
            normed = (centred * lax.rsqrt(variance + 1e-05) * gain + bias).astype(BF16)
            for start, (lo, hi) in zip(starts, cuts, strict=True):
                size = hi - lo
                at = pl.multiple_of(start + (offset * rows + row) * size, 16)
                normed_ref[pl.ds(at, size), :] = normed[lo:hi]

    head_width = weight_ref.shape[2]
    slot = padded(head_width)
    for start, out_ref in zip(starts, outs, strict=True):
        block = normed_ref[start : start + out_ref.shape[0], :]
        if slot == head_width:
            weights = jnp.concatenate([weight_ref[t] for t in range(3)], axis=1)
            out_ref[...] = jnp.dot(block, weights, preferred_element_type=F32).astype(BF16)
        else:
            for t in range(3):
                product = jnp.dot(block, weight_ref[t], preferred_element_type=F32)
                out_ref[:, t * slot : t * slot + head_width] = product.astype(BF16)


def project(pieces, weights, gain, bias, cuts, name):
    count = len(pieces)
    rows, cols, width = pieces[0].shape
    slot = padded(weights.shape[2])
    sizes = [count * rows * (hi - lo) for lo, hi in cuts]
    total = sum(sizes)
    vmem = pl.BlockSpec(memory_space=pltpu.VMEM)
    return pl.pallas_call(
        functools.partial(project_kernel, count, cuts),
        out_shape=[jax.ShapeDtypeStruct((size, 3 * slot), BF16) for size in sizes],
        in_specs=[vmem] * (count + 3),
        out_specs=[vmem] * len(cuts),
        scratch_shapes=[pltpu.VMEM((total, width), BF16)],
        compiler_params=pltpu.CompilerParams(vmem_limit_bytes=24 << 20),
        cost_estimate=pl.CostEstimate(
            flops=2 * total * width * 3 * slot,
            bytes_accessed=2 * (total * width + weights.size + total * 3 * slot),
            transcendentals=0,
        ),
        name=name,
    )(*pieces, weights, gain[None], bias[None])


def attend_kernel(count, parts, ranges, head_width, *refs):
    blocks = refs[:parts]
    query_tags = refs[parts : 2 * parts]
    key_tags = refs[2 * parts : 3 * parts]
    scale_ref = refs[3 * parts]
    outs = refs[3 * parts + 1 :]
    slot = padded(head_width)
    sizes = [block.shape[0] // count for block in blocks]
    low, high = min(lo for lo, _ in ranges), max(hi for _, hi in ranges)
    heads = head_width // CHANNEL_PER_PART
    base = math.log2(math.e) / math.sqrt(CHANNEL_PER_PART)
    tiles = [None] * (slot // LANE)
    for head in range(heads):
        first = head * CHANNEL_PER_PART
        last = first + CHANNEL_PER_PART
        left, right = first // LANE * LANE, padded(last)
        reps = (right - left) // LANE
        lane = lax.broadcasted_iota(jnp.int32, (1, right - left), 1)
        inside = (lane >= first - left) & (lane < last - left)
        queries = jnp.concatenate(
            [b[low * z : high * z, left:right] for b, z in zip(blocks, sizes, strict=True)], axis=0
        )
        tags = jnp.concatenate(
            [t[low * z : high * z, :] for t, z in zip(query_tags, sizes, strict=True)], axis=0
        )
        queries = jnp.where(inside, queries, jnp.concatenate([tags] * reps, axis=1))
        keys = jnp.concatenate([b[:, slot + left : slot + right] for b in blocks], axis=0)
        tags = jnp.concatenate([t[...] for t in key_tags], axis=0)
        keys = jnp.where(inside, keys, jnp.concatenate([tags] * reps, axis=1))
        values = jnp.concatenate([b[:, 2 * slot + left : 2 * slot + right] for b in blocks], axis=0)
        scores = lax.dot_general(
            queries, keys, (((1,), (1,)), ((), ())), preferred_element_type=F32
        )
        row_max = jnp.max(scores, axis=-1, keepdims=True)
        numerators = jnp.exp2((scores - row_max) * (scale_ref[head] * base))
        total = jnp.sum(numerators, axis=-1, keepdims=True)
        mixed = jnp.dot(numerators.astype(BF16), values, preferred_element_type=F32) / total
        for i in range(reps):
            tile = left // LANE + i
            own = mixed[:, i * LANE : (i + 1) * LANE]
            held = tiles[tile]
            tiles[tile] = own if held is None else jnp.where(inside[:, i * LANE : (i + 1) * LANE], own, held)
    result = jnp.concatenate(tiles, axis=1)[:, :head_width].astype(BF16)
    for out_ref, (lo, hi) in zip(outs, ranges, strict=True):
        for offset in range(lo, hi):
            start, into = 0, 0
            for z in sizes:
                at = start + (offset - low) * z
                out_ref[offset - lo, into : into + z, :] = result[at : at + z]
                start += (high - low) * z
                into += z


def attend(blocks, query_tags, key_tags, scales, count, ranges, head_width, name):
    parts = len(blocks)
    per_offset = sum(b.shape[0] for b in blocks) // count
    pixels = count * per_offset
    asked = sum(hi - lo for lo, hi in ranges) * per_offset
    vmem = pl.BlockSpec(memory_space=pltpu.VMEM)
    heads = head_width // CHANNEL_PER_PART
    return pl.pallas_call(
        functools.partial(attend_kernel, count, parts, ranges, head_width),
        out_shape=[
            jax.ShapeDtypeStruct((hi - lo, per_offset, head_width), BF16) for lo, hi in ranges
        ],
        in_specs=[vmem] * (3 * parts) + [pl.BlockSpec(memory_space=pltpu.SMEM)],
        out_specs=[vmem] * len(ranges),
        compiler_params=pltpu.CompilerParams(vmem_limit_bytes=28 << 20),
        cost_estimate=pl.CostEstimate(
            flops=4 * heads * asked * pixels * 2 * LANE,
            bytes_accessed=2 * pixels * 3 * padded(head_width),
            transcendentals=heads * asked * pixels,
        ),
        name=name,
    )(*blocks, *query_tags, *key_tags, scales)


def finish_kernel(count, rows, near, *refs):
    refs = list(refs)
    first = [refs.pop(0) for _ in range(count)]
    second = [refs.pop(0) for _ in range(count)]
    weights = [refs.pop(0) for _ in range(count)]
    local, south, east, corner, out_ref = refs
    for window, attended in enumerate((first, second)):
        total = None
        for piece, weight in zip(attended, weights, strict=True):
            term = jnp.dot(piece[...], weight[...], preferred_element_type=F32)
            total = term if total is None else total + term
        if window == 0:
            spans = [(local, 0, 0, WS, 0), (south, 0, 0, WS, 1)]
        else:
            spans = [
                (local, WS, WS, near, 0),
                (south, WS, WS, near, 1),
                (east, 0, WS + near, WS - near, 0),
                (corner, 0, WS + near, WS - near, 1),
            ]
        at = 0
        for source, left, column, size, half in spans:
            for row in range(rows):
                held = source[row, left : left + size, :].astype(F32)
                out_ref[half * rows + row, column : column + size, :] = (
                    held + total[at : at + size]
                ).astype(BF16)
                at += size


def finish(first, second, weights, pieces):
    count = len(weights)
    local, south, east, corner = pieces
    rows, near = local.shape[0], local.shape[1] - WS
    width = local.shape[2]
    vmem = pl.BlockSpec(memory_space=pltpu.VMEM)
    pixels = 2 * first[0].shape[0]
    return pl.pallas_call(
        functools.partial(finish_kernel, count, rows, near),
        out_shape=jax.ShapeDtypeStruct((2 * rows, 2 * WS, width), BF16),
        in_specs=[vmem] * (3 * count + 4),
        out_specs=vmem,
        compiler_params=pltpu.CompilerParams(vmem_limit_bytes=24 << 20),
        cost_estimate=pl.CostEstimate(
            flops=2 * pixels * width * width, bytes_accessed=2 * width * (width + 3 * pixels), transcendentals=0
        ),
        name="finish",
    )(*first, *second, *weights, local, south, east, corner)


def ranges_of(count):
    return [(mask, 2 * mask) for mask in masks_of(count)] + [(0, 1)]


def scatter_heads(outs, count):
    held = {}
    for (lo, hi), out in zip(ranges_of(count), outs, strict=True):
        for offset in range(lo, hi):
            held[offset] = [(0, out, offset - lo)]
    for mask in masks_of(count):
        fresh = {offset: list(held[offset]) for offset in range(mask)}
        groups = len(held[mask])
        for group in range(groups):
            origin, array, index = held[mask][group]
            whole = array.shape[0] == mask and all(
                held[mask + i][group][1] is array and held[mask + i][group][2] == i for i in range(mask)
            )
            if not whole:
                array = jnp.stack([held[mask + i][group][1][held[mask + i][group][2]] for i in range(mask)])
            arrived = exchange(array, mask)
            for i in range(mask):
                fresh[i].append((origin ^ mask, arrived, i))
        held = fresh
    own = {origin: array[index] for origin, array, index in held[0]}
    return [own[offset] for offset in range(count)]


def gather_weights(block, member, members):
    pieces = {0: block}
    half = block.shape[0] // 2
    for mask in masks_of(lax.axis_size("seq")):
        for offset in list(pieces):
            piece = pieces[offset]
            if mask > 1 and members == 2:
                part = lax.dynamic_slice_in_dim(piece, member * half, half, axis=0)
                near = exchange(part, mask)
                far = exchange(near, 1, "member")
                upper = jnp.where(member == 0, near, far)
                lower = jnp.where(member == 0, far, near)
                pieces[offset ^ mask] = jnp.concatenate([upper, lower], axis=0)
            else:
                pieces[offset ^ mask] = exchange(piece, mask)
    return [pieces[offset] for offset in range(len(pieces))]


def on_device(
    pixel_grid_input,
    mask_zone_labeling,
    standardize_multiplier,
    standardize_offset_vector,
    triple_projection_matrix,
    logit_scaling_per_part,
    final_projection_matrix,
):
    count = lax.axis_size("seq")
    members = lax.axis_size("member")
    member = lax.axis_index("member")
    device = lax.axis_index("seq")
    blocked = pixel_grid_input[0, :, 0]
    row_count, col_count, width = blocked.shape
    rows = row_count // 2
    half = WS // 2
    head_width = triple_projection_matrix.shape[2]

    def west(source, count):
        return (source - 2) % count

    def west_north(source, count):
        return ((source ^ 1) - 2) % count

    local = blocked[rows:, half:]
    south = exchange(blocked[:rows, half:], 1, "win")
    east = permute_by(blocked[rows:, :half], "win", west)
    corner = permute_by(blocked[:rows, :half], "win", west_north)

    labels = mask_zone_labeling[0].reshape(2, rows, count, col_count).transpose(2, 0, 1, 3)
    for mask in masks_of(count):
        paired = labels.reshape(count // (2 * mask), 2, mask, 2, rows, col_count)
        swapped = jnp.where((device & mask) != 0, paired[:, ::-1], paired)
        labels = swapped.reshape(count, 2, rows, col_count)
    near = half
    cut = [(0, WS), (WS, WS + near), (WS + near, 2 * WS)]
    order = [(0, 0), (1, 0), (0, 1), (1, 1), (0, 2), (1, 2)]
    flat = jnp.concatenate([labels[:, h, :, cut[c][0] : cut[c][1]].reshape(-1) for h, c in order])
    lane = lax.broadcasted_iota(jnp.int32, (1, LANE), 1) % REGIONS
    same = flat[:, None] == lane
    query_all = jnp.where(same, 1.0, 0.0).astype(BF16)
    key_all = jnp.where(same, 0.0, FAR).astype(BF16)
    query_tags, key_tags, at = [], [], 0
    for _, c in order:
        size = count * rows * (cut[c][1] - cut[c][0])
        query_tags.append(query_all[at : at + size])
        key_tags.append(key_all[at : at + size])
        at += size

    gain, bias = standardize_multiplier, standardize_offset_vector
    both = [(0, WS), (WS, WS + near)]
    weights = triple_projection_matrix
    local_0, local_1 = project(gather_pieces(local), weights, gain, bias, both, "project_local")
    south_0, south_1 = project(gather_pieces(south), weights, gain, bias, both, "project_south")
    (east_1,) = project(gather_pieces(east), weights, gain, bias, [(0, near)], "project_east")
    (corner_1,) = project(gather_pieces(corner), weights, gain, bias, [(0, near)], "project_corner")

    out_weights = gather_weights(final_projection_matrix, member, members)
    runs = ranges_of(count)

    def window(blocks, tags, name):
        far = attend(blocks, *tags, logit_scaling_per_part, count, runs[:1], head_width, name + "_far")
        close = attend(blocks, *tags, logit_scaling_per_part, count, runs[1:], head_width, name + "_near")
        return scatter_heads(list(far) + list(close), count)

    first = window([local_0, south_0], (query_tags[:2], key_tags[:2]), "attend_0")
    second = window([local_1, south_1, east_1, corner_1], (query_tags[2:], key_tags[2:]), "attend_1")
    mixed = finish(first, second, out_weights, (local, south, east, corner))
    return mixed[None, :, None]


def solution(mesh):
    in_specs = (
        P(("member", "win"), None, "seq", None, None),
        P(("member", "win"), None, None),
        P(),
        P(),
        P(None, None, "seq"),
        P("seq"),
        P("seq", None),
    )
    out_specs = P(("member", "win"), None, "seq", None, None)
    return jax.shard_map(
        on_device, mesh=mesh, in_specs=in_specs, out_specs=out_specs, check_vma=False
    )
```

```python
import functools
import math

import jax
import jax.numpy as jnp
from jax import lax
from jax.experimental import pallas as pl
from jax.experimental.pallas import tpu as pltpu
from jax.sharding import PartitionSpec as P

CHANNEL_PER_PART = 96
WS = 32
REGIONS = 32
LANE = 128
FAR = -1e30
F32 = jnp.float32
BF16 = jnp.bfloat16


def permute_by(value, axis, move):
    count = lax.axis_size(axis)
    return lax.ppermute(value, axis, [(source, move(source, count)) for source in range(count)])


def exchange(value, mask, axis="seq"):
    return permute_by(value, axis, lambda source, count: source ^ mask)


def masks_of(count):
    masks = []
    while count > 1:
        count //= 2
        masks.append(count)
    return masks


def gather_pieces(piece):
    pieces = {0: piece}
    for mask in masks_of(lax.axis_size("seq")):
        for offset in list(pieces):
            pieces[offset ^ mask] = exchange(pieces[offset], mask)
    return [pieces[offset] for offset in range(len(pieces))]


def padded(width):
    return (width + LANE - 1) // LANE * LANE


VMEM = pl.BlockSpec(memory_space=pltpu.VMEM)


def after(value, *earlier):
    return lax.optimization_barrier((value, *earlier))[0]


def normalized(held, gain, bias):
    values = held.astype(F32)
    average = jnp.mean(values, axis=-1, keepdims=True)
    centred = values - average
    variance = jnp.mean(centred * centred, axis=-1, keepdims=True)
    return (centred * lax.rsqrt(variance + 1e-05) * gain + bias).astype(BF16)


def split_kernel(near, pixel_ref, gain_ref, bias_ref, south_ref, east_ref, corner_ref, local_ref):
    rows = pixel_ref.shape[0] // 2
    south_ref[...] = pixel_ref[:rows, near:, :]
    east_ref[...] = pixel_ref[rows:, :near, :]
    corner_ref[...] = pixel_ref[:rows, :near, :]
    spans = [(0, rows + row, near, WS) for row in range(rows)]
    spans += [(0, rows + row, near + WS, WS - near) for row in range(rows)]
    norm_kernel(spans, pixel_ref, gain_ref, bias_ref, local_ref)


def split(pixels, gain, bias, near):
    row_count, col_count, width = pixels.shape
    rows, rest = row_count // 2, col_count - near
    return pl.pallas_call(
        functools.partial(split_kernel, near),
        out_shape=[
            jax.ShapeDtypeStruct((rows, rest, width), BF16),
            jax.ShapeDtypeStruct((rows, near, width), BF16),
            jax.ShapeDtypeStruct((rows, near, width), BF16),
            jax.ShapeDtypeStruct((rows * rest, width), BF16),
        ],
        in_specs=[VMEM] * 3,
        out_specs=[VMEM] * 4,
        compiler_params=pltpu.CompilerParams(vmem_limit_bytes=12 << 20),
        cost_estimate=pl.CostEstimate(
            flops=10 * pixels.size, bytes_accessed=4 * pixels.size, transcendentals=0
        ),
        name="split",
    )(pixels, gain, bias)


def norm_kernel(spans, *refs):
    *sources, gain_ref, bias_ref, out_ref = refs
    into = 0
    gain, bias = gain_ref[...], bias_ref[...]
    for which, row, left, size in spans:
        held = sources[which][row, left : left + size, :]
        out_ref[into : into + size, :] = normalized(held, gain, bias)
        into += size


def norm(sources, gain, bias, spans, name):
    width = sources[0].shape[-1]
    total = sum(span[-1] for span in spans)
    return pl.pallas_call(
        functools.partial(norm_kernel, spans),
        out_shape=jax.ShapeDtypeStruct((total, width), BF16),
        in_specs=[VMEM] * (len(sources) + 2),
        out_specs=VMEM,
        compiler_params=pltpu.CompilerParams(vmem_limit_bytes=8 << 20),
        cost_estimate=pl.CostEstimate(
            flops=10 * total * width, bytes_accessed=4 * total * width, transcendentals=0
        ),
        name=name,
    )(*sources, gain, bias)


def tag_kernel(count, near, label_ref, *outs):
    query_0, key_0, query_1, key_1 = outs
    row_count, col_count = label_ref.shape
    rows = row_count // (2 * count)
    device = lax.axis_index("seq")
    turned = jnp.transpose(label_ref[...].astype(F32)).astype(BF16)
    place = lax.broadcasted_iota(jnp.int32, (row_count, LANE), 0)
    lane = (lax.broadcasted_iota(jnp.int32, (1, LANE), 1) % REGIONS).astype(F32)
    group = count * rows
    for half in range(2):
        for offset in range(count):
            for row in range(rows):
                at = (half * rows + row) * count + jnp.bitwise_xor(device, offset)
                chosen = jnp.where(place == at, 1.0, 0.0).astype(BF16)
                region = jnp.dot(turned, chosen, preferred_element_type=F32)
                same = region == lane
                query = jnp.where(same, 1.0, 0.0).astype(BF16)
                key = jnp.where(same, 0.0, FAR).astype(BF16)
                slot = offset * rows + row
                spots = [
                    (query_0, key_0, (half * group + slot) * WS, 0, WS),
                    (query_1, key_1, half * group * near + slot * near, WS, near),
                    (
                        query_1,
                        key_1,
                        2 * group * near + half * group * (WS - near) + slot * (WS - near),
                        WS + near,
                        WS - near,
                    ),
                ]
                for query_ref, key_ref, into, left, size in spots:
                    query_ref[into : into + size, :] = query[left : left + size]
                    key_ref[into : into + size, :] = key[left : left + size]


def region_tags(labels, count, near):
    pixels = labels.shape[0] * WS
    return pl.pallas_call(
        functools.partial(tag_kernel, count, near),
        out_shape=[jax.ShapeDtypeStruct((pixels, LANE), BF16)] * 4,
        in_specs=[VMEM],
        out_specs=[VMEM] * 4,
        compiler_params=pltpu.CompilerParams(vmem_limit_bytes=8 << 20),
        cost_estimate=pl.CostEstimate(
            flops=8 * pixels * LANE * labels.shape[0], bytes_accessed=8 * pixels * LANE, transcendentals=0
        ),
        name="tags",
    )(labels)


def project_kernel(count, cuts, *refs):
    pieces = refs[:count]
    weight_ref = refs[count]
    outs = refs[count + 1 :]
    head_width = weight_ref.shape[2]
    slot = padded(head_width)
    block = jnp.concatenate([piece[lo:hi, :] for lo, hi in cuts for piece in pieces], axis=0)
    if slot == head_width:
        weights = jnp.concatenate([weight_ref[t] for t in range(3)], axis=1)
        products = [(0, jnp.dot(block, weights, preferred_element_type=F32).astype(BF16))]
    else:
        products = [
            (t * slot, jnp.dot(block, weight_ref[t], preferred_element_type=F32).astype(BF16))
            for t in range(3)
        ]
    at = 0
    for out_ref in outs:
        for left, product in products:
            part = product[at : at + out_ref.shape[0]]
            out_ref[:, left : left + part.shape[1]] = part
        at += out_ref.shape[0]


def project(pieces, weights, cuts, name):
    count = len(pieces)
    width = pieces[0].shape[1]
    slot = padded(weights.shape[2])
    sizes = [count * (hi - lo) for lo, hi in cuts]
    total = sum(sizes)
    return pl.pallas_call(
        functools.partial(project_kernel, count, cuts),
        out_shape=[jax.ShapeDtypeStruct((size, 3 * slot), BF16) for size in sizes],
        in_specs=[VMEM] * (count + 1),
        out_specs=[VMEM] * len(cuts),
        compiler_params=pltpu.CompilerParams(vmem_limit_bytes=24 << 20),
        cost_estimate=pl.CostEstimate(
            flops=2 * total * width * 3 * slot,
            bytes_accessed=2 * (total * width + weights.size + total * 3 * slot),
            transcendentals=0,
        ),
        name=name,
    )(*pieces, weights)


def attend_kernel(count, parts, ranges, head_width, *refs):
    blocks = refs[:parts]
    query_tags, key_tags, scale_ref = refs[parts : parts + 3]
    outs = refs[parts + 3 :]
    slot = padded(head_width)
    sizes = [block.shape[0] // count for block in blocks]
    low, high = min(lo for lo, _ in ranges), max(hi for _, hi in ranges)
    heads = head_width // CHANNEL_PER_PART
    base = math.log2(math.e) / math.sqrt(CHANNEL_PER_PART)
    tiles = [None] * (slot // LANE)
    for head in range(heads):
        first = head * CHANNEL_PER_PART
        last = first + CHANNEL_PER_PART
        left, right = first // LANE * LANE, padded(last)
        reps = (right - left) // LANE
        lane = lax.broadcasted_iota(jnp.int32, (1, right - left), 1)
        inside = (lane >= first - left) & (lane < last - left)
        queries = jnp.concatenate(
            [b[low * z : high * z, left:right] for b, z in zip(blocks, sizes, strict=True)], axis=0
        )
        tags, at = [], 0
        for z in sizes:
            tags.append(query_tags[at + low * z : at + high * z, :])
            at += count * z
        tags = jnp.concatenate(tags, axis=0)
        queries = jnp.where(inside, queries, jnp.concatenate([tags] * reps, axis=1))
        keys = jnp.concatenate([b[:, slot + left : slot + right] for b in blocks], axis=0)
        tags = key_tags[...]
        keys = jnp.where(inside, keys, jnp.concatenate([tags] * reps, axis=1))
        values = jnp.concatenate([b[:, 2 * slot + left : 2 * slot + right] for b in blocks], axis=0)
        scores = lax.dot_general(
            queries, keys, (((1,), (1,)), ((), ())), preferred_element_type=F32
        )
        row_max = jnp.max(scores, axis=-1, keepdims=True)
        numerators = jnp.exp2((scores - row_max) * (scale_ref[head] * base))
        total = jnp.sum(numerators, axis=-1, keepdims=True)
        mixed = jnp.dot(numerators.astype(BF16), values, preferred_element_type=F32) / total
        for i in range(reps):
            tile = left // LANE + i
            own = mixed[:, i * LANE : (i + 1) * LANE]
            held = tiles[tile]
            tiles[tile] = own if held is None else jnp.where(inside[:, i * LANE : (i + 1) * LANE], own, held)
    result = jnp.concatenate(tiles, axis=1)[:, :head_width].astype(BF16)
    for out_ref, (lo, hi) in zip(outs, ranges, strict=True):
        for offset in range(lo, hi):
            start, into = 0, 0
            for z in sizes:
                at = start + (offset - low) * z
                out_ref[offset - lo, into : into + z, :] = result[at : at + z]
                start += (high - low) * z
                into += z


def attend(blocks, query_tags, key_tags, scales, count, ranges, head_width, name):
    parts = len(blocks)
    per_offset = sum(b.shape[0] for b in blocks) // count
    pixels = count * per_offset
    asked = sum(hi - lo for lo, hi in ranges) * per_offset
    vmem = pl.BlockSpec(memory_space=pltpu.VMEM)
    heads = head_width // CHANNEL_PER_PART
    return pl.pallas_call(
        functools.partial(attend_kernel, count, parts, ranges, head_width),
        out_shape=[
            jax.ShapeDtypeStruct((hi - lo, per_offset, head_width), BF16) for lo, hi in ranges
        ],
        in_specs=[vmem] * (parts + 2) + [pl.BlockSpec(memory_space=pltpu.SMEM)],
        out_specs=[vmem] * len(ranges),
        compiler_params=pltpu.CompilerParams(vmem_limit_bytes=28 << 20),
        cost_estimate=pl.CostEstimate(
            flops=4 * heads * asked * pixels * 2 * LANE,
            bytes_accessed=2 * pixels * 3 * padded(head_width),
            transcendentals=heads * asked * pixels,
        ),
        name=name,
    )(*blocks, query_tags, key_tags, scales)


def finish_kernel(count, spans, out_spans, *refs):
    refs = list(refs)
    attended = [refs.pop(0) for _ in range(count)]
    weights = [refs.pop(0) for _ in range(count)]
    *sources, out_ref = refs
    total = None
    for piece, weight in zip(attended, weights, strict=True):
        term = jnp.dot(piece[...], weight[...], preferred_element_type=F32)
        total = term if total is None else total + term
    at = 0
    for which, row, left, size, into, column in spans:
        held = sources[which][row, left : left + size, :].astype(F32)
        out_ref[into, column : column + size, :] = (held + total[at : at + size]).astype(BF16)
        at += size
    for which, row, left, size, into, column in out_spans:
        out_ref[into, column : column + size, :] = sources[which][row, left : left + size, :]


def finish(attended, weights, sources, spans, out_spans, shape, name):
    count = len(weights)
    width = shape[-1]
    pixels = attended[0].shape[0]
    return pl.pallas_call(
        functools.partial(finish_kernel, count, spans, out_spans),
        out_shape=jax.ShapeDtypeStruct(shape, BF16),
        in_specs=[VMEM] * (2 * count + len(sources)),
        out_specs=VMEM,
        compiler_params=pltpu.CompilerParams(vmem_limit_bytes=20 << 20),
        cost_estimate=pl.CostEstimate(
            flops=2 * pixels * width * width, bytes_accessed=2 * width * (width + 3 * pixels), transcendentals=0
        ),
        name=name,
    )(*attended, *weights, *sources)


def ranges_of(count):
    return [(mask, 2 * mask) for mask in masks_of(count)] + [(0, 1)]


def scatter_heads(outs, count, gate=None):
    held = {}
    for (lo, hi), out in zip(ranges_of(count), outs, strict=True):
        for offset in range(lo, hi):
            held[offset] = [(0, out, offset - lo)]
    for mask in masks_of(count):
        fresh = {offset: list(held[offset]) for offset in range(mask)}
        groups = len(held[mask])
        for group in range(groups):
            origin, array, index = held[mask][group]
            whole = array.shape[0] == mask and all(
                held[mask + i][group][1] is array and held[mask + i][group][2] == i for i in range(mask)
            )
            if not whole:
                array = jnp.stack([held[mask + i][group][1][held[mask + i][group][2]] for i in range(mask)])
            arrived = exchange(array, mask)
            if gate is not None and mask > 1:
                arrived = after(arrived, gate)
            for i in range(mask):
                fresh[i].append((origin ^ mask, arrived, i))
        held = fresh
    own = {origin: array[index] for origin, array, index in held[0]}
    return [own[offset] for offset in range(count)]


def pick_kernel(place, source_ref, out_ref):
    size = out_ref.shape[0]
    out_ref[...] = source_ref[pl.ds(pl.multiple_of(place() * size, 16), size), :]


def join_kernel(place, own_ref, other_ref, out_ref):
    size = own_ref.shape[0]
    at = place()
    out_ref[pl.ds(pl.multiple_of(at * size, 16), size), :] = own_ref[...]
    out_ref[pl.ds(pl.multiple_of((1 - at) * size, 16), size), :] = other_ref[...]


def small_call(kernel, rows, name, *operands):
    width = operands[0].shape[1]
    return pl.pallas_call(
        kernel,
        out_shape=jax.ShapeDtypeStruct((rows, width), BF16),
        in_specs=[VMEM] * len(operands),
        out_specs=VMEM,
        compiler_params=pltpu.CompilerParams(vmem_limit_bytes=8 << 20),
        cost_estimate=pl.CostEstimate(flops=0, bytes_accessed=4 * rows * width, transcendentals=0),
        name=name,
    )(*operands)


def gather_weights(block, held_back):
    levels = []
    rows = block.shape[0]
    for axis in ("member", "win"):
        if lax.axis_size(axis) % 2 == 0 and rows % (32 << len(levels)) == 0:
            levels.append(axis)

    def bit(axis):
        return lax.axis_index(axis) & 1

    def part_index():
        index = 0
        for axis in levels:
            index = index * 2 + bit(axis)
        return index

    pieces = {0: block}
    for mask in masks_of(lax.axis_size("seq")):
        for offset in list(pieces):
            piece = pieces[offset]
            if mask > 1 and levels:
                size = rows >> len(levels)
                part = small_call(functools.partial(pick_kernel, part_index), size, "pick", held_back(piece))
                part = exchange(part, mask)
                for axis in reversed(levels):
                    other = exchange(part, 1, axis)
                    size *= 2
                    part = small_call(
                        functools.partial(join_kernel, functools.partial(bit, axis)), size, "join_" + axis, part, other
                    )
                pieces[offset ^ mask] = part
            else:
                pieces[offset ^ mask] = exchange(piece, mask)
    return [pieces[offset] for offset in range(len(pieces))]


def on_device(
    pixel_grid_input,
    mask_zone_labeling,
    standardize_multiplier,
    standardize_offset_vector,
    triple_projection_matrix,
    logit_scaling_per_part,
    final_projection_matrix,
):
    count = lax.axis_size("seq")
    blocked = pixel_grid_input[0, :, 0]
    row_count, col_count, width = blocked.shape
    rows = row_count // 2
    half = WS // 2
    head_width = triple_projection_matrix.shape[2]

    def west(source, count):
        return (source - 2) % count

    def west_north(source, count):
        return ((source ^ 1) - 2) % count

    near = WS - half
    gain, bias = standardize_multiplier[None], standardize_offset_vector[None]
    weights = triple_projection_matrix
    scales = logit_scaling_per_part
    runs = ranges_of(count)

    south, east, corner, local_normed = split(blocked, gain, bias, half)
    local_pieces = gather_pieces(local_normed)
    south = exchange(south, 1, "win")
    east = permute_by(east, "win", west)
    corner = permute_by(corner, "win", west_north)
    query_0, key_0, query_1, key_1 = region_tags(mask_zone_labeling[0], count, near)
    spans = [(0, row, 0, WS) for row in range(rows)] + [(0, row, WS, near) for row in range(rows)]
    south_normed = norm([south], gain, bias, spans, "norm_south")
    south_pieces = gather_pieces(south_normed)
    out_weights = gather_weights(final_projection_matrix, lambda piece: after(piece, south_normed))
    cuts = [(0, rows * WS), (rows * WS, rows * (WS + near))]
    local_pieces[0] = after(local_normed, south_normed)
    local_0, local_1 = project(local_pieces, weights, cuts, "project_local")
    south_pieces[0] = after(south_normed, local_0)
    south_0, south_1 = project(south_pieces, weights, cuts, "project_south")

    spans = [(which, row, 0, half) for which in range(2) for row in range(rows)]
    far_normed = norm([after(east, local_0), corner], gain, bias, spans, "norm_far")
    far_pieces = gather_pieces(far_normed)

    def attend_both(blocks, tags, name):
        far = attend(blocks, *tags, scales, count, runs[:1], head_width, name + "_far")
        blocks = [after(blocks[0], *far), *blocks[1:]]
        close = attend(blocks, *tags, scales, count, runs[1:], head_width, name + "_near")
        return list(far) + list(close)

    outs_0 = attend_both([local_0, south_0], (query_0, key_0), "attend_0")
    cuts = [(0, rows * half), (rows * half, 2 * rows * half)]
    far_pieces[0] = after(far_normed, *outs_0)
    east_1, corner_1 = project(far_pieces, weights, cuts, "project_far")
    outs_1 = attend_both([local_1, south_1, east_1, corner_1], (query_1, key_1), "attend_1")

    first = scatter_heads(outs_0, count)
    first[0] = after(first[0], *outs_1)
    spans = [(0, rows + row, half, WS, row, 0) for row in range(rows)]
    spans += [(1, row, 0, WS, rows + row, 0) for row in range(rows)]
    done = finish(first, out_weights, [blocked, south], spans, [], (row_count, WS, width), "finish_0")
    second = scatter_heads(outs_1, count, done)
    spans = [(0, rows + row, half + WS, near, row, WS) for row in range(rows)]
    spans += [(1, row, WS, near, rows + row, WS) for row in range(rows)]
    spans += [(2, row, 0, half, row, WS + near) for row in range(rows)]
    spans += [(3, row, 0, half, rows + row, WS + near) for row in range(rows)]
    kept = [(4, row, 0, WS, row, 0) for row in range(row_count)]
    mixed = finish(
        second, out_weights, [blocked, south, east, corner, done], spans, kept, (row_count, col_count, width), "finish_1"
    )
    return mixed[None, :, None]


def solution(mesh):
    in_specs = (
        P(("member", "win"), None, "seq", None, None),
        P(("member", "win"), None, None),
        P(),
        P(),
        P(None, None, "seq"),
        P("seq"),
        P("seq", None),
    )
    out_specs = P(("member", "win"), None, "seq", None, None)
    return jax.shard_map(
        on_device, mesh=mesh, in_specs=in_specs, out_specs=out_specs, check_vma=False
    )
```

```python
import functools
import math

import jax
import jax.numpy as jnp
from jax import lax
from jax.experimental import pallas as pl
from jax.experimental.pallas import tpu as pltpu
from jax.sharding import PartitionSpec as P


CHANNEL_PER_PART = 96
WS = 32
REGIONS = 32
LANE = 128
FAR = -1e30
F32 = jnp.float32
BF16 = jnp.bfloat16


def permute_by(value, axis, move):
    count = lax.axis_size(axis)
    pairs = [(source, move(source, count)) for source in range(count)]
    return lax.ppermute(value, axis, pairs)


def exchange(value, mask, axis="seq"):
    return permute_by(value, axis, lambda source, count: source ^ mask)


def masks_of(count):
    masks = []
    while count > 1:
        count //= 2
        masks.append(count)
    return masks


def gather_pieces(piece):
    pieces = {0: piece}
    for mask in masks_of(lax.axis_size("seq")):
        for offset in list(pieces):
            pieces[offset ^ mask] = exchange(pieces[offset], mask)
    return [pieces[offset] for offset in range(len(pieces))]


def padded(width):
    return (width + LANE - 1) // LANE * LANE


VMEM = pl.BlockSpec(memory_space=pltpu.VMEM)


def after(value, *earlier):
    return lax.optimization_barrier((value, *earlier))[0]


def normalized(held, gain, bias):
    values = held.astype(F32)
    average = jnp.mean(values, axis=-1, keepdims=True)
    centred = values - average
    variance = jnp.mean(centred * centred, axis=-1, keepdims=True)
    return (centred * lax.rsqrt(variance + 1e-05) * gain + bias).astype(BF16)


HELD = pl.BlockSpec(memory_space=pltpu.HBM)


def cut_kernel(boxes, pixel_ref, *refs):
    outs, semaphore = refs[:-1], refs[-1]
    copies = [
        pltpu.make_async_copy(
            pixel_ref.at[pl.ds(row, rows), pl.ds(left, size), :], out_ref, semaphore.at[index]
        )
        for index, ((row, rows, left, size), out_ref) in enumerate(zip(boxes, outs, strict=True))
    ]
    for copy in copies:
        copy.start()
    for copy in copies:
        copy.wait()


def cut(pixels, boxes):
    width = pixels.shape[2]
    return pl.pallas_call(
        functools.partial(cut_kernel, boxes),
        out_shape=[jax.ShapeDtypeStruct((rows, size, width), BF16) for _, rows, _, size in boxes],
        in_specs=[HELD],
        out_specs=[VMEM] * len(boxes),
        scratch_shapes=[pltpu.SemaphoreType.DMA((len(boxes),))],
        compiler_params=pltpu.CompilerParams(vmem_limit_bytes=8 << 20),
        cost_estimate=pl.CostEstimate(flops=0, bytes_accessed=2 * pixels.size, transcendentals=0),
        name="cut",
    )(pixels)


def norm_local_kernel(boxes, pixel_ref, gain_ref, bias_ref, *refs):
    outs, helds, semaphore = refs[: len(boxes)], refs[len(boxes) : -1], refs[-1]
    copies = [
        pltpu.make_async_copy(
            pixel_ref.at[pl.ds(row, rows), pl.ds(left, size), :], held, semaphore.at[index]
        )
        for index, ((row, rows, left, size), held) in enumerate(zip(boxes, helds, strict=True))
    ]
    for copy in copies:
        copy.start()
    gain, bias = gain_ref[...], bias_ref[...]
    for copy, held, out_ref in zip(copies, helds, outs, strict=True):
        copy.wait()
        size = held.shape[1]
        for row in range(held.shape[0]):
            out_ref[row * size : (row + 1) * size, :] = normalized(held[row], gain, bias)


def norm_local(pixels, gain, bias, boxes):
    width = pixels.shape[2]
    return pl.pallas_call(
        functools.partial(norm_local_kernel, boxes),
        out_shape=[jax.ShapeDtypeStruct((rows * size, width), BF16) for _, rows, _, size in boxes],
        in_specs=[HELD, VMEM, VMEM],
        out_specs=[VMEM] * len(boxes),
        scratch_shapes=[pltpu.VMEM((rows, size, width), BF16) for _, rows, _, size in boxes]
        + [pltpu.SemaphoreType.DMA((len(boxes),))],
        compiler_params=pltpu.CompilerParams(vmem_limit_bytes=8 << 20),
        cost_estimate=pl.CostEstimate(flops=5 * pixels.size, bytes_accessed=2 * pixels.size, transcendentals=0),
        name="norm_local",
    )(pixels, gain, bias)


def norm_kernel(spans, *refs):
    *sources, gain_ref, bias_ref, out_ref = refs
    into = 0
    gain, bias = gain_ref[...], bias_ref[...]
    for which, row, left, size in spans:
        held = sources[which][row, left : left + size, :]
        out_ref[into : into + size, :] = normalized(held, gain, bias)
        into += size


def norm(sources, gain, bias, spans):
    width = sources[0].shape[-1]
    total = sum(span[-1] for span in spans)
    return pl.pallas_call(
        functools.partial(norm_kernel, spans),
        out_shape=jax.ShapeDtypeStruct((total, width), BF16),
        in_specs=[VMEM] * (len(sources) + 2),
        out_specs=VMEM,
        compiler_params=pltpu.CompilerParams(vmem_limit_bytes=8 << 20),
        cost_estimate=pl.CostEstimate(
            flops=10 * total * width, bytes_accessed=4 * total * width, transcendentals=0
        ),
    )(*sources, gain, bias)


def tag_kernel(count, near, label_ref, *outs):
    query_0, key_0, query_1, key_1 = outs
    row_count, _ = label_ref.shape
    rows = row_count // (2 * count)
    device = lax.axis_index("seq")
    turned = jnp.transpose(label_ref[...].astype(F32)).astype(BF16)
    place = lax.broadcasted_iota(jnp.int32, (row_count, LANE), 0)
    lane = (lax.broadcasted_iota(jnp.int32, (1, LANE), 1) % REGIONS).astype(F32)
    group = count * rows
    for half in range(2):
        for offset in range(count):
            for row in range(rows):
                at = (half * rows + row) * count + jnp.bitwise_xor(device, offset)
                chosen = jnp.where(place == at, 1.0, 0.0).astype(BF16)
                region = jnp.dot(turned, chosen, preferred_element_type=F32)
                same = region == lane
                query = jnp.where(same, 1.0, 0.0).astype(BF16)
                key = jnp.where(same, 0.0, FAR).astype(BF16)
                slot = offset * rows + row
                apart, span = group * near, near + 2 * (WS - near)
                beside = apart + offset * rows * span
                spots = [
                    (query_0, key_0, (half * group + slot) * WS, 0, WS),
                    (query_1, key_1, beside + row * near if half else slot * near, WS, near),
                    (
                        query_1,
                        key_1,
                        beside + rows * near + (half * rows + row) * (WS - near),
                        WS + near,
                        WS - near,
                    ),
                ]
                for query_ref, key_ref, into, left, size in spots:
                    query_ref[into : into + size, :] = query[left : left + size]
                    key_ref[into : into + size, :] = key[left : left + size]


def region_tags(labels, count, near):
    pixels = labels.shape[0] * WS
    return pl.pallas_call(
        functools.partial(tag_kernel, count, near),
        out_shape=[jax.ShapeDtypeStruct((pixels, LANE), BF16)] * 4,
        in_specs=[VMEM],
        out_specs=[VMEM] * 4,
        compiler_params=pltpu.CompilerParams(vmem_limit_bytes=8 << 20),
        cost_estimate=pl.CostEstimate(
            flops=8 * pixels * LANE * labels.shape[0], bytes_accessed=8 * pixels * LANE, transcendentals=0
        ),
        name="tags",
    )(labels)


def project_kernel(counts, *refs):
    groups = []
    for count in counts:
        groups.append(refs[:count])
        refs = refs[count:]
    weight_ref, *outs = refs
    head_width = weight_ref.shape[2]
    slot = padded(head_width)
    block = jnp.concatenate([piece[...] for group in groups for piece in group], axis=0)
    if slot == head_width:
        weights = jnp.concatenate([weight_ref[t] for t in range(3)], axis=1)
        products = [(0, jnp.dot(block, weights, preferred_element_type=F32).astype(BF16))]
    else:
        products = [
            (t * slot, jnp.dot(block, weight_ref[t], preferred_element_type=F32).astype(BF16))
            for t in range(3)
        ]
    at = 0
    for out_ref in outs:
        for left, product in products:
            part = product[at : at + out_ref.shape[0]]
            out_ref[:, left : left + part.shape[1]] = part
        at += out_ref.shape[0]


def project(groups, weights):
    width = weights.shape[1]
    slot = padded(weights.shape[2])
    sizes = [sum(piece.shape[0] for piece in group) for group in groups]
    total = sum(sizes)
    return pl.pallas_call(
        functools.partial(project_kernel, [len(group) for group in groups]),
        out_shape=[jax.ShapeDtypeStruct((size, 3 * slot), BF16) for size in sizes],
        in_specs=[VMEM] * (sum(len(group) for group in groups) + 1),
        out_specs=[VMEM] * len(groups),
        compiler_params=pltpu.CompilerParams(vmem_limit_bytes=24 << 20),
        cost_estimate=pl.CostEstimate(
            flops=2 * total * width * 3 * slot,
            bytes_accessed=2 * (total * width + weights.size + total * 3 * slot),
            transcendentals=0,
        ),
    )(*[piece for group in groups for piece in group], weights)


def attend_kernel(count, parts, ranges, head_width, *refs):
    blocks = refs[:parts]
    query_tags, key_tags, scale_ref = refs[parts : parts + 3]
    outs = refs[parts + 3 :]
    slot = padded(head_width)
    sizes = [block.shape[0] // count for block in blocks]
    low, high = min(lo for lo, _ in ranges), max(hi for _, hi in ranges)
    heads = head_width // CHANNEL_PER_PART
    base = math.log2(math.e) / math.sqrt(CHANNEL_PER_PART)
    tiles = [None] * (slot // LANE)
    for head in range(heads):
        first = head * CHANNEL_PER_PART
        last = first + CHANNEL_PER_PART
        left, right = first // LANE * LANE, padded(last)
        reps = (right - left) // LANE
        lane = lax.broadcasted_iota(jnp.int32, (1, right - left), 1)
        inside = (lane >= first - left) & (lane < last - left)
        queries = jnp.concatenate(
            [b[low * z : high * z, left:right] for b, z in zip(blocks, sizes, strict=True)], axis=0
        )
        tags, at = [], 0
        for z in sizes:
            tags.append(query_tags[at + low * z : at + high * z, :])
            at += count * z
        tags = jnp.concatenate(tags, axis=0)
        queries = jnp.where(inside, queries, jnp.concatenate([tags] * reps, axis=1))
        keys = jnp.concatenate([b[:, slot + left : slot + right] for b in blocks], axis=0)
        tags = key_tags[...]
        keys = jnp.where(inside, keys, jnp.concatenate([tags] * reps, axis=1))
        values = jnp.concatenate([b[:, 2 * slot + left : 2 * slot + right] for b in blocks], axis=0)
        scores = lax.dot_general(
            queries, keys, (((1,), (1,)), ((), ())), preferred_element_type=F32
        )
        row_max = jnp.max(scores, axis=-1, keepdims=True)
        numerators = jnp.exp2((scores - row_max) * (scale_ref[head] * base))
        total = jnp.sum(numerators, axis=-1, keepdims=True)
        mixed = jnp.dot(numerators.astype(BF16), values, preferred_element_type=F32) / total
        for i in range(reps):
            tile = left // LANE + i
            own = mixed[:, i * LANE : (i + 1) * LANE]
            held = tiles[tile]
            tiles[tile] = own if held is None else jnp.where(inside[:, i * LANE : (i + 1) * LANE], own, held)
    result = jnp.concatenate(tiles, axis=1)[:, :head_width].astype(BF16)
    for out_ref, (lo, hi) in zip(outs, ranges, strict=True):
        for offset in range(lo, hi):
            start, into = 0, 0
            for z in sizes:
                at = start + (offset - low) * z
                out_ref[offset - lo, into : into + z, :] = result[at : at + z]
                start += (high - low) * z
                into += z


def attend(blocks, query_tags, key_tags, scales, count, ranges, head_width):
    parts = len(blocks)
    per_offset = sum(b.shape[0] for b in blocks) // count
    pixels = count * per_offset
    asked = sum(hi - lo for lo, hi in ranges) * per_offset
    vmem = pl.BlockSpec(memory_space=pltpu.VMEM)
    heads = head_width // CHANNEL_PER_PART
    return pl.pallas_call(
        functools.partial(attend_kernel, count, parts, ranges, head_width),
        out_shape=[
            jax.ShapeDtypeStruct((hi - lo, per_offset, head_width), BF16) for lo, hi in ranges
        ],
        in_specs=[vmem] * (parts + 2) + [pl.BlockSpec(memory_space=pltpu.SMEM)],
        out_specs=[vmem] * len(ranges),
        compiler_params=pltpu.CompilerParams(vmem_limit_bytes=28 << 20),
        cost_estimate=pl.CostEstimate(
            flops=4 * heads * asked * pixels * 2 * LANE,
            bytes_accessed=2 * pixels * 3 * padded(head_width),
            transcendentals=heads * asked * pixels,
        ),
    )(*blocks, query_tags, key_tags, scales)


def finish_kernel(count, spans, out_spans, *refs):
    refs = list(refs)
    attended = [refs.pop(0) for _ in range(count)]
    weights = [refs.pop(0) for _ in range(count)]
    *sources, out_ref = refs
    total = None
    for piece, weight in zip(attended, weights, strict=True):
        term = jnp.dot(piece[...], weight[...], preferred_element_type=F32)
        total = term if total is None else total + term
    at = 0
    for which, row, left, size, into, column in spans:
        held = sources[which][row, left : left + size, :].astype(F32)
        out_ref[into, column : column + size, :] = (held + total[at : at + size]).astype(BF16)
        at += size
    for which, row, left, size, into, column in out_spans:
        out_ref[into, column : column + size, :] = sources[which][row, left : left + size, :]


def finish(attended, weights, sources, spans, out_spans, shape):
    count = len(weights)
    width = shape[-1]
    pixels = attended[0].shape[0]
    return pl.pallas_call(
        functools.partial(finish_kernel, count, spans, out_spans),
        out_shape=jax.ShapeDtypeStruct(shape, BF16),
        in_specs=[VMEM] * (2 * count + len(sources)),
        out_specs=VMEM,
        compiler_params=pltpu.CompilerParams(vmem_limit_bytes=20 << 20),
        cost_estimate=pl.CostEstimate(
            flops=2 * pixels * width * width, bytes_accessed=2 * width * (width + 3 * pixels), transcendentals=0
        ),
    )(*attended, *weights, *sources)


def send_heads(outs):
    own = [outs[0]]
    for offset in range(1, len(outs)):
        own.append(exchange(outs[offset], offset))
    return [piece[0] for piece in own]


def pick_kernel(place, source_ref, out_ref, semaphore):
    size = out_ref.shape[0]
    start = pl.multiple_of(place() * size, 16)
    copy = pltpu.make_async_copy(source_ref.at[pl.ds(start, size), :], out_ref, semaphore)
    copy.start()
    copy.wait()


def join_kernel(place, own_ref, other_ref, out_ref):
    size = own_ref.shape[0]
    at = place()
    out_ref[pl.ds(pl.multiple_of(at * size, 16), size), :] = own_ref[...]
    out_ref[pl.ds(pl.multiple_of((1 - at) * size, 16), size), :] = other_ref[...]


def small_call(kernel, rows, *operands, spec=VMEM, scratch=()):
    width = operands[0].shape[1]
    return pl.pallas_call(
        kernel,
        out_shape=jax.ShapeDtypeStruct((rows, width), BF16),
        in_specs=[spec] * len(operands),
        out_specs=VMEM,
        scratch_shapes=scratch,
        compiler_params=pltpu.CompilerParams(vmem_limit_bytes=8 << 20),
        cost_estimate=pl.CostEstimate(flops=0, bytes_accessed=4 * rows * width, transcendentals=0),
    )(*operands)


def gather_weights(block):
    levels = []
    rows = block.shape[0]
    for axis in ("member", "win"):
        if lax.axis_size(axis) % 2 == 0 and rows % (32 << len(levels)) == 0:
            levels.append(axis)

    def bit(axis):
        return lax.axis_index(axis) & 1

    def part_index():
        index = 0
        for axis in levels:
            index = index * 2 + bit(axis)
        return index

    pieces = {0: block}
    for mask in masks_of(lax.axis_size("seq")):
        for offset in list(pieces):
            piece = pieces[offset]
            if mask > 1 and levels:
                size = rows >> len(levels)
                part = small_call(
                    functools.partial(pick_kernel, part_index),
                    size,
                    piece,
                    spec=HELD,
                    scratch=[pltpu.SemaphoreType.DMA],
                )
                part = exchange(part, mask)
                for axis in reversed(levels):
                    other = exchange(part, 1, axis)
                    size *= 2
                    part = small_call(functools.partial(join_kernel, functools.partial(bit, axis)), size, part, other)
                pieces[offset ^ mask] = part
            else:
                pieces[offset ^ mask] = exchange(piece, mask)
    return [pieces[offset] for offset in range(len(pieces))]


def on_device(
    pixel_grid_input,
    mask_zone_labeling,
    standardize_multiplier,
    standardize_offset_vector,
    triple_projection_matrix,
    logit_scaling_per_part,
    final_projection_matrix,
):
    count = lax.axis_size("seq")
    blocked = pixel_grid_input[0, :, 0]
    row_count, col_count, width = blocked.shape
    rows = row_count // 2
    half = WS // 2
    head_width = triple_projection_matrix.shape[2]

    def west(source, count):
        return (source - 2) % count

    def west_north(source, count):
        return ((source ^ 1) - 2) % count

    near = WS - half
    gain, bias = standardize_multiplier[None], standardize_offset_vector[None]
    weights = triple_projection_matrix
    scales = logit_scaling_per_part

    local_0, local_1 = norm_local(blocked, gain, bias, [(rows, rows, half, WS), (rows, rows, half + WS, near)])
    south_0, south_1, east, corner = cut(
        blocked, [(0, rows, half, WS), (0, rows, half + WS, near), (rows, rows, 0, half), (0, rows, 0, half)]
    )
    south_0 = exchange(south_0, 1, "win")
    south_1 = exchange(south_1, 1, "win")
    east = permute_by(east, "win", west)
    corner = permute_by(corner, "win", west_north)
    local_0_pieces = gather_pieces(local_0)
    local_1_pieces = gather_pieces(local_1)
    query_0, key_0, query_1, key_1 = region_tags(mask_zone_labeling[0], count, near)
    out_weights = gather_weights(final_projection_matrix)

    spans = [(0, row, 0, WS) for row in range(rows)]
    south_normed = norm([south_0], gain, bias, spans)
    south_pieces = gather_pieces(south_normed)
    local_0_pieces[0] = after(local_0, south_normed)
    local_0, local_1 = project([local_0_pieces, local_1_pieces], weights)
    spans = [(0, row, 0, near) for row in range(rows)]
    spans += [(which, row, 0, half) for which in (1, 2) for row in range(rows)]
    rest_normed = norm([after(south_1, local_0), east, corner], gain, bias, spans)
    rest_pieces = gather_pieces(rest_normed)
    south_pieces[0] = after(south_normed, local_0)
    (south_0_projected,) = project([south_pieces], weights)

    def attend_run(blocks, tags, earlier, lo, hi):
        blocks = [after(blocks[0], *earlier), *blocks[1:]]
        return list(attend(blocks, *tags, scales, count, [(i, i + 1) for i in range(lo, hi)], head_width))

    split = count // 2
    blocks, tags = [local_0, south_0_projected], (query_0, key_0)
    far = attend_run(blocks, tags, [], split, count)
    close = attend_run(blocks, tags, far, 0, split)
    outs_0 = close + far
    rest_pieces[0] = after(rest_normed, *outs_0)
    (rest_projected,) = project([rest_pieces], weights)
    blocks, tags = [local_1, rest_projected], (query_1, key_1)
    far = attend_run(blocks, tags, [], split, count)
    close = attend_run(blocks, tags, far, 0, split)
    outs_1 = close + far

    first = send_heads(outs_0)
    second = send_heads(outs_1)
    first[0] = after(first[0], *outs_1)
    spans = [(0, rows + row, half, WS, row, 0) for row in range(rows)]
    spans += [(1, row, 0, WS, rows + row, 0) for row in range(rows)]
    done = finish(first, out_weights, [blocked, south_0], spans, [], (row_count, WS, width))
    spans = [(0, rows + row, half + WS, near, row, WS) for row in range(rows)]
    spans += [(1, row, 0, near, rows + row, WS) for row in range(rows)]
    spans += [(2, row, 0, half, row, WS + near) for row in range(rows)]
    spans += [(3, row, 0, half, rows + row, WS + near) for row in range(rows)]
    kept = [(4, row, 0, WS, row, 0) for row in range(row_count)]
    mixed = finish(
        second, out_weights, [blocked, south_1, east, corner, done], spans, kept, (row_count, col_count, width)
    )
    return mixed[None, :, None]


def solution(mesh):
    in_specs = (
        P(("member", "win"), None, "seq", None, None),
        P(("member", "win"), None, None),
        P(),
        P(),
        P(None, None, "seq"),
        P("seq"),
        P("seq", None),
    )
    out_specs = P(("member", "win"), None, "seq", None, None)

    return jax.shard_map(on_device, mesh=mesh, in_specs=in_specs, out_specs=out_specs, check_vma=False)
```

```python
import functools
import math

import jax
import jax.numpy as jnp
from jax import lax
from jax.experimental import pallas as pl
from jax.experimental.pallas import tpu as pltpu
from jax.sharding import PartitionSpec as P


CHANNEL_PER_PART = 96
WS = 32
REGIONS = 32
LANE = 128
FAR = -1e30
F32 = jnp.float32
BF16 = jnp.bfloat16


def permute_by(value, axis, move):
    count = lax.axis_size(axis)
    pairs = [(source, move(source, count)) for source in range(count)]
    return lax.ppermute(value, axis, pairs)


def exchange(value, mask, axis="seq"):
    return permute_by(value, axis, lambda source, count: source ^ mask)


def masks_of(count):
    masks = []
    while count > 1:
        count //= 2
        masks.append(count)
    return masks


def gather_pieces(piece):
    pieces = {0: piece}
    for mask in masks_of(lax.axis_size("seq")):
        for offset in list(pieces):
            pieces[offset ^ mask] = exchange(pieces[offset], mask)
    return [pieces[offset] for offset in range(len(pieces))]


def padded(width):
    return (width + LANE - 1) // LANE * LANE


VMEM = pl.BlockSpec(memory_space=pltpu.VMEM)


def after(value, *earlier):
    return lax.optimization_barrier((value, *earlier))[0]


def normalized(held, gain, bias):
    values = held.astype(F32)
    average = jnp.mean(values, axis=-1, keepdims=True)
    centred = values - average
    variance = jnp.mean(centred * centred, axis=-1, keepdims=True)
    return (centred * lax.rsqrt(variance + 1e-05) * gain + bias).astype(BF16)


HELD = pl.BlockSpec(memory_space=pltpu.HBM)


def cut_kernel(boxes, pixel_ref, *refs):
    outs, semaphore = refs[:-1], refs[-1]
    copies = [
        pltpu.make_async_copy(
            pixel_ref.at[pl.ds(row, rows), pl.ds(left, size), :], out_ref, semaphore.at[index]
        )
        for index, ((row, rows, left, size), out_ref) in enumerate(zip(boxes, outs, strict=True))
    ]
    for copy in copies:
        copy.start()
    for copy in copies:
        copy.wait()


def cut(pixels, boxes):
    width = pixels.shape[2]
    return pl.pallas_call(
        functools.partial(cut_kernel, boxes),
        out_shape=[jax.ShapeDtypeStruct((rows, size, width), BF16) for _, rows, _, size in boxes],
        in_specs=[HELD],
        out_specs=[VMEM] * len(boxes),
        scratch_shapes=[pltpu.SemaphoreType.DMA((len(boxes),))],
        compiler_params=pltpu.CompilerParams(vmem_limit_bytes=8 << 20),
        cost_estimate=pl.CostEstimate(flops=0, bytes_accessed=2 * pixels.size, transcendentals=0),
        name="cut",
    )(pixels)


def norm_local_kernel(boxes, pixel_ref, gain_ref, bias_ref, *refs):
    outs, helds, semaphore = refs[: len(boxes)], refs[len(boxes) : -1], refs[-1]
    copies = [
        pltpu.make_async_copy(
            pixel_ref.at[pl.ds(row, rows), pl.ds(left, size), :], held, semaphore.at[index]
        )
        for index, ((row, rows, left, size), held) in enumerate(zip(boxes, helds, strict=True))
    ]
    for copy in copies:
        copy.start()
    gain, bias = gain_ref[...][None], bias_ref[...][None]
    for copy, held, out_ref in zip(copies, helds, outs, strict=True):
        copy.wait()
        size = held.shape[1]
        for row in range(held.shape[0]):
            out_ref[row * size : (row + 1) * size, :] = normalized(held[row], gain, bias)


def norm_local(pixels, gain, bias, boxes):
    width = pixels.shape[2]
    return pl.pallas_call(
        functools.partial(norm_local_kernel, boxes),
        out_shape=[jax.ShapeDtypeStruct((rows * size, width), BF16) for _, rows, _, size in boxes],
        in_specs=[HELD, VMEM, VMEM],
        out_specs=[VMEM] * len(boxes),
        scratch_shapes=[pltpu.VMEM((rows, size, width), BF16) for _, rows, _, size in boxes]
        + [pltpu.SemaphoreType.DMA((len(boxes),))],
        compiler_params=pltpu.CompilerParams(vmem_limit_bytes=8 << 20),
        cost_estimate=pl.CostEstimate(flops=5 * pixels.size, bytes_accessed=2 * pixels.size, transcendentals=0),
        name="norm_local",
    )(pixels, gain, bias)


def norm_kernel(spans, *refs):
    *sources, gain_ref, bias_ref, out_ref = refs
    into = 0
    gain, bias = gain_ref[...][None], bias_ref[...][None]
    for which, row, left, size in spans:
        held = sources[which][row, left : left + size, :]
        out_ref[into : into + size, :] = normalized(held, gain, bias)
        into += size


def norm(sources, gain, bias, spans):
    width = sources[0].shape[-1]
    total = sum(span[-1] for span in spans)
    return pl.pallas_call(
        functools.partial(norm_kernel, spans),
        out_shape=jax.ShapeDtypeStruct((total, width), BF16),
        in_specs=[VMEM] * (len(sources) + 2),
        out_specs=VMEM,
        compiler_params=pltpu.CompilerParams(vmem_limit_bytes=8 << 20),
        cost_estimate=pl.CostEstimate(
            flops=10 * total * width, bytes_accessed=4 * total * width, transcendentals=0
        ),
    )(*sources, gain, bias)


def tag_kernel(count, near, label_ref, *outs):
    query_0, key_0, query_1, key_1 = outs
    row_count, _ = label_ref.shape
    rows = row_count // (2 * count)
    device = lax.axis_index("seq")
    turned = jnp.transpose(label_ref[...].astype(F32)).astype(BF16)
    place = lax.broadcasted_iota(jnp.int32, (row_count, LANE), 0)
    lane = (lax.broadcasted_iota(jnp.int32, (1, LANE), 1) % REGIONS).astype(F32)
    group = count * rows
    for half in range(2):
        for offset in range(count):
            for row in range(rows):
                at = (half * rows + row) * count + jnp.bitwise_xor(device, offset)
                chosen = jnp.where(place == at, 1.0, 0.0).astype(BF16)
                region = jnp.dot(turned, chosen, preferred_element_type=F32)
                same = region == lane
                query = jnp.where(same, 1.0, 0.0).astype(BF16)
                key = jnp.where(same, 0.0, FAR).astype(BF16)
                slot = offset * rows + row
                apart, span = group * near, near + 2 * (WS - near)
                beside = apart + offset * rows * span
                spots = [
                    (query_0, key_0, (half * group + slot) * WS, 0, WS),
                    (query_1, key_1, beside + row * near if half else slot * near, WS, near),
                    (
                        query_1,
                        key_1,
                        beside + rows * near + (half * rows + row) * (WS - near),
                        WS + near,
                        WS - near,
                    ),
                ]
                for query_ref, key_ref, into, left, size in spots:
                    query_ref[into : into + size, :] = query[left : left + size]
                    key_ref[into : into + size, :] = key[left : left + size]


def region_tags(labels, count, near):
    pixels = labels.shape[0] * WS
    return pl.pallas_call(
        functools.partial(tag_kernel, count, near),
        out_shape=[jax.ShapeDtypeStruct((pixels, LANE), BF16)] * 4,
        in_specs=[VMEM],
        out_specs=[VMEM] * 4,
        compiler_params=pltpu.CompilerParams(vmem_limit_bytes=8 << 20),
        cost_estimate=pl.CostEstimate(
            flops=8 * pixels * LANE * labels.shape[0], bytes_accessed=8 * pixels * LANE, transcendentals=0
        ),
        name="tags",
    )(labels)


def project_kernel(counts, *refs):
    groups = []
    for count in counts:
        groups.append(refs[:count])
        refs = refs[count:]
    weight_ref, *outs = refs
    head_width = weight_ref.shape[2]
    slot = padded(head_width)
    block = jnp.concatenate([piece[...] for group in groups for piece in group], axis=0)
    if slot == head_width:
        weights = jnp.concatenate([weight_ref[t] for t in range(3)], axis=1)
        products = [(0, jnp.dot(block, weights, preferred_element_type=F32).astype(BF16))]
    else:
        products = [
            (t * slot, jnp.dot(block, weight_ref[t], preferred_element_type=F32).astype(BF16))
            for t in range(3)
        ]
    at = 0
    for out_ref in outs:
        for left, product in products:
            part = product[at : at + out_ref.shape[0]]
            out_ref[:, left : left + part.shape[1]] = part
        at += out_ref.shape[0]


def project(groups, weights):
    width = weights.shape[1]
    slot = padded(weights.shape[2])
    sizes = [sum(piece.shape[0] for piece in group) for group in groups]
    total = sum(sizes)
    return pl.pallas_call(
        functools.partial(project_kernel, [len(group) for group in groups]),
        out_shape=[jax.ShapeDtypeStruct((size, 3 * slot), BF16) for size in sizes],
        in_specs=[VMEM] * (sum(len(group) for group in groups) + 1),
        out_specs=[VMEM] * len(groups),
        compiler_params=pltpu.CompilerParams(vmem_limit_bytes=24 << 20),
        cost_estimate=pl.CostEstimate(
            flops=2 * total * width * 3 * slot,
            bytes_accessed=2 * (total * width + weights.size + total * 3 * slot),
            transcendentals=0,
        ),
    )(*[piece for group in groups for piece in group], weights)


def attend_kernel(count, parts, ranges, head_width, *refs):
    blocks = refs[:parts]
    query_tags, key_tags, scale_ref = refs[parts : parts + 3]
    outs = refs[parts + 3 :]
    slot = padded(head_width)
    sizes = [block.shape[0] // count for block in blocks]
    low, high = min(lo for lo, _ in ranges), max(hi for _, hi in ranges)
    heads = head_width // CHANNEL_PER_PART
    base = math.log2(math.e) / math.sqrt(CHANNEL_PER_PART)
    tiles = [None] * (slot // LANE)
    for head in range(heads):
        first = head * CHANNEL_PER_PART
        last = first + CHANNEL_PER_PART
        left, right = first // LANE * LANE, padded(last)
        reps = (right - left) // LANE
        lane = lax.broadcasted_iota(jnp.int32, (1, right - left), 1)
        inside = (lane >= first - left) & (lane < last - left)
        queries = jnp.concatenate(
            [b[low * z : high * z, left:right] for b, z in zip(blocks, sizes, strict=True)], axis=0
        )
        tags, at = [], 0
        for z in sizes:
            tags.append(query_tags[at + low * z : at + high * z, :])
            at += count * z
        tags = jnp.concatenate(tags, axis=0)
        queries = jnp.where(inside, queries, jnp.concatenate([tags] * reps, axis=1))
        keys = jnp.concatenate([b[:, slot + left : slot + right] for b in blocks], axis=0)
        tags = key_tags[...]
        keys = jnp.where(inside, keys, jnp.concatenate([tags] * reps, axis=1))
        values = jnp.concatenate([b[:, 2 * slot + left : 2 * slot + right] for b in blocks], axis=0)
        scores = lax.dot_general(
            queries, keys, (((1,), (1,)), ((), ())), preferred_element_type=F32
        )
        row_max = jnp.max(scores, axis=-1, keepdims=True)
        numerators = jnp.exp2((scores - row_max) * (scale_ref[head] * base))
        total = jnp.sum(numerators, axis=-1, keepdims=True)
        mixed = jnp.dot(numerators.astype(BF16), values, preferred_element_type=F32) / total
        for i in range(reps):
            tile = left // LANE + i
            own = mixed[:, i * LANE : (i + 1) * LANE]
            held = tiles[tile]
            tiles[tile] = own if held is None else jnp.where(inside[:, i * LANE : (i + 1) * LANE], own, held)
    result = jnp.concatenate(tiles, axis=1)[:, :head_width].astype(BF16)
    for out_ref, (lo, hi) in zip(outs, ranges, strict=True):
        for offset in range(lo, hi):
            start, into = 0, 0
            for z in sizes:
                at = start + (offset - low) * z
                out_ref[offset - lo, into : into + z, :] = result[at : at + z]
                start += (high - low) * z
                into += z


def attend(blocks, query_tags, key_tags, scales, count, ranges, head_width):
    parts = len(blocks)
    per_offset = sum(b.shape[0] for b in blocks) // count
    pixels = count * per_offset
    asked = sum(hi - lo for lo, hi in ranges) * per_offset
    vmem = pl.BlockSpec(memory_space=pltpu.VMEM)
    heads = head_width // CHANNEL_PER_PART
    return pl.pallas_call(
        functools.partial(attend_kernel, count, parts, ranges, head_width),
        out_shape=[
            jax.ShapeDtypeStruct((hi - lo, per_offset, head_width), BF16) for lo, hi in ranges
        ],
        in_specs=[vmem] * (parts + 2) + [pl.BlockSpec(memory_space=pltpu.SMEM)],
        out_specs=[vmem] * len(ranges),
        compiler_params=pltpu.CompilerParams(vmem_limit_bytes=28 << 20),
        cost_estimate=pl.CostEstimate(
            flops=4 * heads * asked * pixels * 2 * LANE,
            bytes_accessed=2 * pixels * 3 * padded(head_width),
            transcendentals=heads * asked * pixels,
        ),
    )(*blocks, query_tags, key_tags, scales)


def finish_kernel(count, spans, out_spans, *refs):
    refs = list(refs)
    attended = [refs.pop(0) for _ in range(count)]
    weights = [refs.pop(0) for _ in range(count)]
    *sources, out_ref = refs
    total = None
    for piece, weight in zip(attended, weights, strict=True):
        term = jnp.dot(piece[...], weight[...], preferred_element_type=F32)
        total = term if total is None else total + term
    at = 0
    for which, row, left, size, into, column in spans:
        held = sources[which][row, left : left + size, :].astype(F32)
        out_ref[into, column : column + size, :] = (held + total[at : at + size]).astype(BF16)
        at += size
    for which, row, left, size, into, column in out_spans:
        out_ref[into, column : column + size, :] = sources[which][row, left : left + size, :]


def finish(attended, weights, sources, spans, out_spans, shape):
    count = len(weights)
    width = shape[-1]
    pixels = attended[0].shape[0]
    return pl.pallas_call(
        functools.partial(finish_kernel, count, spans, out_spans),
        out_shape=jax.ShapeDtypeStruct(shape, BF16),
        in_specs=[VMEM] * (2 * count + len(sources)),
        out_specs=VMEM,
        compiler_params=pltpu.CompilerParams(vmem_limit_bytes=20 << 20),
        cost_estimate=pl.CostEstimate(
            flops=2 * pixels * width * width, bytes_accessed=2 * width * (width + 3 * pixels), transcendentals=0
        ),
    )(*attended, *weights, *sources)


def send_heads(outs):
    own = [outs[0]]
    for offset in range(1, len(outs)):
        own.append(exchange(outs[offset], offset))
    return [piece[0] for piece in own]


def pick_kernel(place, source_ref, out_ref, semaphore):
    size = out_ref.shape[0]
    start = pl.multiple_of(place() * size, 16)
    copy = pltpu.make_async_copy(source_ref.at[pl.ds(start, size), :], out_ref, semaphore)
    copy.start()
    copy.wait()


def join_kernel(place, own_ref, other_ref, out_ref):
    size = own_ref.shape[0]
    at = place()
    out_ref[pl.ds(pl.multiple_of(at * size, 16), size), :] = own_ref[...]
    out_ref[pl.ds(pl.multiple_of((1 - at) * size, 16), size), :] = other_ref[...]


def small_call(kernel, rows, *operands, spec=VMEM, scratch=()):
    width = operands[0].shape[1]
    return pl.pallas_call(
        kernel,
        out_shape=jax.ShapeDtypeStruct((rows, width), BF16),
        in_specs=[spec] * len(operands),
        out_specs=VMEM,
        scratch_shapes=scratch,
        compiler_params=pltpu.CompilerParams(vmem_limit_bytes=8 << 20),
        cost_estimate=pl.CostEstimate(flops=0, bytes_accessed=4 * rows * width, transcendentals=0),
    )(*operands)


def gather_weights(block):
    levels = []
    rows = block.shape[0]
    for axis in ("member", "win"):
        if lax.axis_size(axis) % 2 == 0 and rows % (32 << len(levels)) == 0:
            levels.append(axis)

    def bit(axis):
        return lax.axis_index(axis) & 1

    def part_index():
        index = 0
        for axis in levels:
            index = index * 2 + bit(axis)
        return index

    pieces = {0: block}
    for mask in masks_of(lax.axis_size("seq")):
        for offset in list(pieces):
            piece = pieces[offset]
            if mask > 1 and levels:
                size = rows >> len(levels)
                part = small_call(
                    functools.partial(pick_kernel, part_index),
                    size,
                    piece,
                    spec=HELD,
                    scratch=[pltpu.SemaphoreType.DMA],
                )
                part = exchange(part, mask)
                for axis in reversed(levels):
                    other = exchange(part, 1, axis)
                    size *= 2
                    part = small_call(functools.partial(join_kernel, functools.partial(bit, axis)), size, part, other)
                pieces[offset ^ mask] = part
            else:
                pieces[offset ^ mask] = exchange(piece, mask)
    return [pieces[offset] for offset in range(len(pieces))]


def on_device(
    pixel_grid_input,
    mask_zone_labeling,
    standardize_multiplier,
    standardize_offset_vector,
    triple_projection_matrix,
    logit_scaling_per_part,
    final_projection_matrix,
):
    count = lax.axis_size("seq")
    blocked = pixel_grid_input[0, :, 0]
    row_count, col_count, width = blocked.shape
    rows = row_count // 2
    half = WS // 2
    head_width = triple_projection_matrix.shape[2]

    def west(source, count):
        return (source - 2) % count

    def west_north(source, count):
        return ((source ^ 1) - 2) % count

    near = WS - half
    gain, bias = standardize_multiplier, standardize_offset_vector
    weights = triple_projection_matrix
    scales = logit_scaling_per_part

    local_0, local_1 = norm_local(blocked, gain, bias, [(rows, rows, half, WS), (rows, rows, half + WS, near)])
    south_0, south_1, east, corner = cut(
        blocked, [(0, rows, half, WS), (0, rows, half + WS, near), (rows, rows, 0, half), (0, rows, 0, half)]
    )
    south_0 = exchange(south_0, 1, "win")
    south_1 = exchange(south_1, 1, "win")
    east = permute_by(east, "win", west)
    corner = permute_by(corner, "win", west_north)
    local_0_pieces = gather_pieces(local_0)
    local_1_pieces = gather_pieces(local_1)
    query_0, key_0, query_1, key_1 = region_tags(mask_zone_labeling[0], count, near)
    out_weights = gather_weights(final_projection_matrix)

    spans = [(0, row, 0, WS) for row in range(rows)]
    south_normed = norm([south_0], gain, bias, spans)
    south_pieces = gather_pieces(south_normed)
    local_0_pieces[0] = after(local_0, south_normed)
    local_0, local_1 = project([local_0_pieces, local_1_pieces], weights)
    spans = [(0, row, 0, near) for row in range(rows)]
    spans += [(which, row, 0, half) for which in (1, 2) for row in range(rows)]
    rest_normed = norm([after(south_1, local_0), east, corner], gain, bias, spans)
    rest_pieces = gather_pieces(rest_normed)
    south_pieces[0] = after(south_normed, local_0)
    (south_0_projected,) = project([south_pieces], weights)

    def attend_run(blocks, tags, earlier, lo, hi):
        blocks = [after(blocks[0], *earlier), *blocks[1:]]
        return list(attend(blocks, *tags, scales, count, [(i, i + 1) for i in range(lo, hi)], head_width))

    split = count // 2
    blocks, tags = [local_0, south_0_projected], (query_0, key_0)
    far = attend_run(blocks, tags, [], split, count)
    close = attend_run(blocks, tags, far, 0, split)
    outs_0 = close + far
    rest_pieces[0] = after(rest_normed, *outs_0)
    (rest_projected,) = project([rest_pieces], weights)
    blocks, tags = [local_1, rest_projected], (query_1, key_1)
    far = attend_run(blocks, tags, [], split, count)
    close = attend_run(blocks, tags, far, 0, split)
    outs_1 = close + far

    first = send_heads(outs_0)
    second = send_heads(outs_1)
    first[0] = after(first[0], *outs_1)
    spans = [(0, rows + row, half, WS, row, 0) for row in range(rows)]
    spans += [(1, row, 0, WS, rows + row, 0) for row in range(rows)]
    done = finish(first, out_weights, [blocked, south_0], spans, [], (row_count, WS, width))
    spans = [(0, rows + row, half + WS, near, row, WS) for row in range(rows)]
    spans += [(1, row, 0, near, rows + row, WS) for row in range(rows)]
    spans += [(2, row, 0, half, row, WS + near) for row in range(rows)]
    spans += [(3, row, 0, half, rows + row, WS + near) for row in range(rows)]
    kept = [(4, row, 0, WS, row, 0) for row in range(row_count)]
    mixed = finish(
        second, out_weights, [blocked, south_1, east, corner, done], spans, kept, (row_count, col_count, width)
    )
    return mixed[None, :, None]


def solution(mesh):
    in_specs = (
        P(("member", "win"), None, "seq", None, None),
        P(("member", "win"), None, None),
        P(),
        P(),
        P(None, None, "seq"),
        P("seq"),
        P("seq", None),
    )
    out_specs = P(("member", "win"), None, "seq", None, None)

    return jax.shard_map(on_device, mesh=mesh, in_specs=in_specs, out_specs=out_specs, check_vma=False)
```

```python
import functools
import math

import jax
import jax.numpy as jnp
from jax import lax
from jax.experimental import pallas as pl
from jax.experimental.pallas import tpu as pltpu
from jax.sharding import PartitionSpec as P


CHANNEL_PER_PART = 96
WS = 32
REGIONS = 32
LANE = 128
FAR = -1e30
ALL_VMEM = 67_043_328
F32 = jnp.float32
BF16 = jnp.bfloat16


def permute_by(value, axis, move):
    count = lax.axis_size(axis)
    pairs = [(source, move(source, count)) for source in range(count)]
    return lax.ppermute(value, axis, pairs)


def exchange(value, mask, axis="seq"):
    return permute_by(value, axis, lambda source, count: source ^ mask)


def masks_of(count):
    masks = []
    while count > 1:
        count //= 2
        masks.append(count)
    return masks


def gather_pieces(piece):
    pieces = {0: piece}
    for mask in masks_of(lax.axis_size("seq")):
        for offset in list(pieces):
            pieces[offset ^ mask] = exchange(pieces[offset], mask)
    return [pieces[offset] for offset in range(len(pieces))]


def padded(width):
    return (width + LANE - 1) // LANE * LANE


VMEM = pl.BlockSpec(memory_space=pltpu.VMEM)


def after(value, *earlier):
    return lax.optimization_barrier((value, *earlier))[0]


def normalized(held, gain, bias):
    values = held.astype(F32)
    average = jnp.mean(values, axis=-1, keepdims=True)
    centred = values - average
    variance = jnp.mean(centred * centred, axis=-1, keepdims=True)
    return (centred * lax.rsqrt(variance + 1e-05) * gain + bias).astype(BF16)


HELD = pl.BlockSpec(memory_space=pltpu.HBM)


def cut_kernel(boxes, pixel_ref, *refs):
    outs, semaphore = refs[:-1], refs[-1]
    copies = [
        pltpu.make_async_copy(
            pixel_ref.at[pl.ds(row, rows), pl.ds(left, size), :], out_ref, semaphore.at[index]
        )
        for index, ((row, rows, left, size), out_ref) in enumerate(zip(boxes, outs, strict=True))
    ]
    for copy in copies:
        copy.start()
    for copy in copies:
        copy.wait()


def cut(pixels, boxes):
    width = pixels.shape[2]
    return pl.pallas_call(
        functools.partial(cut_kernel, boxes),
        out_shape=[jax.ShapeDtypeStruct((rows, size, width), BF16) for _, rows, _, size in boxes],
        in_specs=[HELD],
        out_specs=[VMEM] * len(boxes),
        scratch_shapes=[pltpu.SemaphoreType.DMA((len(boxes),))],
        compiler_params=pltpu.CompilerParams(vmem_limit_bytes=ALL_VMEM - (22 << 20) // 10),
        cost_estimate=pl.CostEstimate(flops=0, bytes_accessed=2 * pixels.size, transcendentals=0),
        name="cut",
    )(pixels)


def norm_local_kernel(boxes, pixel_ref, gain_ref, bias_ref, *refs):
    outs, helds, semaphore = refs[: len(boxes)], refs[len(boxes) : -1], refs[-1]
    copies = [
        pltpu.make_async_copy(
            pixel_ref.at[pl.ds(row, rows), pl.ds(left, size), :], held, semaphore.at[index]
        )
        for index, ((row, rows, left, size), held) in enumerate(zip(boxes, helds, strict=True))
    ]
    for copy in copies:
        copy.start()
    gain, bias = gain_ref[...][None], bias_ref[...][None]
    for copy, held, out_ref in zip(copies, helds, outs, strict=True):
        copy.wait()
        size = held.shape[1]
        for row in range(held.shape[0]):
            out_ref[row * size : (row + 1) * size, :] = normalized(held[row], gain, bias)


def norm_local(pixels, gain, bias, boxes):
    width = pixels.shape[2]
    return pl.pallas_call(
        functools.partial(norm_local_kernel, boxes),
        out_shape=[jax.ShapeDtypeStruct((rows * size, width), BF16) for _, rows, _, size in boxes],
        in_specs=[HELD, VMEM, VMEM],
        out_specs=[VMEM] * len(boxes),
        scratch_shapes=[pltpu.VMEM((rows, size, width), BF16) for _, rows, _, size in boxes]
        + [pltpu.SemaphoreType.DMA((len(boxes),))],
        compiler_params=pltpu.CompilerParams(vmem_limit_bytes=ALL_VMEM - (12 << 20) // 10),
        cost_estimate=pl.CostEstimate(flops=5 * pixels.size, bytes_accessed=2 * pixels.size, transcendentals=0),
        name="norm_local",
    )(pixels, gain, bias)


def norm_kernel(spans, *refs):
    *sources, gain_ref, bias_ref, out_ref = refs
    into = 0
    gain, bias = gain_ref[...][None], bias_ref[...][None]
    for which, row, left, size in spans:
        held = sources[which][row, left : left + size, :]
        out_ref[into : into + size, :] = normalized(held, gain, bias)
        into += size


def norm(sources, gain, bias, spans):
    width = sources[0].shape[-1]
    total = sum(span[-1] for span in spans)
    return pl.pallas_call(
        functools.partial(norm_kernel, spans),
        out_shape=jax.ShapeDtypeStruct((total, width), BF16),
        in_specs=[VMEM] * (len(sources) + 2),
        out_specs=VMEM,
        compiler_params=pltpu.CompilerParams(vmem_limit_bytes=8 << 20),
        cost_estimate=pl.CostEstimate(
            flops=10 * total * width, bytes_accessed=4 * total * width, transcendentals=0
        ),
    )(*sources, gain, bias)


def tag_kernel(count, near, label_ref, weight_ref, *outs):
    del weight_ref
    query_0, key_0, query_1, key_1 = outs
    row_count, _ = label_ref.shape
    rows = row_count // (2 * count)
    device = lax.axis_index("seq")
    turned = jnp.transpose(label_ref[...].astype(F32)).astype(BF16)
    place = lax.broadcasted_iota(jnp.int32, (row_count, LANE), 0)
    lane = (lax.broadcasted_iota(jnp.int32, (1, LANE), 1) % REGIONS).astype(F32)
    group = count * rows
    for half in range(2):
        for offset in range(count):
            for row in range(rows):
                at = (half * rows + row) * count + jnp.bitwise_xor(device, offset)
                chosen = jnp.where(place == at, 1.0, 0.0).astype(BF16)
                region = jnp.dot(turned, chosen, preferred_element_type=F32)
                same = region == lane
                query = jnp.where(same, 1.0, 0.0).astype(BF16)
                key = jnp.where(same, 0.0, FAR).astype(BF16)
                slot = offset * rows + row
                apart, span = group * near, near + 2 * (WS - near)
                beside = apart + offset * rows * span
                spots = [
                    (query_0, key_0, (half * group + slot) * WS, 0, WS),
                    (query_1, key_1, beside + row * near if half else slot * near, WS, near),
                    (
                        query_1,
                        key_1,
                        beside + rows * near + (half * rows + row) * (WS - near),
                        WS + near,
                        WS - near,
                    ),
                ]
                for query_ref, key_ref, into, left, size in spots:
                    query_ref[into : into + size, :] = query[left : left + size]
                    key_ref[into : into + size, :] = key[left : left + size]


def region_tags(labels, weights, count, near):
    pixels = labels.shape[0] * WS
    return pl.pallas_call(
        functools.partial(tag_kernel, count, near),
        out_shape=[jax.ShapeDtypeStruct((pixels, LANE), BF16)] * 4,
        in_specs=[VMEM] * 2,
        out_specs=[VMEM] * 4,
        compiler_params=pltpu.CompilerParams(vmem_limit_bytes=8 << 20),
        cost_estimate=pl.CostEstimate(
            flops=8 * pixels * LANE * labels.shape[0], bytes_accessed=8 * pixels * LANE, transcendentals=0
        ),
        name="tags",
    )(labels, weights)


def project_kernel(counts, *refs):
    groups = []
    for count in counts:
        groups.append(refs[:count])
        refs = refs[count:]
    weight_ref, *outs = refs
    block = jnp.concatenate([piece[...] for group in groups for piece in group], axis=0)
    head_width = weight_ref.shape[2]
    slot = padded(head_width)
    if slot == head_width:
        weights = jnp.concatenate([weight_ref[t] for t in range(3)], axis=1)
        products = [(0, jnp.dot(block, weights, preferred_element_type=F32).astype(BF16))]
    else:
        products = [
            (t * slot, jnp.dot(block, weight_ref[t], preferred_element_type=F32).astype(BF16))
            for t in range(3)
        ]
    at = 0
    for out_ref in outs:
        for left, product in products:
            part = product[at : at + out_ref.shape[0]]
            out_ref[:, left : left + part.shape[1]] = part
        at += out_ref.shape[0]


def project(groups, weights):
    width = groups[0][0].shape[1]
    slot = padded(weights.shape[2])
    sizes = [sum(piece.shape[0] for piece in group) for group in groups]
    total = sum(sizes)
    return pl.pallas_call(
        functools.partial(project_kernel, [len(group) for group in groups]),
        out_shape=[jax.ShapeDtypeStruct((size, 3 * slot), BF16) for size in sizes],
        in_specs=[VMEM] * (sum(len(group) for group in groups) + 1),
        out_specs=[VMEM] * len(groups),
        compiler_params=pltpu.CompilerParams(vmem_limit_bytes=24 << 20),
        cost_estimate=pl.CostEstimate(
            flops=2 * total * width * 3 * slot,
            bytes_accessed=2 * (total * width + weights.size + total * 3 * slot),
            transcendentals=0,
        ),
    )(*[piece for group in groups for piece in group], weights)


def attend_kernel(count, parts, ranges, head_width, *refs):
    blocks = refs[:parts]
    query_tags, key_tags, scale_ref = refs[parts : parts + 3]
    outs = refs[parts + 3 :]
    slot = padded(head_width)
    sizes = [block.shape[0] // count for block in blocks]
    low, high = min(lo for lo, _ in ranges), max(hi for _, hi in ranges)
    heads = head_width // CHANNEL_PER_PART
    base = math.log2(math.e) / math.sqrt(CHANNEL_PER_PART)
    tiles = [None] * (slot // LANE)
    key_rows = key_tags[...]
    query_rows, at = [], 0
    for z in sizes:
        query_rows.append(query_tags[at + low * z : at + high * z, :])
        at += count * z
    query_rows = jnp.concatenate(query_rows, axis=0)

    def span(head):
        first = head * CHANNEL_PER_PART
        last = first + CHANNEL_PER_PART
        left, right = first // LANE * LANE, padded(last)
        lane = lax.broadcasted_iota(jnp.int32, (1, right - left), 1)
        return left, right, (lane >= first - left) & (lane < last - left)

    def scores_of(head):
        left, right, inside = span(head)
        reps = (right - left) // LANE
        queries = jnp.concatenate(
            [b[low * z : high * z, left:right] for b, z in zip(blocks, sizes, strict=True)], axis=0
        )
        queries = jnp.where(inside, queries, jnp.concatenate([query_rows] * reps, axis=1))
        keys = jnp.concatenate([b[:, slot + left : slot + right] for b in blocks], axis=0)
        keys = jnp.where(inside, keys, jnp.concatenate([key_rows] * reps, axis=1))
        return lax.dot_general(queries, keys, (((1,), (1,)), ((), ())), preferred_element_type=F32)

    following = scores_of(0)
    for head in range(heads):
        scores = following
        if head + 1 < heads:
            following = scores_of(head + 1)
        left, right, inside = span(head)
        row_max = jnp.max(scores, axis=-1, keepdims=True)
        numerators = jnp.exp2((scores - row_max) * (scale_ref[head] * base))
        total = jnp.sum(numerators, axis=-1, keepdims=True)
        values = jnp.concatenate([b[:, 2 * slot + left : 2 * slot + right] for b in blocks], axis=0)
        mixed = jnp.dot(numerators.astype(BF16), values, preferred_element_type=F32) / total
        for i in range((right - left) // LANE):
            tile = left // LANE + i
            own = mixed[:, i * LANE : (i + 1) * LANE]
            held = tiles[tile]
            tiles[tile] = own if held is None else jnp.where(inside[:, i * LANE : (i + 1) * LANE], own, held)
    result = jnp.concatenate(tiles, axis=1)[:, :head_width].astype(BF16)
    for out_ref, (lo, hi) in zip(outs, ranges, strict=True):
        for offset in range(lo, hi):
            start, into = 0, 0
            for z in sizes:
                at = start + (offset - low) * z
                out_ref[offset - lo, into : into + z, :] = result[at : at + z]
                start += (high - low) * z
                into += z


def attend(blocks, query_tags, key_tags, scales, count, ranges, head_width):
    parts = len(blocks)
    per_offset = sum(b.shape[0] for b in blocks) // count
    pixels = count * per_offset
    asked = sum(hi - lo for lo, hi in ranges) * per_offset
    vmem = pl.BlockSpec(memory_space=pltpu.VMEM)
    heads = head_width // CHANNEL_PER_PART
    return pl.pallas_call(
        functools.partial(attend_kernel, count, parts, ranges, head_width),
        out_shape=[
            jax.ShapeDtypeStruct((hi - lo, per_offset, head_width), BF16) for lo, hi in ranges
        ],
        in_specs=[vmem] * (parts + 2) + [pl.BlockSpec(memory_space=pltpu.SMEM)],
        out_specs=[vmem] * len(ranges),
        compiler_params=pltpu.CompilerParams(vmem_limit_bytes=28 << 20),
        cost_estimate=pl.CostEstimate(
            flops=4 * heads * asked * pixels * 2 * LANE,
            bytes_accessed=2 * pixels * 3 * padded(head_width),
            transcendentals=heads * asked * pixels,
        ),
    )(*blocks, query_tags, key_tags, scales)


def product(attended, weights, columns=slice(None)):
    total = None
    for piece, weight in zip(attended, weights, strict=True):
        term = jnp.dot(piece[...], weight[:, columns], preferred_element_type=F32)
        total = term if total is None else total + term
    return total


def partial_kernel(count, *refs):
    *refs, out_ref = refs
    out_ref[...] = product(refs[:count], refs[count:])


def partial(attended, weights):
    pixels, depth = attended[0].shape
    width = weights[0].shape[1]
    return pl.pallas_call(
        functools.partial(partial_kernel, len(weights)),
        out_shape=jax.ShapeDtypeStruct((pixels, width), F32),
        in_specs=[VMEM] * (2 * len(weights)),
        out_specs=VMEM,
        compiler_params=pltpu.CompilerParams(vmem_limit_bytes=20 << 20),
        cost_estimate=pl.CostEstimate(
            flops=2 * pixels * width * depth * len(weights), bytes_accessed=2 * width * (depth + 2 * pixels), transcendentals=0
        ),
    )(*attended, *weights)


def finish_kernel(count, chunks, spans, box, with_base, with_held, *refs):
    refs = list(refs)
    attended = [refs.pop(0) for _ in range(count)]
    weights = [refs.pop(0) for _ in range(count)]
    base_ref = refs.pop(0) if with_base else None
    if with_held:
        refs.pop(0)
    *sources, out_ref, ready, semaphore = refs
    left, size = box
    wide = out_ref.shape[2] // chunks
    copies = []
    for chunk in range(chunks):
        columns = slice(chunk * wide, (chunk + 1) * wide)
        total = product(attended, weights, columns)
        if base_ref is not None:
            total = total + base_ref[:, columns]
        at = 0
        for which, row, start, pixels, into, column in spans:
            held = sources[which][row, start : start + pixels, columns].astype(F32)
            ready[into, column - left : column - left + pixels, columns] = (
                held + total[at : at + pixels]
            ).astype(BF16)
            at += pixels
        place = pl.ds(chunk * wide, wide)
        copy = pltpu.make_async_copy(
            ready.at[:, :, place], out_ref.at[:, pl.ds(left, size), place], semaphore.at[chunk]
        )
        copy.start()
        copies.append(copy)
    for copy in copies:
        copy.wait()


def finish(attended, weights, base, held, sources, spans, box, shape):
    count = len(weights)
    row_count, _, width = shape
    pixels = attended[0].shape[0]
    chunks = 3 if width % (3 * 2 * LANE) == 0 else 1
    operands = [*attended, *weights, *([] if base is None else [base])]
    specs = [VMEM] * len(operands)
    aliases = {}
    if held is not None:
        aliases = {len(operands): 0}
        operands.append(held)
        specs.append(HELD)
    return pl.pallas_call(
        functools.partial(finish_kernel, count, chunks, spans, box, base is not None, held is not None),
        out_shape=jax.ShapeDtypeStruct(shape, BF16),
        in_specs=specs + [VMEM] * len(sources),
        out_specs=HELD,
        scratch_shapes=[pltpu.VMEM((row_count, box[1], width), BF16), pltpu.SemaphoreType.DMA((chunks,))],
        input_output_aliases=aliases,
        compiler_params=pltpu.CompilerParams(vmem_limit_bytes=20 << 20),
        cost_estimate=pl.CostEstimate(
            flops=2 * pixels * width * width, bytes_accessed=2 * width * (width + 3 * pixels), transcendentals=0
        ),
    )(*operands, *sources)


def send_heads(outs):
    own = [outs[0]]
    for offset in range(1, len(outs)):
        own.append(exchange(outs[offset], offset))
    return [piece[0] for piece in own]


def pick_kernel(place, source_ref, out_ref, semaphore):
    size = out_ref.shape[0]
    start = pl.multiple_of(place() * size, 16)
    copy = pltpu.make_async_copy(source_ref.at[pl.ds(start, size), :], out_ref, semaphore)
    copy.start()
    copy.wait()


def join_kernel(place, own_ref, other_ref, out_ref):
    size = own_ref.shape[0]
    at = place()
    out_ref[pl.ds(pl.multiple_of(at * size, 16), size), :] = own_ref[...]
    out_ref[pl.ds(pl.multiple_of((1 - at) * size, 16), size), :] = other_ref[...]


def small_call(kernel, rows, *operands, spec=VMEM, scratch=()):
    width = operands[0].shape[1]
    return pl.pallas_call(
        kernel,
        out_shape=jax.ShapeDtypeStruct((rows, width), BF16),
        in_specs=[spec] * len(operands),
        out_specs=VMEM,
        scratch_shapes=scratch,
        compiler_params=pltpu.CompilerParams(vmem_limit_bytes=8 << 20),
        cost_estimate=pl.CostEstimate(flops=0, bytes_accessed=4 * rows * width, transcendentals=0),
    )(*operands)


def gather_weights(block):
    levels = []
    rows = block.shape[0]
    for axis in ("member", "win"):
        if lax.axis_size(axis) % 2 == 0 and rows % (32 << len(levels)) == 0:
            levels.append(axis)

    def bit(axis):
        return lax.axis_index(axis) & 1

    def part_index():
        index = 0
        for axis in levels:
            index = index * 2 + bit(axis)
        return index

    pieces = {0: block}
    for mask in masks_of(lax.axis_size("seq")):
        for offset in list(pieces):
            piece = pieces[offset]
            if mask > 1 and levels:
                size = rows >> len(levels)
                part = small_call(
                    functools.partial(pick_kernel, part_index),
                    size,
                    piece,
                    spec=HELD,
                    scratch=[pltpu.SemaphoreType.DMA],
                )
                part = exchange(part, mask)
                for axis in reversed(levels):
                    other = exchange(part, 1, axis)
                    size *= 2
                    part = small_call(functools.partial(join_kernel, functools.partial(bit, axis)), size, part, other)
                pieces[offset ^ mask] = part
            else:
                pieces[offset ^ mask] = exchange(piece, mask)
    return [pieces[offset] for offset in range(len(pieces))]


def on_device(
    pixel_grid_input,
    mask_zone_labeling,
    standardize_multiplier,
    standardize_offset_vector,
    triple_projection_matrix,
    logit_scaling_per_part,
    final_projection_matrix,
):
    count = lax.axis_size("seq")
    blocked = pixel_grid_input[0, :, 0]
    row_count, col_count, width = blocked.shape
    rows = row_count // 2
    half = WS // 2
    head_width = triple_projection_matrix.shape[2]

    def west(source, count):
        return (source - 2) % count

    def west_north(source, count):
        return ((source ^ 1) - 2) % count

    near = WS - half
    gain, bias = standardize_multiplier, standardize_offset_vector
    weights = triple_projection_matrix
    scales = logit_scaling_per_part

    local_0, local_1 = norm_local(blocked, gain, bias, [(rows, rows, half, WS), (rows, rows, half + WS, near)])
    south_0, south_1, east, corner = cut(
        blocked, [(0, rows, half, WS), (0, rows, half + WS, near), (rows, rows, 0, half), (0, rows, 0, half)]
    )
    south_0 = exchange(south_0, 1, "win")
    south_1 = exchange(south_1, 1, "win")
    east = permute_by(east, "win", west)
    corner = permute_by(corner, "win", west_north)
    local_0_pieces = gather_pieces(local_0)
    local_1_pieces = gather_pieces(local_1)
    query_0, key_0, query_1, key_1 = region_tags(mask_zone_labeling[0], weights, count, near)
    out_weights = gather_weights(final_projection_matrix)

    spans = [(0, row, 0, WS) for row in range(rows)]
    south_normed = norm([south_0], gain, bias, spans)
    south_pieces = gather_pieces(south_normed)
    local_0_pieces[0] = after(local_0, south_normed)
    local_0, local_1 = project([local_0_pieces, local_1_pieces], weights)
    spans = [(0, row, 0, near) for row in range(rows)]
    spans += [(which, row, 0, half) for which in (1, 2) for row in range(rows)]
    rest_normed = norm([after(south_1, local_0), east, corner], gain, bias, spans)
    rest_pieces = gather_pieces(rest_normed)
    south_pieces[0] = after(south_normed, local_0)
    (south_0_projected,) = project([south_pieces], weights)

    def attend_run(blocks, tags, earlier, lo, hi):
        blocks = [after(blocks[0], *earlier), *blocks[1:]]
        return list(attend(blocks, *tags, scales, count, [(i, i + 1) for i in range(lo, hi)], head_width))

    split = count // 2
    blocks, tags = [local_0, south_0_projected], (query_0, key_0)
    far = attend_run(blocks, tags, [], split, count)
    close = attend_run(blocks, tags, far, 0, split)
    outs_0 = close + far
    rest_pieces[0] = after(rest_normed, *outs_0)
    (rest_projected,) = project([rest_pieces], weights)
    blocks, tags = [local_1, rest_projected], (query_1, key_1)
    far = attend_run(blocks, tags, [], split, count)
    close = attend_run(blocks, tags, far, 0, split)
    outs_1 = close + far

    first = send_heads(outs_0)
    second = send_heads(outs_1)
    first[0] = after(first[0], *outs_1)
    spans = [(0, rows + row, half, WS, row, 0) for row in range(rows)]
    spans += [(1, row, 0, WS, rows + row, 0) for row in range(rows)]
    shape = (row_count, col_count, width)
    done = finish(first, out_weights, None, None, [blocked, south_0], spans, (0, WS), shape)
    second[0] = after(second[0], done)
    base = partial(second[:split], out_weights[:split])
    spans = [(0, rows + row, half + WS, near, row, WS) for row in range(rows)]
    spans += [(1, row, 0, near, rows + row, WS) for row in range(rows)]
    spans += [(2, row, 0, half, row, WS + near) for row in range(rows)]
    spans += [(3, row, 0, half, rows + row, WS + near) for row in range(rows)]
    mixed = finish(
        second[split:], out_weights[split:], base, done, [blocked, south_1, east, corner], spans, (WS, WS), shape
    )
    return mixed[None, :, None]


def solution(mesh):
    in_specs = (
        P(("member", "win"), None, "seq", None, None),
        P(("member", "win"), None, None),
        P(),
        P(),
        P(None, None, "seq"),
        P("seq"),
        P("seq", None),
    )
    out_specs = P(("member", "win"), None, "seq", None, None)

    return jax.shard_map(on_device, mesh=mesh, in_specs=in_specs, out_specs=out_specs, check_vma=False)
```

```python
import functools
import math

import jax
import jax.numpy as jnp
from jax import lax
from jax.experimental import pallas as pl
from jax.experimental.pallas import tpu as pltpu
from jax.sharding import PartitionSpec as P


CHANNEL_PER_PART = 96
WS = 32
REGIONS = 32
LANE = 128
FAR = -1e30
F32 = jnp.float32
BF16 = jnp.bfloat16


def permute_by(value, axis, move):
    count = lax.axis_size(axis)
    pairs = [(source, move(source, count)) for source in range(count)]
    return lax.ppermute(value, axis, pairs)


def exchange(value, mask, axis="seq"):
    return permute_by(value, axis, lambda source, count: source ^ mask)


def masks_of(count):
    masks = []
    while count > 1:
        count //= 2
        masks.append(count)
    return masks


def gather_pieces(piece):
    pieces = {0: piece}
    for mask in masks_of(lax.axis_size("seq")):
        for offset in list(pieces):
            pieces[offset ^ mask] = exchange(pieces[offset], mask)
    return [pieces[offset] for offset in range(len(pieces))]


def padded(width):
    return (width + LANE - 1) // LANE * LANE


VMEM = pl.BlockSpec(memory_space=pltpu.VMEM)


def after(value, *earlier):
    return lax.optimization_barrier((value, *earlier))[0]


def normalized(held, gain, bias):
    values = held.astype(F32)
    average = jnp.mean(values, axis=-1, keepdims=True)
    centred = values - average
    variance = jnp.mean(centred * centred, axis=-1, keepdims=True)
    return (centred * lax.rsqrt(variance + 1e-05) * gain + bias).astype(BF16)


HELD = pl.BlockSpec(memory_space=pltpu.HBM)


def cut_kernel(boxes, pixel_ref, *outs):
    for (row, left, size), out_ref in zip(boxes, outs, strict=True):
        out_ref[...] = pixel_ref[row : row + out_ref.shape[0], left : left + size, :]


def cut(pixels, rows, boxes):
    width = pixels.shape[2]
    return pl.pallas_call(
        functools.partial(cut_kernel, boxes),
        out_shape=[jax.ShapeDtypeStruct((rows, size, width), BF16) for _, _, size in boxes],
        in_specs=[VMEM],
        out_specs=[VMEM] * len(boxes),
        compiler_params=pltpu.CompilerParams(vmem_limit_bytes=8 << 20),
        cost_estimate=pl.CostEstimate(flops=0, bytes_accessed=2 * pixels.size, transcendentals=0),
        name="cut",
    )(pixels)


def norm_kernel(groups, *refs):
    refs, outs = refs[: -len(groups)], refs[-len(groups) :]
    *sources, gain_ref, bias_ref = refs
    gain, bias = gain_ref[...][None], bias_ref[...][None]
    for spans, out_ref in zip(groups, outs, strict=True):
        into = 0
        for which, row, left, size in spans:
            held = sources[which][row, left : left + size, :]
            out_ref[into : into + size, :] = normalized(held, gain, bias)
            into += size


def norm(sources, gain, bias, groups):
    width = sources[0].shape[-1]
    totals = [sum(span[-1] for span in spans) for spans in groups]
    return pl.pallas_call(
        functools.partial(norm_kernel, groups),
        out_shape=[jax.ShapeDtypeStruct((total, width), BF16) for total in totals],
        in_specs=[VMEM] * (len(sources) + 2),
        out_specs=[VMEM] * len(groups),
        compiler_params=pltpu.CompilerParams(vmem_limit_bytes=8 << 20),
        cost_estimate=pl.CostEstimate(
            flops=10 * sum(totals) * width, bytes_accessed=4 * sum(totals) * width, transcendentals=0
        ),
    )(*sources, gain, bias)


def tag_kernel(count, near, label_ref, weight_ref, *outs):
    del weight_ref
    query_0, key_0, query_1, key_1 = outs
    row_count, _ = label_ref.shape
    rows = row_count // (2 * count)
    device = lax.axis_index("seq")
    turned = jnp.transpose(label_ref[...].astype(F32)).astype(BF16)
    place = lax.broadcasted_iota(jnp.int32, (row_count, LANE), 0)
    lane = (lax.broadcasted_iota(jnp.int32, (1, LANE), 1) % REGIONS).astype(F32)
    group = count * rows
    for half in range(2):
        for offset in range(count):
            for row in range(rows):
                at = (half * rows + row) * count + jnp.bitwise_xor(device, offset)
                chosen = jnp.where(place == at, 1.0, 0.0).astype(BF16)
                region = jnp.dot(turned, chosen, preferred_element_type=F32)
                same = region == lane
                query = jnp.where(same, 1.0, 0.0).astype(BF16)
                key = jnp.where(same, 0.0, FAR).astype(BF16)
                slot = offset * rows + row
                apart, span = group * near, near + 2 * (WS - near)
                beside = apart + offset * rows * span
                spots = [
                    (query_0, key_0, (half * group + slot) * WS, 0, WS),
                    (query_1, key_1, beside + row * near if half else slot * near, WS, near),
                    (
                        query_1,
                        key_1,
                        beside + rows * near + (half * rows + row) * (WS - near),
                        WS + near,
                        WS - near,
                    ),
                ]
                for query_ref, key_ref, into, left, size in spots:
                    query_ref[into : into + size, :] = query[left : left + size]
                    key_ref[into : into + size, :] = key[left : left + size]


def region_tags(labels, weights, count, near):
    pixels = labels.shape[0] * WS
    return pl.pallas_call(
        functools.partial(tag_kernel, count, near),
        out_shape=[jax.ShapeDtypeStruct((pixels, LANE), BF16)] * 4,
        in_specs=[VMEM] * 2,
        out_specs=[VMEM] * 4,
        compiler_params=pltpu.CompilerParams(vmem_limit_bytes=8 << 20),
        cost_estimate=pl.CostEstimate(
            flops=8 * pixels * LANE * labels.shape[0], bytes_accessed=8 * pixels * LANE, transcendentals=0
        ),
        name="tags",
    )(labels, weights)


def project_kernel(counts, *refs):
    groups = []
    for count in counts:
        groups.append(refs[:count])
        refs = refs[count:]
    weight_ref, *outs = refs
    block = jnp.concatenate([piece[...] for group in groups for piece in group], axis=0)
    head_width = weight_ref.shape[2]
    slot = padded(head_width)
    if slot == head_width:
        weights = jnp.concatenate([weight_ref[t] for t in range(3)], axis=1)
        products = [(0, jnp.dot(block, weights, preferred_element_type=F32).astype(BF16))]
    else:
        products = [
            (t * slot, jnp.dot(block, weight_ref[t], preferred_element_type=F32).astype(BF16))
            for t in range(3)
        ]
    at = 0
    for out_ref in outs:
        for left, product in products:
            part = product[at : at + out_ref.shape[0]]
            out_ref[:, left : left + part.shape[1]] = part
        at += out_ref.shape[0]


def project(groups, weights):
    width = groups[0][0].shape[1]
    slot = padded(weights.shape[2])
    sizes = [sum(piece.shape[0] for piece in group) for group in groups]
    total = sum(sizes)
    return pl.pallas_call(
        functools.partial(project_kernel, [len(group) for group in groups]),
        out_shape=[jax.ShapeDtypeStruct((size, 3 * slot), BF16) for size in sizes],
        in_specs=[VMEM] * (sum(len(group) for group in groups) + 1),
        out_specs=[VMEM] * len(groups),
        compiler_params=pltpu.CompilerParams(vmem_limit_bytes=24 << 20),
        cost_estimate=pl.CostEstimate(
            flops=2 * total * width * 3 * slot,
            bytes_accessed=2 * (total * width + weights.size + total * 3 * slot),
            transcendentals=0,
        ),
    )(*[piece for group in groups for piece in group], weights)


def attend_kernel(count, parts, ranges, head_width, *refs):
    blocks = refs[:parts]
    query_tags, key_tags, scale_ref = refs[parts : parts + 3]
    outs = refs[parts + 3 :]
    slot = padded(head_width)
    sizes = [block.shape[0] // count for block in blocks]
    low, high = min(lo for lo, _ in ranges), max(hi for _, hi in ranges)
    heads = head_width // CHANNEL_PER_PART
    base = math.log2(math.e) / math.sqrt(CHANNEL_PER_PART)
    tiles = [None] * (slot // LANE)
    key_rows = key_tags[...]
    query_rows, at = [], 0
    for z in sizes:
        query_rows.append(query_tags[at + low * z : at + high * z, :])
        at += count * z
    query_rows = jnp.concatenate(query_rows, axis=0)

    def span(head):
        first = head * CHANNEL_PER_PART
        last = first + CHANNEL_PER_PART
        left, right = first // LANE * LANE, padded(last)
        lane = lax.broadcasted_iota(jnp.int32, (1, right - left), 1)
        return left, right, (lane >= first - left) & (lane < last - left)

    def scores_of(head):
        left, right, inside = span(head)
        reps = (right - left) // LANE
        queries = jnp.concatenate(
            [b[low * z : high * z, left:right] for b, z in zip(blocks, sizes, strict=True)], axis=0
        )
        queries = jnp.where(inside, queries, jnp.concatenate([query_rows] * reps, axis=1))
        keys = jnp.concatenate([b[:, slot + left : slot + right] for b in blocks], axis=0)
        keys = jnp.where(inside, keys, jnp.concatenate([key_rows] * reps, axis=1))
        return lax.dot_general(queries, keys, (((1,), (1,)), ((), ())), preferred_element_type=F32)

    following = scores_of(0)
    for head in range(heads):
        scores = following
        if head + 1 < heads:
            following = scores_of(head + 1)
        left, right, inside = span(head)
        row_max = jnp.max(scores, axis=-1, keepdims=True)
        numerators = jnp.exp2((scores - row_max) * (scale_ref[head] * base))
        total = jnp.sum(numerators, axis=-1, keepdims=True)
        values = jnp.concatenate([b[:, 2 * slot + left : 2 * slot + right] for b in blocks], axis=0)
        mixed = jnp.dot(numerators.astype(BF16), values, preferred_element_type=F32) / total
        for i in range((right - left) // LANE):
            tile = left // LANE + i
            own = mixed[:, i * LANE : (i + 1) * LANE]
            held = tiles[tile]
            tiles[tile] = own if held is None else jnp.where(inside[:, i * LANE : (i + 1) * LANE], own, held)
    result = jnp.concatenate(tiles, axis=1)[:, :head_width].astype(BF16)
    for out_ref, (lo, hi) in zip(outs, ranges, strict=True):
        for offset in range(lo, hi):
            start, into = 0, 0
            for z in sizes:
                at = start + (offset - low) * z
                out_ref[offset - lo, into : into + z, :] = result[at : at + z]
                start += (high - low) * z
                into += z


def attend(blocks, query_tags, key_tags, scales, count, ranges, head_width):
    parts = len(blocks)
    per_offset = sum(b.shape[0] for b in blocks) // count
    pixels = count * per_offset
    asked = sum(hi - lo for lo, hi in ranges) * per_offset
    vmem = pl.BlockSpec(memory_space=pltpu.VMEM)
    heads = head_width // CHANNEL_PER_PART
    return pl.pallas_call(
        functools.partial(attend_kernel, count, parts, ranges, head_width),
        out_shape=[
            jax.ShapeDtypeStruct((hi - lo, per_offset, head_width), BF16) for lo, hi in ranges
        ],
        in_specs=[vmem] * (parts + 2) + [pl.BlockSpec(memory_space=pltpu.SMEM)],
        out_specs=[vmem] * len(ranges),
        compiler_params=pltpu.CompilerParams(vmem_limit_bytes=28 << 20),
        cost_estimate=pl.CostEstimate(
            flops=4 * heads * asked * pixels * 2 * LANE,
            bytes_accessed=2 * pixels * 3 * padded(head_width),
            transcendentals=heads * asked * pixels,
        ),
    )(*blocks, query_tags, key_tags, scales)


def product(attended, weights, columns=slice(None)):
    total = None
    for piece, weight in zip(attended, weights, strict=True):
        term = jnp.dot(piece[...], weight[:, columns], preferred_element_type=F32)
        total = term if total is None else total + term
    return total


def partial_kernel(count, *refs):
    *refs, out_ref = refs
    out_ref[...] = product(refs[:count], refs[count:])


def partial(attended, weights):
    pixels, depth = attended[0].shape
    width = weights[0].shape[1]
    return pl.pallas_call(
        functools.partial(partial_kernel, len(weights)),
        out_shape=jax.ShapeDtypeStruct((pixels, width), F32),
        in_specs=[VMEM] * (2 * len(weights)),
        out_specs=VMEM,
        compiler_params=pltpu.CompilerParams(vmem_limit_bytes=20 << 20),
        cost_estimate=pl.CostEstimate(
            flops=2 * pixels * width * depth * len(weights), bytes_accessed=2 * width * (depth + 2 * pixels), transcendentals=0
        ),
    )(*attended, *weights)


def finish_kernel(count, spans, *refs):
    attended, weights, sources, out_ref = refs[:count], refs[count : 2 * count], refs[2 * count : -1], refs[-1]
    total = product(attended, weights)
    at = 0
    for which, row, start, pixels, into, column in spans:
        held = sources[which][row, start : start + pixels, :].astype(F32)
        out_ref[into, column : column + pixels, :] = (held + total[at : at + pixels]).astype(BF16)
        at += pixels


def finish(attended, weights, sources, spans, shape):
    count = len(weights)
    pixels, width = attended[0].shape[0], shape[-1]
    return pl.pallas_call(
        functools.partial(finish_kernel, count, spans),
        out_shape=jax.ShapeDtypeStruct(shape, BF16),
        in_specs=[VMEM] * (2 * count + len(sources)),
        out_specs=VMEM,
        compiler_params=pltpu.CompilerParams(vmem_limit_bytes=20 << 20),
        cost_estimate=pl.CostEstimate(
            flops=2 * pixels * width * width, bytes_accessed=2 * width * (width + 3 * pixels), transcendentals=0
        ),
    )(*attended, *weights, *sources)


def last_kernel(count, chunks, spans, *refs):
    attended, weights = refs[:count], refs[count : 2 * count]
    base_ref, done_ref, *sources, out_ref, ready, semaphore = refs[2 * count :]
    left, size, width = done_ref.shape[1], ready.shape[1], ready.shape[2]
    wide = width // chunks
    copies = [
        pltpu.make_async_copy(done_ref, out_ref.at[:, pl.ds(0, left), :], semaphore.at[chunks])
    ]
    copies[0].start()
    for chunk in range(chunks):
        columns = slice(chunk * wide, (chunk + 1) * wide)
        total = product(attended, weights, columns) + base_ref[:, columns]
        at = 0
        for which, row, start, pixels, into, column in spans:
            held = sources[which][row, start : start + pixels, columns].astype(F32)
            ready[into, column - left : column - left + pixels, columns] = (
                held + total[at : at + pixels]
            ).astype(BF16)
            at += pixels
        place = pl.ds(chunk * wide, wide)
        copy = pltpu.make_async_copy(
            ready.at[:, :, place], out_ref.at[:, pl.ds(left, size), place], semaphore.at[chunk]
        )
        copy.start()
        copies.append(copy)
    for copy in copies:
        copy.wait()


def finish_last(attended, weights, base, done, sources, spans, shape):
    count = len(weights)
    row_count, col_count, width = shape
    pixels, depth = attended[0].shape
    chunks = 3 if width % (3 * 2 * LANE) == 0 else 1
    return pl.pallas_call(
        functools.partial(last_kernel, count, chunks, spans),
        out_shape=jax.ShapeDtypeStruct(shape, BF16),
        in_specs=[VMEM] * (2 * count + 2 + len(sources)),
        out_specs=HELD,
        scratch_shapes=[
            pltpu.VMEM((row_count, col_count - done.shape[1], width), BF16),
            pltpu.SemaphoreType.DMA((chunks + 1,)),
        ],
        compiler_params=pltpu.CompilerParams(vmem_limit_bytes=20 << 20),
        cost_estimate=pl.CostEstimate(
            flops=2 * pixels * width * depth * count, bytes_accessed=2 * width * (width + 3 * pixels), transcendentals=0
        ),
    )(*attended, *weights, base, done, *sources)


def send_heads(outs):
    own = [outs[0]]
    for offset in range(1, len(outs)):
        own.append(exchange(outs[offset], offset))
    return [piece[0] for piece in own]


def pick_kernel(place, source_ref, out_ref, semaphore):
    size = out_ref.shape[0]
    start = pl.multiple_of(place() * size, 16)
    copy = pltpu.make_async_copy(source_ref.at[pl.ds(start, size), :], out_ref, semaphore)
    copy.start()
    copy.wait()


def join_kernel(place, own_ref, other_ref, out_ref):
    size = own_ref.shape[0]
    at = place()
    out_ref[pl.ds(pl.multiple_of(at * size, 16), size), :] = own_ref[...]
    out_ref[pl.ds(pl.multiple_of((1 - at) * size, 16), size), :] = other_ref[...]


def small_call(kernel, rows, *operands, spec=VMEM, scratch=()):
    width = operands[0].shape[1]
    return pl.pallas_call(
        kernel,
        out_shape=jax.ShapeDtypeStruct((rows, width), BF16),
        in_specs=[spec] * len(operands),
        out_specs=VMEM,
        scratch_shapes=scratch,
        compiler_params=pltpu.CompilerParams(vmem_limit_bytes=8 << 20),
        cost_estimate=pl.CostEstimate(flops=0, bytes_accessed=4 * rows * width, transcendentals=0),
    )(*operands)


def gather_weights(block):
    levels = []
    rows = block.shape[0]
    for axis in ("member", "win"):
        if lax.axis_size(axis) % 2 == 0 and rows % (32 << len(levels)) == 0:
            levels.append(axis)

    def bit(axis):
        return lax.axis_index(axis) & 1

    def part_index():
        index = 0
        for axis in levels:
            index = index * 2 + bit(axis)
        return index

    pieces = {0: block}
    for mask in masks_of(lax.axis_size("seq")):
        for offset in list(pieces):
            piece = pieces[offset]
            if mask > 1 and levels:
                size = rows >> len(levels)
                part = small_call(
                    functools.partial(pick_kernel, part_index),
                    size,
                    piece,
                    spec=HELD,
                    scratch=[pltpu.SemaphoreType.DMA],
                )
                part = exchange(part, mask)
                for axis in reversed(levels):
                    other = exchange(part, 1, axis)
                    size *= 2
                    part = small_call(functools.partial(join_kernel, functools.partial(bit, axis)), size, part, other)
                pieces[offset ^ mask] = part
            else:
                pieces[offset ^ mask] = exchange(piece, mask)
    return [pieces[offset] for offset in range(len(pieces))]


def on_device(
    pixel_grid_input,
    mask_zone_labeling,
    standardize_multiplier,
    standardize_offset_vector,
    triple_projection_matrix,
    logit_scaling_per_part,
    final_projection_matrix,
):
    count = lax.axis_size("seq")
    blocked = pixel_grid_input[0, :, 0]
    row_count, col_count, width = blocked.shape
    rows = row_count // 2
    half = WS // 2
    head_width = triple_projection_matrix.shape[2]

    def west(source, count):
        return (source - 2) % count

    def west_north(source, count):
        return ((source ^ 1) - 2) % count

    near = WS - half
    gain, bias = standardize_multiplier, standardize_offset_vector
    weights = triple_projection_matrix
    scales = logit_scaling_per_part

    groups = [[(0, rows + row, left, size) for row in range(rows)] for left, size in ((half, WS), (half + WS, near))]
    local_0, local_1 = norm([blocked], gain, bias, groups)
    boxes = [(0, half, WS), (0, half + WS, near), (rows, 0, half), (0, 0, half)]
    south_0, south_1, east, corner = cut(blocked, rows, boxes)
    south_0 = exchange(south_0, 1, "win")
    south_1 = exchange(south_1, 1, "win")
    east = permute_by(east, "win", west)
    corner = permute_by(corner, "win", west_north)
    local_0_pieces = gather_pieces(local_0)
    local_1_pieces = gather_pieces(local_1)
    query_0, key_0, query_1, key_1 = region_tags(mask_zone_labeling[0], weights, count, near)
    out_weights = gather_weights(final_projection_matrix)

    spans = [(0, row, 0, WS) for row in range(rows)]
    (south_normed,) = norm([south_0], gain, bias, [spans])
    south_pieces = gather_pieces(south_normed)
    local_0_pieces[0] = after(local_0, south_normed)
    local_0, local_1 = project([local_0_pieces, local_1_pieces], weights)
    spans = [(0, row, 0, near) for row in range(rows)]
    spans += [(which, row, 0, half) for which in (1, 2) for row in range(rows)]
    (rest_normed,) = norm([after(south_1, local_0), east, corner], gain, bias, [spans])
    rest_pieces = gather_pieces(rest_normed)
    south_pieces[0] = after(south_normed, local_0)
    (south_0_projected,) = project([south_pieces], weights)

    def attend_run(blocks, tags, earlier, lo, hi):
        blocks = [after(blocks[0], *earlier), *blocks[1:]]
        return list(attend(blocks, *tags, scales, count, [(i, i + 1) for i in range(lo, hi)], head_width))

    split = count // 2
    blocks, tags = [local_0, south_0_projected], (query_0, key_0)
    outs_0 = attend_run(blocks, tags, [], 0, count)
    rest_pieces[0] = after(rest_normed, *outs_0)
    (rest_projected,) = project([rest_pieces], weights)
    blocks, tags = [local_1, rest_projected], (query_1, key_1)
    far = attend_run(blocks, tags, [], split, count)
    close = attend_run(blocks, tags, far, 0, split)
    outs_1 = close + far

    first = send_heads(outs_0)
    second = send_heads(outs_1)
    first[0] = after(first[0], *outs_1)
    spans = [(0, rows + row, half, WS, row, 0) for row in range(rows)]
    spans += [(1, row, 0, WS, rows + row, 0) for row in range(rows)]
    shape = (row_count, col_count, width)
    done = finish(first, out_weights, [blocked, south_0], spans, (row_count, WS, width))
    second[0] = after(second[0], done)
    base = partial(second[:split], out_weights[:split])
    spans = [(0, rows + row, half + WS, near, row, WS) for row in range(rows)]
    spans += [(1, row, 0, near, rows + row, WS) for row in range(rows)]
    spans += [(2, row, 0, half, row, WS + near) for row in range(rows)]
    spans += [(3, row, 0, half, rows + row, WS + near) for row in range(rows)]
    mixed = finish_last(second[split:], out_weights[split:], base, done, [blocked, south_1, east, corner], spans, shape)
    return mixed[None, :, None]


def solution(mesh):
    in_specs = (
        P(("member", "win"), None, "seq", None, None),
        P(("member", "win"), None, None),
        P(),
        P(),
        P(None, None, "seq"),
        P("seq"),
        P("seq", None),
    )
    out_specs = P(("member", "win"), None, "seq", None, None)

    return jax.shard_map(on_device, mesh=mesh, in_specs=in_specs, out_specs=out_specs, check_vma=False)
```

```python
import functools
import math

import jax
import jax.numpy as jnp
from jax import lax
from jax.experimental import pallas as pl
from jax.experimental.pallas import tpu as pltpu
from jax.sharding import PartitionSpec as P


CHANNEL_PER_PART = 96
WS = 32
REGIONS = 32
LANE = 128
FAR = -1e30
F32 = jnp.float32
BF16 = jnp.bfloat16


def permute_by(value, axis, move):
    count = lax.axis_size(axis)
    pairs = [(source, move(source, count)) for source in range(count)]
    return lax.ppermute(value, axis, pairs)


def exchange(value, mask, axis="seq"):
    return permute_by(value, axis, lambda source, count: source ^ mask)


def masks_of(count):
    masks = []
    while count > 1:
        count //= 2
        masks.append(count)
    return masks


def gather_pieces(piece):
    pieces = {0: piece}
    for mask in masks_of(lax.axis_size("seq")):
        for offset in list(pieces):
            pieces[offset ^ mask] = exchange(pieces[offset], mask)
    return [pieces[offset] for offset in range(len(pieces))]


def padded(width):
    return (width + LANE - 1) // LANE * LANE


VMEM = pl.BlockSpec(memory_space=pltpu.VMEM)


def after(value, *earlier):
    return lax.optimization_barrier((value, *earlier))[0]


def normalized(held, gain, bias):
    values = held.astype(F32)
    average = jnp.mean(values, axis=-1, keepdims=True)
    centred = values - average
    variance = jnp.mean(centred * centred, axis=-1, keepdims=True)
    return (centred * lax.rsqrt(variance + 1e-05) * gain + bias).astype(BF16)


HELD = pl.BlockSpec(memory_space=pltpu.HBM)


def cut_kernel(boxes, pixel_ref, *outs):
    for (row, left, size), out_ref in zip(boxes, outs, strict=True):
        out_ref[...] = pixel_ref[row : row + out_ref.shape[0], left : left + size, :]


def cut(pixels, rows, boxes):
    width = pixels.shape[2]
    return pl.pallas_call(
        functools.partial(cut_kernel, boxes),
        out_shape=[jax.ShapeDtypeStruct((rows, size, width), BF16) for _, _, size in boxes],
        in_specs=[VMEM],
        out_specs=[VMEM] * len(boxes),
        compiler_params=pltpu.CompilerParams(vmem_limit_bytes=8 << 20),
        cost_estimate=pl.CostEstimate(flops=0, bytes_accessed=2 * pixels.size, transcendentals=0),
        name="cut",
    )(pixels)


def norm_kernel(groups, *refs):
    refs, outs = refs[: -len(groups)], refs[-len(groups) :]
    *sources, gain_ref, bias_ref = refs
    gain, bias = gain_ref[...][None], bias_ref[...][None]
    for spans, out_ref in zip(groups, outs, strict=True):
        into = 0
        for which, row, left, size in spans:
            held = sources[which][row, left : left + size, :]
            out_ref[into : into + size, :] = normalized(held, gain, bias)
            into += size


def norm(sources, gain, bias, groups):
    width = sources[0].shape[-1]
    totals = [sum(span[-1] for span in spans) for spans in groups]
    return pl.pallas_call(
        functools.partial(norm_kernel, groups),
        out_shape=[jax.ShapeDtypeStruct((total, width), BF16) for total in totals],
        in_specs=[VMEM] * (len(sources) + 2),
        out_specs=[VMEM] * len(groups),
        compiler_params=pltpu.CompilerParams(vmem_limit_bytes=8 << 20),
        cost_estimate=pl.CostEstimate(
            flops=10 * sum(totals) * width, bytes_accessed=4 * sum(totals) * width, transcendentals=0
        ),
    )(*sources, gain, bias)


def tag_kernel(count, near, label_ref, weight_ref, *outs):
    del weight_ref
    query_0, key_0, query_1, key_1 = outs
    row_count, _ = label_ref.shape
    rows = row_count // (2 * count)
    device = lax.axis_index("seq")
    turned = jnp.transpose(label_ref[...].astype(F32)).astype(BF16)
    place = lax.broadcasted_iota(jnp.int32, (row_count, LANE), 0)
    lane = (lax.broadcasted_iota(jnp.int32, (1, LANE), 1) % REGIONS).astype(F32)
    group = count * rows
    for half in range(2):
        for offset in range(count):
            for row in range(rows):
                at = (half * rows + row) * count + jnp.bitwise_xor(device, offset)
                chosen = jnp.where(place == at, 1.0, 0.0).astype(BF16)
                region = jnp.dot(turned, chosen, preferred_element_type=F32)
                same = region == lane
                query = jnp.where(same, 1.0, 0.0).astype(BF16)
                key = jnp.where(same, 0.0, FAR).astype(BF16)
                slot = offset * rows + row
                apart, span = group * near, near + 2 * (WS - near)
                beside = apart + offset * rows * span
                spots = [
                    (query_0, key_0, (half * group + slot) * WS, 0, WS),
                    (query_1, key_1, beside + row * near if half else slot * near, WS, near),
                    (
                        query_1,
                        key_1,
                        beside + rows * near + (half * rows + row) * (WS - near),
                        WS + near,
                        WS - near,
                    ),
                ]
                for query_ref, key_ref, into, left, size in spots:
                    query_ref[into : into + size, :] = query[left : left + size]
                    key_ref[into : into + size, :] = key[left : left + size]


def region_tags(labels, weights, count, near):
    pixels = labels.shape[0] * WS
    return pl.pallas_call(
        functools.partial(tag_kernel, count, near),
        out_shape=[jax.ShapeDtypeStruct((pixels, LANE), BF16)] * 4,
        in_specs=[VMEM] * 2,
        out_specs=[VMEM] * 4,
        compiler_params=pltpu.CompilerParams(vmem_limit_bytes=8 << 20),
        cost_estimate=pl.CostEstimate(
            flops=8 * pixels * LANE * labels.shape[0], bytes_accessed=8 * pixels * LANE, transcendentals=0
        ),
        name="tags",
    )(labels, weights)


def project_kernel(counts, *refs):
    groups = []
    for count in counts:
        groups.append(refs[:count])
        refs = refs[count:]
    weight_ref, *outs = refs
    block = jnp.concatenate([piece[...] for group in groups for piece in group], axis=0)
    head_width = weight_ref.shape[2]
    slot = padded(head_width)
    if slot == head_width:
        weights = jnp.concatenate([weight_ref[t] for t in range(3)], axis=1)
        products = [(0, jnp.dot(block, weights, preferred_element_type=F32).astype(BF16))]
    else:
        products = [
            (t * slot, jnp.dot(block, weight_ref[t], preferred_element_type=F32).astype(BF16))
            for t in range(3)
        ]
    at = 0
    for out_ref in outs:
        for left, product in products:
            part = product[at : at + out_ref.shape[0]]
            out_ref[:, left : left + part.shape[1]] = part
        at += out_ref.shape[0]


def project(groups, weights):
    width = groups[0][0].shape[1]
    slot = padded(weights.shape[2])
    sizes = [sum(piece.shape[0] for piece in group) for group in groups]
    total = sum(sizes)
    return pl.pallas_call(
        functools.partial(project_kernel, [len(group) for group in groups]),
        out_shape=[jax.ShapeDtypeStruct((size, 3 * slot), BF16) for size in sizes],
        in_specs=[VMEM] * (sum(len(group) for group in groups) + 1),
        out_specs=[VMEM] * len(groups),
        compiler_params=pltpu.CompilerParams(vmem_limit_bytes=24 << 20),
        cost_estimate=pl.CostEstimate(
            flops=2 * total * width * 3 * slot,
            bytes_accessed=2 * (total * width + weights.size + total * 3 * slot),
            transcendentals=0,
        ),
    )(*[piece for group in groups for piece in group], weights)


def attend_kernel(count, parts, ranges, head_width, *refs):
    blocks = refs[:parts]
    query_tags, key_tags, scale_ref = refs[parts : parts + 3]
    outs = refs[parts + 3 :]
    slot = padded(head_width)
    sizes = [block.shape[0] // count for block in blocks]
    low, high = min(lo for lo, _ in ranges), max(hi for _, hi in ranges)
    heads = head_width // CHANNEL_PER_PART
    base = math.log2(math.e) / math.sqrt(CHANNEL_PER_PART)
    tiles = [None] * (slot // LANE)
    key_rows = key_tags[...]
    query_rows, at = [], 0
    for z in sizes:
        query_rows.append(query_tags[at + low * z : at + high * z, :])
        at += count * z
    query_rows = jnp.concatenate(query_rows, axis=0)

    def span(head):
        first = head * CHANNEL_PER_PART
        last = first + CHANNEL_PER_PART
        left, right = first // LANE * LANE, padded(last)
        lane = lax.broadcasted_iota(jnp.int32, (1, right - left), 1)
        return left, right, (lane >= first - left) & (lane < last - left)

    def scores_of(head):
        left, right, inside = span(head)
        reps = (right - left) // LANE
        queries = jnp.concatenate(
            [b[low * z : high * z, left:right] for b, z in zip(blocks, sizes, strict=True)], axis=0
        )
        queries = jnp.where(inside, queries, jnp.concatenate([query_rows] * reps, axis=1))
        keys = jnp.concatenate([b[:, slot + left : slot + right] for b in blocks], axis=0)
        keys = jnp.where(inside, keys, jnp.concatenate([key_rows] * reps, axis=1))
        return lax.dot_general(queries, keys, (((1,), (1,)), ((), ())), preferred_element_type=F32)

    following = scores_of(0)
    for head in range(heads):
        scores = following
        if head + 1 < heads:
            following = scores_of(head + 1)
        left, right, inside = span(head)
        row_max = jnp.max(scores, axis=-1, keepdims=True)
        numerators = jnp.exp2((scores - row_max) * (scale_ref[head] * base))
        total = jnp.sum(numerators, axis=-1, keepdims=True)
        values = jnp.concatenate([b[:, 2 * slot + left : 2 * slot + right] for b in blocks], axis=0)
        mixed = jnp.dot(numerators.astype(BF16), values, preferred_element_type=F32) / total
        for i in range((right - left) // LANE):
            tile = left // LANE + i
            own = mixed[:, i * LANE : (i + 1) * LANE]
            held = tiles[tile]
            tiles[tile] = own if held is None else jnp.where(inside[:, i * LANE : (i + 1) * LANE], own, held)
    result = jnp.concatenate(tiles, axis=1)[:, :head_width].astype(BF16)
    for out_ref, (lo, hi) in zip(outs, ranges, strict=True):
        for offset in range(lo, hi):
            start, into = 0, 0
            for z in sizes:
                at = start + (offset - low) * z
                out_ref[offset - lo, into : into + z, :] = result[at : at + z]
                start += (high - low) * z
                into += z


def attend(blocks, query_tags, key_tags, scales, count, ranges, head_width):
    parts = len(blocks)
    per_offset = sum(b.shape[0] for b in blocks) // count
    pixels = count * per_offset
    asked = sum(hi - lo for lo, hi in ranges) * per_offset
    vmem = pl.BlockSpec(memory_space=pltpu.VMEM)
    heads = head_width // CHANNEL_PER_PART
    return pl.pallas_call(
        functools.partial(attend_kernel, count, parts, ranges, head_width),
        out_shape=[
            jax.ShapeDtypeStruct((hi - lo, per_offset, head_width), BF16) for lo, hi in ranges
        ],
        in_specs=[vmem] * (parts + 2) + [pl.BlockSpec(memory_space=pltpu.SMEM)],
        out_specs=[vmem] * len(ranges),
        compiler_params=pltpu.CompilerParams(vmem_limit_bytes=28 << 20),
        cost_estimate=pl.CostEstimate(
            flops=4 * heads * asked * pixels * 2 * LANE,
            bytes_accessed=2 * pixels * 3 * padded(head_width),
            transcendentals=heads * asked * pixels,
        ),
    )(*blocks, query_tags, key_tags, scales)


def product(attended, weights, columns=slice(None)):
    total = None
    for piece, weight in zip(attended, weights, strict=True):
        term = jnp.dot(piece[...], weight[:, columns], preferred_element_type=F32)
        total = term if total is None else total + term
    return total


def partial_kernel(count, *refs):
    *refs, out_ref = refs
    out_ref[...] = product(refs[:count], refs[count:])


def partial(attended, weights):
    pixels, depth = attended[0].shape
    width = weights[0].shape[1]
    return pl.pallas_call(
        functools.partial(partial_kernel, len(weights)),
        out_shape=jax.ShapeDtypeStruct((pixels, width), F32),
        in_specs=[VMEM] * (2 * len(weights)),
        out_specs=VMEM,
        compiler_params=pltpu.CompilerParams(vmem_limit_bytes=20 << 20),
        cost_estimate=pl.CostEstimate(
            flops=2 * pixels * width * depth * len(weights), bytes_accessed=2 * width * (depth + 2 * pixels), transcendentals=0
        ),
    )(*attended, *weights)


def finish_kernel(count, spans, *refs):
    attended, weights, sources, out_ref = refs[:count], refs[count : 2 * count], refs[2 * count : -1], refs[-1]
    total = product(attended, weights)
    at = 0
    for which, row, start, pixels, into, column in spans:
        held = sources[which][row, start : start + pixels, :].astype(F32)
        out_ref[into, column : column + pixels, :] = (held + total[at : at + pixels]).astype(BF16)
        at += pixels


def finish(attended, weights, sources, spans, shape):
    count = len(weights)
    pixels, width = attended[0].shape[0], shape[-1]
    return pl.pallas_call(
        functools.partial(finish_kernel, count, spans),
        out_shape=jax.ShapeDtypeStruct(shape, BF16),
        in_specs=[VMEM] * (2 * count + len(sources)),
        out_specs=VMEM,
        compiler_params=pltpu.CompilerParams(vmem_limit_bytes=20 << 20),
        cost_estimate=pl.CostEstimate(
            flops=2 * pixels * width * width, bytes_accessed=2 * width * (width + 3 * pixels), transcendentals=0
        ),
    )(*attended, *weights, *sources)


def last_kernel(count, chunks, spans, *refs):
    attended, weights = refs[:count], refs[count : 2 * count]
    base_ref, done_ref, *sources, out_ref, ready, semaphore = refs[2 * count :]
    left, size, width = done_ref.shape[1], ready.shape[1], ready.shape[2]
    wide = width // chunks
    copies = [
        pltpu.make_async_copy(done_ref, out_ref.at[:, pl.ds(0, left), :], semaphore.at[chunks])
    ]
    copies[0].start()
    for chunk in range(chunks):
        columns = slice(chunk * wide, (chunk + 1) * wide)
        total = product(attended, weights, columns) + base_ref[:, columns]
        at = 0
        for which, row, start, pixels, into, column in spans:
            held = sources[which][row, start : start + pixels, columns].astype(F32)
            ready[into, column - left : column - left + pixels, columns] = (
                held + total[at : at + pixels]
            ).astype(BF16)
            at += pixels
        place = pl.ds(chunk * wide, wide)
        copy = pltpu.make_async_copy(
            ready.at[:, :, place], out_ref.at[:, pl.ds(left, size), place], semaphore.at[chunk]
        )
        copy.start()
        copies.append(copy)
    for copy in copies:
        copy.wait()


def finish_last(attended, weights, base, done, sources, spans, shape):
    count = len(weights)
    row_count, col_count, width = shape
    pixels, depth = attended[0].shape
    chunks = 3 if width % (3 * 2 * LANE) == 0 else 1
    return pl.pallas_call(
        functools.partial(last_kernel, count, chunks, spans),
        out_shape=jax.ShapeDtypeStruct(shape, BF16),
        in_specs=[VMEM] * (2 * count + 2 + len(sources)),
        out_specs=HELD,
        scratch_shapes=[
            pltpu.VMEM((row_count, col_count - done.shape[1], width), BF16),
            pltpu.SemaphoreType.DMA((chunks + 1,)),
        ],
        compiler_params=pltpu.CompilerParams(vmem_limit_bytes=20 << 20),
        cost_estimate=pl.CostEstimate(
            flops=2 * pixels * width * depth * count, bytes_accessed=2 * width * (width + 3 * pixels), transcendentals=0
        ),
    )(*attended, *weights, base, done, *sources)


def send_heads(outs):
    own = [outs[0]]
    for offset in range(1, len(outs)):
        own.append(exchange(outs[offset], offset))
    return [piece[0] for piece in own]


def pick_kernel(place, source_ref, out_ref, semaphore):
    size = out_ref.shape[0]
    start = pl.multiple_of(place() * size, 16)
    copy = pltpu.make_async_copy(source_ref.at[pl.ds(start, size), :], out_ref, semaphore)
    copy.start()
    copy.wait()


def join_kernel(place, own_ref, other_ref, out_ref):
    size = own_ref.shape[0]
    at = place()
    out_ref[pl.ds(pl.multiple_of(at * size, 16), size), :] = own_ref[...]
    out_ref[pl.ds(pl.multiple_of((1 - at) * size, 16), size), :] = other_ref[...]


def small_call(kernel, rows, *operands, spec=VMEM, scratch=()):
    width = operands[0].shape[1]
    return pl.pallas_call(
        kernel,
        out_shape=jax.ShapeDtypeStruct((rows, width), BF16),
        in_specs=[spec] * len(operands),
        out_specs=VMEM,
        scratch_shapes=scratch,
        compiler_params=pltpu.CompilerParams(vmem_limit_bytes=8 << 20),
        cost_estimate=pl.CostEstimate(flops=0, bytes_accessed=4 * rows * width, transcendentals=0),
    )(*operands)


def gather_weights(block):
    levels = []
    rows = block.shape[0]
    for axis in ("member", "win"):
        if lax.axis_size(axis) % 2 == 0 and rows % (32 << len(levels)) == 0:
            levels.append(axis)

    def bit(axis):
        return lax.axis_index(axis) & 1

    def part_index():
        index = 0
        for axis in levels:
            index = index * 2 + bit(axis)
        return index

    pieces = {0: block}
    for mask in masks_of(lax.axis_size("seq")):
        for offset in list(pieces):
            piece = pieces[offset]
            if mask > 1 and levels:
                size = rows >> len(levels)
                part = small_call(
                    functools.partial(pick_kernel, part_index),
                    size,
                    piece,
                    spec=HELD,
                    scratch=[pltpu.SemaphoreType.DMA],
                )
                part = exchange(part, mask)
                for axis in reversed(levels):
                    other = exchange(part, 1, axis)
                    size *= 2
                    part = small_call(functools.partial(join_kernel, functools.partial(bit, axis)), size, part, other)
                pieces[offset ^ mask] = part
            else:
                pieces[offset ^ mask] = exchange(piece, mask)
    return [pieces[offset] for offset in range(len(pieces))]


def on_device(
    pixel_grid_input,
    mask_zone_labeling,
    standardize_multiplier,
    standardize_offset_vector,
    triple_projection_matrix,
    logit_scaling_per_part,
    final_projection_matrix,
):
    count = lax.axis_size("seq")
    blocked = pixel_grid_input[0, :, 0]
    row_count, col_count, width = blocked.shape
    rows = row_count // 2
    half = WS // 2
    head_width = triple_projection_matrix.shape[2]

    def west(source, count):
        return (source - 2) % count

    def west_north(source, count):
        return ((source ^ 1) - 2) % count

    near = WS - half
    gain, bias = standardize_multiplier, standardize_offset_vector
    weights = triple_projection_matrix
    scales = logit_scaling_per_part

    boxes = [(rows, half, WS), (0, half, WS), (0, half + WS, near), (rows, 0, half), (0, 0, half)]
    local_0, south_0, south_1, east, corner = cut(blocked, rows, boxes)
    spans = [(0, rows + row, half + WS, near) for row in range(rows)]
    (local_1,) = norm([blocked], gain, bias, [spans])
    south_0 = exchange(south_0, 1, "win")
    south_1 = exchange(south_1, 1, "win")
    east = permute_by(east, "win", west)
    corner = permute_by(corner, "win", west_north)
    local_0_pieces = gather_pieces(local_0)
    local_1_pieces = gather_pieces(local_1)
    query_0, key_0, query_1, key_1 = region_tags(mask_zone_labeling[0], weights, count, near)
    out_weights = gather_weights(final_projection_matrix)

    spans = [(0, row, 0, WS) for row in range(rows)]
    (south_normed,) = norm([south_0], gain, bias, [spans])
    south_pieces = gather_pieces(south_normed)
    spans = [(piece, row, 0, WS) for piece in range(count) for row in range(rows)]
    (local_0_normed,) = norm(local_0_pieces, gain, bias, [spans])
    local_1_pieces[0] = after(local_1, south_normed)
    local_0, local_1 = project([[local_0_normed], local_1_pieces], weights)
    spans = [(0, row, 0, near) for row in range(rows)]
    spans += [(which, row, 0, half) for which in (1, 2) for row in range(rows)]
    (rest_normed,) = norm([after(south_1, local_0), east, corner], gain, bias, [spans])
    rest_pieces = gather_pieces(rest_normed)
    south_pieces[0] = after(south_normed, local_0)
    (south_0_projected,) = project([south_pieces], weights)

    def attend_run(blocks, tags, earlier, lo, hi):
        blocks = [after(blocks[0], *earlier), *blocks[1:]]
        return list(attend(blocks, *tags, scales, count, [(i, i + 1) for i in range(lo, hi)], head_width))

    split = count // 2
    blocks, tags = [local_0, south_0_projected], (query_0, key_0)
    outs_0 = attend_run(blocks, tags, [], 0, count)
    rest_pieces[0] = after(rest_normed, *outs_0)
    (rest_projected,) = project([rest_pieces], weights)
    blocks, tags = [local_1, rest_projected], (query_1, key_1)
    far = attend_run(blocks, tags, [], split, count)
    close = attend_run(blocks, tags, far, 0, split)
    outs_1 = close + far

    first = send_heads(outs_0)
    second = send_heads(outs_1)
    first[0] = after(first[0], *outs_1)
    spans = [(0, rows + row, half, WS, row, 0) for row in range(rows)]
    spans += [(1, row, 0, WS, rows + row, 0) for row in range(rows)]
    shape = (row_count, col_count, width)
    done = finish(first, out_weights, [blocked, south_0], spans, (row_count, WS, width))
    second[0] = after(second[0], done)
    base = partial(second[:split], out_weights[:split])
    spans = [(0, rows + row, half + WS, near, row, WS) for row in range(rows)]
    spans += [(1, row, 0, near, rows + row, WS) for row in range(rows)]
    spans += [(2, row, 0, half, row, WS + near) for row in range(rows)]
    spans += [(3, row, 0, half, rows + row, WS + near) for row in range(rows)]
    mixed = finish_last(second[split:], out_weights[split:], base, done, [blocked, south_1, east, corner], spans, shape)
    return mixed[None, :, None]


def solution(mesh):
    in_specs = (
        P(("member", "win"), None, "seq", None, None),
        P(("member", "win"), None, None),
        P(),
        P(),
        P(None, None, "seq"),
        P("seq"),
        P("seq", None),
    )
    out_specs = P(("member", "win"), None, "seq", None, None)

    return jax.shard_map(on_device, mesh=mesh, in_specs=in_specs, out_specs=out_specs, check_vma=False)
```

```python
import functools
import math

import jax
import jax.numpy as jnp
from jax import lax
from jax.experimental import pallas as pl
from jax.experimental.pallas import tpu as pltpu
from jax.sharding import PartitionSpec as P


CHANNEL_PER_PART = 96
WS = 32
REGIONS = 32
LANE = 128
FAR = -1e30
F32 = jnp.float32
BF16 = jnp.bfloat16


def permute_by(value, axis, move):
    count = lax.axis_size(axis)
    pairs = [(source, move(source, count)) for source in range(count)]
    return lax.ppermute(value, axis, pairs)


def exchange(value, mask, axis="seq"):
    return permute_by(value, axis, lambda source, count: source ^ mask)


def masks_of(count):
    masks = []
    while count > 1:
        count //= 2
        masks.append(count)
    return masks


def gather_pieces(piece):
    pieces = {0: piece}
    for mask in masks_of(lax.axis_size("seq")):
        for offset in list(pieces):
            pieces[offset ^ mask] = exchange(pieces[offset], mask)
    return [pieces[offset] for offset in range(len(pieces))]


def padded(width):
    return (width + LANE - 1) // LANE * LANE


VMEM = pl.BlockSpec(memory_space=pltpu.VMEM)


def after(value, *earlier):
    return lax.optimization_barrier((value, *earlier))[0]


def normalized(held, gain, bias):
    values = held.astype(F32)
    average = jnp.mean(values, axis=-1, keepdims=True)
    centred = values - average
    variance = jnp.mean(centred * centred, axis=-1, keepdims=True)
    return (centred * lax.rsqrt(variance + 1e-05) * gain + bias).astype(BF16)


HELD = pl.BlockSpec(memory_space=pltpu.HBM)


def cut_kernel(boxes, pixel_ref, *outs):
    for (row, left, size), out_ref in zip(boxes, outs, strict=True):
        out_ref[...] = pixel_ref[row : row + out_ref.shape[0], left : left + size, :]


def cut(pixels, rows, boxes):
    width = pixels.shape[2]
    return pl.pallas_call(
        functools.partial(cut_kernel, boxes),
        out_shape=[jax.ShapeDtypeStruct((rows, size, width), BF16) for _, _, size in boxes],
        in_specs=[VMEM],
        out_specs=[VMEM] * len(boxes),
        compiler_params=pltpu.CompilerParams(vmem_limit_bytes=8 << 20),
        cost_estimate=pl.CostEstimate(flops=0, bytes_accessed=2 * pixels.size, transcendentals=0),
        name="cut",
    )(pixels)


def norm_kernel(groups, *refs):
    refs, outs = refs[: -len(groups)], refs[-len(groups) :]
    *sources, gain_ref, bias_ref = refs
    gain, bias = gain_ref[...][None], bias_ref[...][None]
    for spans, out_ref in zip(groups, outs, strict=True):
        into = 0
        for which, row, left, size in spans:
            held = sources[which][row, left : left + size, :]
            out_ref[into : into + size, :] = normalized(held, gain, bias)
            into += size


def norm(sources, gain, bias, groups):
    width = sources[0].shape[-1]
    totals = [sum(span[-1] for span in spans) for spans in groups]
    return pl.pallas_call(
        functools.partial(norm_kernel, groups),
        out_shape=[jax.ShapeDtypeStruct((total, width), BF16) for total in totals],
        in_specs=[VMEM] * (len(sources) + 2),
        out_specs=[VMEM] * len(groups),
        compiler_params=pltpu.CompilerParams(vmem_limit_bytes=8 << 20),
        cost_estimate=pl.CostEstimate(
            flops=10 * sum(totals) * width, bytes_accessed=4 * sum(totals) * width, transcendentals=0
        ),
    )(*sources, gain, bias)


def tag_kernel(count, near, label_ref, weight_ref, *outs):
    del weight_ref
    query_0, key_0, query_1, key_1 = outs
    row_count, _ = label_ref.shape
    rows = row_count // (2 * count)
    device = lax.axis_index("seq")
    turned = jnp.transpose(label_ref[...].astype(F32)).astype(BF16)
    place = lax.broadcasted_iota(jnp.int32, (row_count, LANE), 0)
    lane = (lax.broadcasted_iota(jnp.int32, (1, LANE), 1) % REGIONS).astype(F32)
    group = count * rows
    for half in range(2):
        for offset in range(count):
            for row in range(rows):
                at = (half * rows + row) * count + jnp.bitwise_xor(device, offset)
                chosen = jnp.where(place == at, 1.0, 0.0).astype(BF16)
                region = jnp.dot(turned, chosen, preferred_element_type=F32)
                same = region == lane
                query = jnp.where(same, 1.0, 0.0).astype(BF16)
                key = jnp.where(same, 0.0, FAR).astype(BF16)
                slot = offset * rows + row
                apart, span = group * near, near + 2 * (WS - near)
                beside = apart + offset * rows * span
                spots = [
                    (query_0, key_0, (half * group + slot) * WS, 0, WS),
                    (query_1, key_1, beside + row * near if half else slot * near, WS, near),
                    (
                        query_1,
                        key_1,
                        beside + rows * near + (half * rows + row) * (WS - near),
                        WS + near,
                        WS - near,
                    ),
                ]
                for query_ref, key_ref, into, left, size in spots:
                    query_ref[into : into + size, :] = query[left : left + size]
                    key_ref[into : into + size, :] = key[left : left + size]


def region_tags(labels, weights, count, near):
    pixels = labels.shape[0] * WS
    return pl.pallas_call(
        functools.partial(tag_kernel, count, near),
        out_shape=[jax.ShapeDtypeStruct((pixels, LANE), BF16)] * 4,
        in_specs=[VMEM] * 2,
        out_specs=[VMEM] * 4,
        compiler_params=pltpu.CompilerParams(vmem_limit_bytes=8 << 20),
        cost_estimate=pl.CostEstimate(
            flops=8 * pixels * LANE * labels.shape[0], bytes_accessed=8 * pixels * LANE, transcendentals=0
        ),
        name="tags",
    )(labels, weights)


def project_kernel(counts, *refs):
    groups = []
    for count in counts:
        groups.append(refs[:count])
        refs = refs[count:]
    weight_ref, *outs = refs
    block = jnp.concatenate([piece[...] for group in groups for piece in group], axis=0)
    head_width = weight_ref.shape[2]
    slot = padded(head_width)
    if slot == head_width:
        weights = jnp.concatenate([weight_ref[t] for t in range(3)], axis=1)
        products = [(0, jnp.dot(block, weights, preferred_element_type=F32).astype(BF16))]
    else:
        products = [
            (t * slot, jnp.dot(block, weight_ref[t], preferred_element_type=F32).astype(BF16))
            for t in range(3)
        ]
    at = 0
    for out_ref in outs:
        for left, product in products:
            part = product[at : at + out_ref.shape[0]]
            out_ref[:, left : left + part.shape[1]] = part
        at += out_ref.shape[0]


def project(groups, weights):
    width = groups[0][0].shape[1]
    slot = padded(weights.shape[2])
    sizes = [sum(piece.shape[0] for piece in group) for group in groups]
    total = sum(sizes)
    return pl.pallas_call(
        functools.partial(project_kernel, [len(group) for group in groups]),
        out_shape=[jax.ShapeDtypeStruct((size, 3 * slot), BF16) for size in sizes],
        in_specs=[VMEM] * (sum(len(group) for group in groups) + 1),
        out_specs=[VMEM] * len(groups),
        compiler_params=pltpu.CompilerParams(vmem_limit_bytes=24 << 20),
        cost_estimate=pl.CostEstimate(
            flops=2 * total * width * 3 * slot,
            bytes_accessed=2 * (total * width + weights.size + total * 3 * slot),
            transcendentals=0,
        ),
    )(*[piece for group in groups for piece in group], weights)


def attend_kernel(layout, ranges, head_width, *refs):
    parts = len(layout)
    blocks = refs[:parts]
    query_tags, key_tags, scale_ref = refs[parts : parts + 3]
    outs = refs[parts + 3 :]
    slot = padded(head_width)
    low, high = min(lo for lo, _ in ranges), max(hi for _, hi in ranges)
    heads = head_width // CHANNEL_PER_PART
    base = math.log2(math.e) / math.sqrt(CHANNEL_PER_PART)
    tiles = [None] * (slot // LANE)
    key_rows = key_tags[...]
    runs, query_rows, at = [], [], 0
    for block, (lo, hi) in zip(blocks, layout, strict=True):
        z = block.shape[0] // (hi - lo)
        first, last = max(low, lo), min(high, hi)
        if first < last:
            runs.append((block, (first - lo) * z, (last - lo) * z, z, first, last))
            query_rows.append(query_tags[at + (first - lo) * z : at + (last - lo) * z, :])
        at += block.shape[0]
    query_rows = jnp.concatenate(query_rows, axis=0)

    def span(head):
        first = head * CHANNEL_PER_PART
        last = first + CHANNEL_PER_PART
        left, right = first // LANE * LANE, padded(last)
        lane = lax.broadcasted_iota(jnp.int32, (1, right - left), 1)
        return left, right, (lane >= first - left) & (lane < last - left)

    def scores_of(head):
        left, right, inside = span(head)
        reps = (right - left) // LANE
        queries = jnp.concatenate([run[0][run[1] : run[2], left:right] for run in runs], axis=0)
        queries = jnp.where(inside, queries, jnp.concatenate([query_rows] * reps, axis=1))
        keys = jnp.concatenate([b[:, slot + left : slot + right] for b in blocks], axis=0)
        keys = jnp.where(inside, keys, jnp.concatenate([key_rows] * reps, axis=1))
        return lax.dot_general(queries, keys, (((1,), (1,)), ((), ())), preferred_element_type=F32)

    following = scores_of(0)
    for head in range(heads):
        scores = following
        if head + 1 < heads:
            following = scores_of(head + 1)
        left, right, inside = span(head)
        row_max = jnp.max(scores, axis=-1, keepdims=True)
        numerators = jnp.exp2((scores - row_max) * (scale_ref[head] * base))
        total = jnp.sum(numerators, axis=-1, keepdims=True)
        values = jnp.concatenate([b[:, 2 * slot + left : 2 * slot + right] for b in blocks], axis=0)
        mixed = jnp.dot(numerators.astype(BF16), values, preferred_element_type=F32) / total
        for i in range((right - left) // LANE):
            tile = left // LANE + i
            own = mixed[:, i * LANE : (i + 1) * LANE]
            held = tiles[tile]
            tiles[tile] = own if held is None else jnp.where(inside[:, i * LANE : (i + 1) * LANE], own, held)
    result = jnp.concatenate(tiles, axis=1)[:, :head_width].astype(BF16)
    places = {
        offset: (out_ref, offset - lo)
        for out_ref, (lo, hi) in zip(outs, ranges, strict=True)
        for offset in range(lo, hi)
    }
    into = dict.fromkeys(places, 0)
    at = 0
    for _, _, _, z, first, last in runs:
        for offset in range(first, last):
            out_ref, index = places[offset]
            out_ref[index, into[offset] : into[offset] + z, :] = result[at : at + z]
            into[offset] += z
            at += z


def attend(blocks, layout, query_tags, key_tags, scales, count, ranges, head_width):
    pixels = sum(block.shape[0] for block in blocks)
    per_offset = pixels // count
    asked = sum(hi - lo for lo, hi in ranges) * per_offset
    heads = head_width // CHANNEL_PER_PART
    return pl.pallas_call(
        functools.partial(attend_kernel, layout, ranges, head_width),
        out_shape=[
            jax.ShapeDtypeStruct((hi - lo, per_offset, head_width), BF16) for lo, hi in ranges
        ],
        in_specs=[VMEM] * (len(blocks) + 2) + [pl.BlockSpec(memory_space=pltpu.SMEM)],
        out_specs=[VMEM] * len(ranges),
        compiler_params=pltpu.CompilerParams(vmem_limit_bytes=28 << 20),
        cost_estimate=pl.CostEstimate(
            flops=4 * heads * asked * pixels * 2 * LANE,
            bytes_accessed=2 * pixels * 3 * padded(head_width),
            transcendentals=heads * asked * pixels,
        ),
    )(*blocks, query_tags, key_tags, scales)


def product(attended, weights, columns=slice(None)):
    total = None
    for piece, weight in zip(attended, weights, strict=True):
        term = jnp.dot(piece[...], weight[:, columns], preferred_element_type=F32)
        total = term if total is None else total + term
    return total


def partial_kernel(count, *refs):
    *refs, out_ref = refs
    out_ref[...] = product(refs[:count], refs[count:])


def partial(attended, weights):
    pixels, depth = attended[0].shape
    width = weights[0].shape[1]
    return pl.pallas_call(
        functools.partial(partial_kernel, len(weights)),
        out_shape=jax.ShapeDtypeStruct((pixels, width), F32),
        in_specs=[VMEM] * (2 * len(weights)),
        out_specs=VMEM,
        compiler_params=pltpu.CompilerParams(vmem_limit_bytes=20 << 20),
        cost_estimate=pl.CostEstimate(
            flops=2 * pixels * width * depth * len(weights), bytes_accessed=2 * width * (depth + 2 * pixels), transcendentals=0
        ),
    )(*attended, *weights)


def finish_kernel(count, spans, *refs):
    attended, weights, sources, out_ref = refs[:count], refs[count : 2 * count], refs[2 * count : -1], refs[-1]
    total = product(attended, weights)
    at = 0
    for which, row, start, pixels, into, column in spans:
        held = sources[which][row, start : start + pixels, :].astype(F32)
        out_ref[into, column : column + pixels, :] = (held + total[at : at + pixels]).astype(BF16)
        at += pixels


def finish(attended, weights, sources, spans, shape):
    count = len(weights)
    pixels, width = attended[0].shape[0], shape[-1]
    return pl.pallas_call(
        functools.partial(finish_kernel, count, spans),
        out_shape=jax.ShapeDtypeStruct(shape, BF16),
        in_specs=[VMEM] * (2 * count + len(sources)),
        out_specs=VMEM,
        compiler_params=pltpu.CompilerParams(vmem_limit_bytes=20 << 20),
        cost_estimate=pl.CostEstimate(
            flops=2 * pixels * width * width, bytes_accessed=2 * width * (width + 3 * pixels), transcendentals=0
        ),
    )(*attended, *weights, *sources)


def last_kernel(count, chunks, spans, *refs):
    attended, weights = refs[:count], refs[count : 2 * count]
    base_ref, done_ref, *sources, out_ref, ready, semaphore = refs[2 * count :]
    left, size, width = done_ref.shape[1], ready.shape[1], ready.shape[2]
    wide = width // chunks
    copies = [
        pltpu.make_async_copy(done_ref, out_ref.at[:, pl.ds(0, left), :], semaphore.at[chunks])
    ]
    copies[0].start()
    for chunk in range(chunks):
        columns = slice(chunk * wide, (chunk + 1) * wide)
        total = product(attended, weights, columns) + base_ref[:, columns]
        at = 0
        for which, row, start, pixels, into, column in spans:
            held = sources[which][row, start : start + pixels, columns].astype(F32)
            ready[into, column - left : column - left + pixels, columns] = (
                held + total[at : at + pixels]
            ).astype(BF16)
            at += pixels
        place = pl.ds(chunk * wide, wide)
        copy = pltpu.make_async_copy(
            ready.at[:, :, place], out_ref.at[:, pl.ds(left, size), place], semaphore.at[chunk]
        )
        copy.start()
        copies.append(copy)
    for copy in copies:
        copy.wait()


def finish_last(attended, weights, base, done, sources, spans, shape):
    count = len(weights)
    row_count, col_count, width = shape
    pixels, depth = attended[0].shape
    chunks = 3 if width % (3 * 2 * LANE) == 0 else 1
    return pl.pallas_call(
        functools.partial(last_kernel, count, chunks, spans),
        out_shape=jax.ShapeDtypeStruct(shape, BF16),
        in_specs=[VMEM] * (2 * count + 2 + len(sources)),
        out_specs=HELD,
        scratch_shapes=[
            pltpu.VMEM((row_count, col_count - done.shape[1], width), BF16),
            pltpu.SemaphoreType.DMA((chunks + 1,)),
        ],
        compiler_params=pltpu.CompilerParams(vmem_limit_bytes=20 << 20),
        cost_estimate=pl.CostEstimate(
            flops=2 * pixels * width * depth * count, bytes_accessed=2 * width * (width + 3 * pixels), transcendentals=0
        ),
    )(*attended, *weights, base, done, *sources)


def send_heads(outs):
    own = [outs[0]]
    for offset in range(1, len(outs)):
        own.append(exchange(outs[offset], offset))
    return [piece[0] for piece in own]


def pick_kernel(place, source_ref, out_ref, semaphore):
    size = out_ref.shape[0]
    start = pl.multiple_of(place() * size, 16)
    copy = pltpu.make_async_copy(source_ref.at[pl.ds(start, size), :], out_ref, semaphore)
    copy.start()
    copy.wait()


def join_kernel(place, own_ref, other_ref, out_ref):
    size = own_ref.shape[0]
    at = place()
    out_ref[pl.ds(pl.multiple_of(at * size, 16), size), :] = own_ref[...]
    out_ref[pl.ds(pl.multiple_of((1 - at) * size, 16), size), :] = other_ref[...]


def small_call(kernel, rows, *operands, spec=VMEM, scratch=()):
    width = operands[0].shape[1]
    return pl.pallas_call(
        kernel,
        out_shape=jax.ShapeDtypeStruct((rows, width), BF16),
        in_specs=[spec] * len(operands),
        out_specs=VMEM,
        scratch_shapes=scratch,
        compiler_params=pltpu.CompilerParams(vmem_limit_bytes=8 << 20),
        cost_estimate=pl.CostEstimate(flops=0, bytes_accessed=4 * rows * width, transcendentals=0),
    )(*operands)


def gather_weights(block):
    levels = []
    rows = block.shape[0]
    for axis in ("member", "win"):
        if lax.axis_size(axis) % 2 == 0 and rows % (32 << len(levels)) == 0:
            levels.append(axis)

    def bit(axis):
        return lax.axis_index(axis) & 1

    def part_index():
        index = 0
        for axis in levels:
            index = index * 2 + bit(axis)
        return index

    pieces = {0: block}
    for mask in masks_of(lax.axis_size("seq")):
        for offset in list(pieces):
            piece = pieces[offset]
            if mask > 1 and levels:
                size = rows >> len(levels)
                part = small_call(
                    functools.partial(pick_kernel, part_index),
                    size,
                    piece,
                    spec=HELD,
                    scratch=[pltpu.SemaphoreType.DMA],
                )
                part = exchange(part, mask)
                for axis in reversed(levels):
                    other = exchange(part, 1, axis)
                    size *= 2
                    part = small_call(functools.partial(join_kernel, functools.partial(bit, axis)), size, part, other)
                pieces[offset ^ mask] = part
            else:
                pieces[offset ^ mask] = exchange(piece, mask)
    return [pieces[offset] for offset in range(len(pieces))]


def on_device(
    pixel_grid_input,
    mask_zone_labeling,
    standardize_multiplier,
    standardize_offset_vector,
    triple_projection_matrix,
    logit_scaling_per_part,
    final_projection_matrix,
):
    count = lax.axis_size("seq")
    blocked = pixel_grid_input[0, :, 0]
    row_count, col_count, width = blocked.shape
    rows = row_count // 2
    half = WS // 2
    head_width = triple_projection_matrix.shape[2]

    def west(source, count):
        return (source - 2) % count

    def west_north(source, count):
        return ((source ^ 1) - 2) % count

    near = WS - half
    gain, bias = standardize_multiplier, standardize_offset_vector
    weights = triple_projection_matrix
    scales = logit_scaling_per_part

    local_0 = blocked[rows:, half : half + WS]
    boxes = [(0, half, WS), (0, half + WS, near), (rows, 0, half), (0, 0, half)]
    south_0, south_1, east, corner = cut(blocked, rows, boxes)
    spans = [(0, rows + row, half + WS, near) for row in range(rows)]
    (local_1,) = norm([blocked], gain, bias, [spans])
    south_0 = exchange(south_0, 1, "win")
    south_1 = exchange(south_1, 1, "win")
    east = permute_by(east, "win", west)
    corner = permute_by(corner, "win", west_north)
    local_0_pieces = gather_pieces(local_0)
    local_1_pieces = gather_pieces(local_1)
    query_0, key_0, query_1, key_1 = region_tags(mask_zone_labeling[0], weights, count, near)
    out_weights = gather_weights(final_projection_matrix)

    spans = [(0, row, 0, WS) for row in range(rows)]
    (south_normed,) = norm([south_0], gain, bias, [spans])
    south_pieces = gather_pieces(south_normed)
    spans = [(piece, row, 0, WS) for piece in range(count) for row in range(rows)]
    (local_0_normed,) = norm(local_0_pieces, gain, bias, [spans])
    local_1_pieces[0] = after(local_1, south_normed)
    local_0, local_1 = project([[local_0_normed], local_1_pieces], weights)
    spans = [(0, row, 0, near) for row in range(rows)]
    spans += [(which, row, 0, half) for which in (1, 2) for row in range(rows)]
    (rest_normed,) = norm([after(south_1, local_0), east, corner], gain, bias, [spans])
    rest_pieces = gather_pieces(rest_normed)
    split = count // 2
    near_lanes, far_lanes, all_lanes = (0, split), (split, count), (0, count)
    (south_near,) = project([south_pieces[:split]], weights)
    south_pieces[split] = after(south_pieces[split], south_near)
    (south_far,) = project([south_pieces[split:]], weights)
    (rest_near,) = project([rest_pieces[:split]], weights)

    def attend_run(blocks, layout, tags, earlier, lo, hi):
        blocks = [after(blocks[0], *earlier), *blocks[1:]]
        singles = [(i, i + 1) for i in range(lo, hi)]
        return list(attend(blocks, layout, *tags, scales, count, singles, head_width))

    blocks, layout, tags = [local_0, south_near, south_far], [all_lanes, near_lanes, far_lanes], (query_0, key_0)
    outs_0 = attend_run(blocks, layout, tags, [], 0, count)
    rest_pieces[split] = after(rest_pieces[split], *outs_0)
    (rest_far,) = project([rest_pieces[split:]], weights)
    blocks, layout, tags = [local_1, rest_near, rest_far], [all_lanes, near_lanes, far_lanes], (query_1, key_1)
    far = attend_run(blocks, layout, tags, [], split, count)
    close = attend_run(blocks, layout, tags, far, 0, split)
    outs_1 = close + far

    first = send_heads(outs_0)
    second = send_heads(outs_1)
    first[0] = after(first[0], *outs_1)
    spans = [(0, rows + row, half, WS, row, 0) for row in range(rows)]
    spans += [(1, row, 0, WS, rows + row, 0) for row in range(rows)]
    shape = (row_count, col_count, width)
    done = finish(first, out_weights, [blocked, south_0], spans, (row_count, WS, width))
    second[0] = after(second[0], done)
    base = partial(second[:split], out_weights[:split])
    spans = [(0, rows + row, half + WS, near, row, WS) for row in range(rows)]
    spans += [(1, row, 0, near, rows + row, WS) for row in range(rows)]
    spans += [(2, row, 0, half, row, WS + near) for row in range(rows)]
    spans += [(3, row, 0, half, rows + row, WS + near) for row in range(rows)]
    mixed = finish_last(second[split:], out_weights[split:], base, done, [blocked, south_1, east, corner], spans, shape)
    return mixed[None, :, None]


def solution(mesh):
    in_specs = (
        P(("member", "win"), None, "seq", None, None),
        P(("member", "win"), None, None),
        P(),
        P(),
        P(None, None, "seq"),
        P("seq"),
        P("seq", None),
    )
    out_specs = P(("member", "win"), None, "seq", None, None)

    return jax.shard_map(on_device, mesh=mesh, in_specs=in_specs, out_specs=out_specs, check_vma=False)
```

```python
import functools
import math

import jax
import jax.numpy as jnp
from jax import lax
from jax.experimental import pallas as pl
from jax.experimental.pallas import tpu as pltpu
from jax.sharding import PartitionSpec as P


CHANNEL_PER_PART = 96
WS = 32
REGIONS = 32
LANE = 128
FAR = -1e30
F32 = jnp.float32
BF16 = jnp.bfloat16


def permute_by(value, axis, move):
    count = lax.axis_size(axis)
    pairs = [(source, move(source, count)) for source in range(count)]
    return lax.ppermute(value, axis, pairs)


def exchange(value, mask, axis="seq"):
    return permute_by(value, axis, lambda source, count: source ^ mask)


def masks_of(count):
    masks = []
    while count > 1:
        count //= 2
        masks.append(count)
    return masks


def gather_pieces(piece):
    pieces = {0: piece}
    for mask in masks_of(lax.axis_size("seq")):
        for offset in list(pieces):
            pieces[offset ^ mask] = exchange(pieces[offset], mask)
    return [pieces[offset] for offset in range(len(pieces))]


def padded(width):
    return (width + LANE - 1) // LANE * LANE


VMEM = pl.BlockSpec(memory_space=pltpu.VMEM)


def after(value, *earlier):
    return lax.optimization_barrier((value, *earlier))[0]


def normalized(held, gain, bias):
    values = held.astype(F32)
    average = jnp.mean(values, axis=-1, keepdims=True)
    centred = values - average
    variance = jnp.mean(centred * centred, axis=-1, keepdims=True)
    return (centred * lax.rsqrt(variance + 1e-05) * gain + bias).astype(BF16)


HELD = pl.BlockSpec(memory_space=pltpu.HBM)


def cut_kernel(boxes, pixel_ref, *outs):
    for (row, left, size), out_ref in zip(boxes, outs, strict=True):
        out_ref[...] = pixel_ref[row : row + out_ref.shape[0], left : left + size, :]


def cut(pixels, rows, boxes):
    width = pixels.shape[2]
    return pl.pallas_call(
        functools.partial(cut_kernel, boxes),
        out_shape=[jax.ShapeDtypeStruct((rows, size, width), BF16) for _, _, size in boxes],
        in_specs=[VMEM],
        out_specs=[VMEM] * len(boxes),
        compiler_params=pltpu.CompilerParams(vmem_limit_bytes=8 << 20),
        cost_estimate=pl.CostEstimate(flops=0, bytes_accessed=2 * pixels.size, transcendentals=0),
        name="cut",
    )(pixels)


def norm_kernel(groups, *refs):
    refs, outs = refs[: -len(groups)], refs[-len(groups) :]
    *sources, gain_ref, bias_ref = refs
    gain, bias = gain_ref[...][None], bias_ref[...][None]
    for spans, out_ref in zip(groups, outs, strict=True):
        into = 0
        for which, row, left, size in spans:
            held = sources[which][row, left : left + size, :]
            out_ref[into : into + size, :] = normalized(held, gain, bias)
            into += size


def norm(sources, gain, bias, groups):
    width = sources[0].shape[-1]
    totals = [sum(span[-1] for span in spans) for spans in groups]
    return pl.pallas_call(
        functools.partial(norm_kernel, groups),
        out_shape=[jax.ShapeDtypeStruct((total, width), BF16) for total in totals],
        in_specs=[VMEM] * (len(sources) + 2),
        out_specs=[VMEM] * len(groups),
        compiler_params=pltpu.CompilerParams(vmem_limit_bytes=8 << 20),
        cost_estimate=pl.CostEstimate(
            flops=10 * sum(totals) * width, bytes_accessed=4 * sum(totals) * width, transcendentals=0
        ),
    )(*sources, gain, bias)


def tag_kernel(count, near, label_ref, weight_ref, *outs):
    del weight_ref
    query_0, key_0, query_1, key_1 = outs
    row_count, _ = label_ref.shape
    rows = row_count // (2 * count)
    device = lax.axis_index("seq")
    turned = jnp.transpose(label_ref[...].astype(F32)).astype(BF16)
    place = lax.broadcasted_iota(jnp.int32, (row_count, LANE), 0)
    lane = (lax.broadcasted_iota(jnp.int32, (1, LANE), 1) % REGIONS).astype(F32)
    group = count * rows
    for half in range(2):
        for offset in range(count):
            for row in range(rows):
                at = (half * rows + row) * count + jnp.bitwise_xor(device, offset)
                chosen = jnp.where(place == at, 1.0, 0.0).astype(BF16)
                region = jnp.dot(turned, chosen, preferred_element_type=F32)
                same = region == lane
                query = jnp.where(same, 1.0, 0.0).astype(BF16)
                key = jnp.where(same, 0.0, FAR).astype(BF16)
                slot = offset * rows + row
                apart, span = group * near, near + 2 * (WS - near)
                beside = apart + offset * rows * span
                spots = [
                    (query_0, key_0, (half * group + slot) * WS, 0, WS),
                    (query_1, key_1, beside + row * near if half else slot * near, WS, near),
                    (
                        query_1,
                        key_1,
                        beside + rows * near + (half * rows + row) * (WS - near),
                        WS + near,
                        WS - near,
                    ),
                ]
                for query_ref, key_ref, into, left, size in spots:
                    query_ref[into : into + size, :] = query[left : left + size]
                    key_ref[into : into + size, :] = key[left : left + size]


def region_tags(labels, weights, count, near):
    pixels = labels.shape[0] * WS
    return pl.pallas_call(
        functools.partial(tag_kernel, count, near),
        out_shape=[jax.ShapeDtypeStruct((pixels, LANE), BF16)] * 4,
        in_specs=[VMEM] * 2,
        out_specs=[VMEM] * 4,
        compiler_params=pltpu.CompilerParams(vmem_limit_bytes=8 << 20),
        cost_estimate=pl.CostEstimate(
            flops=8 * pixels * LANE * labels.shape[0], bytes_accessed=8 * pixels * LANE, transcendentals=0
        ),
        name="tags",
    )(labels, weights)


def project_kernel(counts, *refs):
    groups = []
    for count in counts:
        groups.append(refs[:count])
        refs = refs[count:]
    weight_ref, *outs = refs
    block = jnp.concatenate([piece[...] for group in groups for piece in group], axis=0)
    head_width = weight_ref.shape[2]
    slot = padded(head_width)
    if slot == head_width:
        weights = jnp.concatenate([weight_ref[t] for t in range(3)], axis=1)
        products = [(0, jnp.dot(block, weights, preferred_element_type=F32).astype(BF16))]
    else:
        products = [
            (t * slot, jnp.dot(block, weight_ref[t], preferred_element_type=F32).astype(BF16))
            for t in range(3)
        ]
    at = 0
    for out_ref in outs:
        for left, product in products:
            part = product[at : at + out_ref.shape[0]]
            out_ref[:, left : left + part.shape[1]] = part
        at += out_ref.shape[0]


def project(groups, weights):
    width = groups[0][0].shape[1]
    slot = padded(weights.shape[2])
    sizes = [sum(piece.shape[0] for piece in group) for group in groups]
    total = sum(sizes)
    return pl.pallas_call(
        functools.partial(project_kernel, [len(group) for group in groups]),
        out_shape=[jax.ShapeDtypeStruct((size, 3 * slot), BF16) for size in sizes],
        in_specs=[VMEM] * (sum(len(group) for group in groups) + 1),
        out_specs=[VMEM] * len(groups),
        compiler_params=pltpu.CompilerParams(vmem_limit_bytes=24 << 20),
        cost_estimate=pl.CostEstimate(
            flops=2 * total * width * 3 * slot,
            bytes_accessed=2 * (total * width + weights.size + total * 3 * slot),
            transcendentals=0,
        ),
    )(*[piece for group in groups for piece in group], weights)


def attend_kernel(layout, ranges, head_width, *refs):
    parts = len(layout)
    blocks = refs[:parts]
    query_tags, key_tags, scale_ref = refs[parts : parts + 3]
    outs = refs[parts + 3 :]
    slot = padded(head_width)
    low, high = min(lo for lo, _ in ranges), max(hi for _, hi in ranges)
    heads = head_width // CHANNEL_PER_PART
    base = math.log2(math.e) / math.sqrt(CHANNEL_PER_PART)
    tiles = [None] * (slot // LANE)
    key_rows = key_tags[...]
    runs, query_rows, at = [], [], 0
    for block, (lo, hi) in zip(blocks, layout, strict=True):
        z = block.shape[0] // (hi - lo)
        first, last = max(low, lo), min(high, hi)
        if first < last:
            runs.append((block, (first - lo) * z, (last - lo) * z, z, first, last))
            query_rows.append(query_tags[at + (first - lo) * z : at + (last - lo) * z, :])
        at += block.shape[0]
    query_rows = jnp.concatenate(query_rows, axis=0)

    def span(head):
        first = head * CHANNEL_PER_PART
        last = first + CHANNEL_PER_PART
        left, right = first // LANE * LANE, padded(last)
        lane = lax.broadcasted_iota(jnp.int32, (1, right - left), 1)
        return left, right, (lane >= first - left) & (lane < last - left)

    def scores_of(head):
        left, right, inside = span(head)
        reps = (right - left) // LANE
        queries = jnp.concatenate([run[0][run[1] : run[2], left:right] for run in runs], axis=0)
        queries = jnp.where(inside, queries, jnp.concatenate([query_rows] * reps, axis=1))
        keys = jnp.concatenate([b[:, slot + left : slot + right] for b in blocks], axis=0)
        keys = jnp.where(inside, keys, jnp.concatenate([key_rows] * reps, axis=1))
        return lax.dot_general(queries, keys, (((1,), (1,)), ((), ())), preferred_element_type=F32)

    following = scores_of(0)
    for head in range(heads):
        scores = following
        if head + 1 < heads:
            following = scores_of(head + 1)
        left, right, inside = span(head)
        row_max = jnp.max(scores, axis=-1, keepdims=True)
        numerators = jnp.exp2((scores - row_max) * (scale_ref[head] * base))
        total = jnp.sum(numerators, axis=-1, keepdims=True)
        values = jnp.concatenate([b[:, 2 * slot + left : 2 * slot + right] for b in blocks], axis=0)
        mixed = jnp.dot(numerators.astype(BF16), values, preferred_element_type=F32) / total
        for i in range((right - left) // LANE):
            tile = left // LANE + i
            own = mixed[:, i * LANE : (i + 1) * LANE]
            held = tiles[tile]
            tiles[tile] = own if held is None else jnp.where(inside[:, i * LANE : (i + 1) * LANE], own, held)
    result = jnp.concatenate(tiles, axis=1)[:, :head_width].astype(BF16)
    places = {
        offset: (out_ref, offset - lo)
        for out_ref, (lo, hi) in zip(outs, ranges, strict=True)
        for offset in range(lo, hi)
    }
    into = dict.fromkeys(places, 0)
    at = 0
    for _, _, _, z, first, last in runs:
        for offset in range(first, last):
            out_ref, index = places[offset]
            out_ref[index, into[offset] : into[offset] + z, :] = result[at : at + z]
            into[offset] += z
            at += z


def attend(blocks, layout, query_tags, key_tags, scales, count, ranges, head_width):
    pixels = sum(block.shape[0] for block in blocks)
    per_offset = pixels // count
    asked = sum(hi - lo for lo, hi in ranges) * per_offset
    heads = head_width // CHANNEL_PER_PART
    return pl.pallas_call(
        functools.partial(attend_kernel, layout, ranges, head_width),
        out_shape=[
            jax.ShapeDtypeStruct((hi - lo, per_offset, head_width), BF16) for lo, hi in ranges
        ],
        in_specs=[VMEM] * (len(blocks) + 2) + [pl.BlockSpec(memory_space=pltpu.SMEM)],
        out_specs=[VMEM] * len(ranges),
        compiler_params=pltpu.CompilerParams(vmem_limit_bytes=28 << 20),
        cost_estimate=pl.CostEstimate(
            flops=4 * heads * asked * pixels * 2 * LANE,
            bytes_accessed=2 * pixels * 3 * padded(head_width),
            transcendentals=heads * asked * pixels,
        ),
    )(*blocks, query_tags, key_tags, scales)


def product(attended, weights, columns=slice(None)):
    total = None
    for piece, weight in zip(attended, weights, strict=True):
        term = jnp.dot(piece[...], weight[:, columns], preferred_element_type=F32)
        total = term if total is None else total + term
    return total


def partial_kernel(count, *refs):
    *refs, out_ref = refs
    out_ref[...] = product(refs[:count], refs[count:])


def partial(attended, weights):
    pixels, depth = attended[0].shape
    width = weights[0].shape[1]
    return pl.pallas_call(
        functools.partial(partial_kernel, len(weights)),
        out_shape=jax.ShapeDtypeStruct((pixels, width), F32),
        in_specs=[VMEM] * (2 * len(weights)),
        out_specs=VMEM,
        compiler_params=pltpu.CompilerParams(vmem_limit_bytes=20 << 20),
        cost_estimate=pl.CostEstimate(
            flops=2 * pixels * width * depth * len(weights), bytes_accessed=2 * width * (depth + 2 * pixels), transcendentals=0
        ),
    )(*attended, *weights)


def finish_kernel(count, spans, *refs):
    attended, weights, sources, out_ref = refs[:count], refs[count : 2 * count], refs[2 * count : -1], refs[-1]
    total = product(attended, weights)
    at = 0
    for which, row, start, pixels, into, column in spans:
        held = sources[which][row, start : start + pixels, :].astype(F32)
        out_ref[into, column : column + pixels, :] = (held + total[at : at + pixels]).astype(BF16)
        at += pixels


def finish(attended, weights, sources, spans, shape):
    count = len(weights)
    pixels, width = attended[0].shape[0], shape[-1]
    return pl.pallas_call(
        functools.partial(finish_kernel, count, spans),
        out_shape=jax.ShapeDtypeStruct(shape, BF16),
        in_specs=[VMEM] * (2 * count + len(sources)),
        out_specs=VMEM,
        compiler_params=pltpu.CompilerParams(vmem_limit_bytes=20 << 20),
        cost_estimate=pl.CostEstimate(
            flops=2 * pixels * width * width, bytes_accessed=2 * width * (width + 3 * pixels), transcendentals=0
        ),
    )(*attended, *weights, *sources)


def last_kernel(count, chunks, spans, *refs):
    attended, weights = refs[:count], refs[count : 2 * count]
    base_ref, done_ref, *sources, out_ref, ready, semaphore = refs[2 * count :]
    left, size, width = done_ref.shape[1], ready.shape[1], ready.shape[2]
    wide = width // chunks
    copies = [
        pltpu.make_async_copy(done_ref, out_ref.at[:, pl.ds(0, left), :], semaphore.at[chunks])
    ]
    copies[0].start()
    for chunk in range(chunks):
        columns = slice(chunk * wide, (chunk + 1) * wide)
        total = product(attended, weights, columns) + base_ref[:, columns]
        at = 0
        for which, row, start, pixels, into, column in spans:
            held = sources[which][row, start : start + pixels, columns].astype(F32)
            ready[into, column - left : column - left + pixels, columns] = (
                held + total[at : at + pixels]
            ).astype(BF16)
            at += pixels
        place = pl.ds(chunk * wide, wide)
        copy = pltpu.make_async_copy(
            ready.at[:, :, place], out_ref.at[:, pl.ds(left, size), place], semaphore.at[chunk]
        )
        copy.start()
        copies.append(copy)
    for copy in copies:
        copy.wait()


def finish_last(attended, weights, base, done, sources, spans, shape):
    count = len(weights)
    row_count, col_count, width = shape
    pixels, depth = attended[0].shape
    chunks = 3 if width % (3 * 2 * LANE) == 0 else 1
    return pl.pallas_call(
        functools.partial(last_kernel, count, chunks, spans),
        out_shape=jax.ShapeDtypeStruct(shape, BF16),
        in_specs=[VMEM] * (2 * count + 2 + len(sources)),
        out_specs=HELD,
        scratch_shapes=[
            pltpu.VMEM((row_count, col_count - done.shape[1], width), BF16),
            pltpu.SemaphoreType.DMA((chunks + 1,)),
        ],
        compiler_params=pltpu.CompilerParams(vmem_limit_bytes=20 << 20),
        cost_estimate=pl.CostEstimate(
            flops=2 * pixels * width * depth * count, bytes_accessed=2 * width * (width + 3 * pixels), transcendentals=0
        ),
    )(*attended, *weights, base, done, *sources)


def send_heads(outs):
    own = [outs[0]]
    for offset in range(1, len(outs)):
        own.append(exchange(outs[offset], offset))
    return [piece[0] for piece in own]


def pick_kernel(place, source_ref, out_ref, semaphore):
    size = out_ref.shape[0]
    start = pl.multiple_of(place() * size, 16)
    copy = pltpu.make_async_copy(source_ref.at[pl.ds(start, size), :], out_ref, semaphore)
    copy.start()
    copy.wait()


def join_kernel(place, own_ref, other_ref, out_ref):
    size = own_ref.shape[0]
    at = place()
    out_ref[pl.ds(pl.multiple_of(at * size, 16), size), :] = own_ref[...]
    out_ref[pl.ds(pl.multiple_of((1 - at) * size, 16), size), :] = other_ref[...]


def small_call(kernel, rows, *operands, spec=VMEM, scratch=()):
    width = operands[0].shape[1]
    return pl.pallas_call(
        kernel,
        out_shape=jax.ShapeDtypeStruct((rows, width), BF16),
        in_specs=[spec] * len(operands),
        out_specs=VMEM,
        scratch_shapes=scratch,
        compiler_params=pltpu.CompilerParams(vmem_limit_bytes=8 << 20),
        cost_estimate=pl.CostEstimate(flops=0, bytes_accessed=4 * rows * width, transcendentals=0),
    )(*operands)


def gather_weights(block):
    levels = []
    rows = block.shape[0]
    for axis in ("win", "member"):
        if lax.axis_size(axis) % 2 == 0 and rows % (32 << len(levels)) == 0:
            levels.append(axis)

    def bit(axis):
        return lax.axis_index(axis) & 1

    def part_index():
        index = 0
        for axis in levels:
            index = index * 2 + bit(axis)
        return index

    pieces = {0: block}
    for mask in masks_of(lax.axis_size("seq")):
        for offset in list(pieces):
            piece = pieces[offset]
            if mask > 1 and levels:
                size = rows >> len(levels)
                part = small_call(
                    functools.partial(pick_kernel, part_index),
                    size,
                    piece,
                    spec=HELD,
                    scratch=[pltpu.SemaphoreType.DMA],
                )
                part = exchange(part, mask)
                for axis in reversed(levels):
                    other = exchange(part, 1, axis)
                    size *= 2
                    part = small_call(functools.partial(join_kernel, functools.partial(bit, axis)), size, part, other)
                pieces[offset ^ mask] = part
            else:
                pieces[offset ^ mask] = exchange(piece, mask)
    return [pieces[offset] for offset in range(len(pieces))]


def on_device(
    pixel_grid_input,
    mask_zone_labeling,
    standardize_multiplier,
    standardize_offset_vector,
    triple_projection_matrix,
    logit_scaling_per_part,
    final_projection_matrix,
):
    count = lax.axis_size("seq")
    blocked = pixel_grid_input[0, :, 0]
    row_count, col_count, width = blocked.shape
    rows = row_count // 2
    half = WS // 2
    head_width = triple_projection_matrix.shape[2]

    def west(source, count):
        return (source - 2) % count

    def west_north(source, count):
        return ((source ^ 1) - 2) % count

    near = WS - half
    gain, bias = standardize_multiplier, standardize_offset_vector
    weights = triple_projection_matrix
    scales = logit_scaling_per_part

    boxes = [(rows, half, WS), (0, half, WS), (0, half + WS, near), (rows, 0, half), (0, 0, half)]
    local_0, south_0, south_1, east, corner = cut(blocked, rows, boxes)
    spans = [(0, rows + row, half + WS, near) for row in range(rows)]
    (local_1,) = norm([blocked], gain, bias, [spans])
    south_0 = exchange(south_0, 1, "win")
    south_1 = exchange(south_1, 1, "win")
    east = permute_by(east, "win", west)
    corner = permute_by(corner, "win", west_north)
    local_0_pieces = gather_pieces(local_0)
    local_1_pieces = gather_pieces(local_1)
    query_0, key_0, query_1, key_1 = region_tags(mask_zone_labeling[0], weights, count, near)
    out_weights = gather_weights(final_projection_matrix)

    spans = [(0, row, 0, WS) for row in range(rows)]
    (south_normed,) = norm([south_0], gain, bias, [spans])
    south_pieces = gather_pieces(south_normed)
    spans = [(piece, row, 0, WS) for piece in range(count) for row in range(rows)]
    (local_0_normed,) = norm(local_0_pieces, gain, bias, [spans])
    local_1_pieces[0] = after(local_1, south_normed)
    local_0, local_1 = project([[local_0_normed], local_1_pieces], weights)
    spans = [(0, row, 0, near) for row in range(rows)]
    spans += [(which, row, 0, half) for which in (1, 2) for row in range(rows)]
    (rest_normed,) = norm([after(south_1, local_0), east, corner], gain, bias, [spans])
    rest_pieces = gather_pieces(rest_normed)
    split = count // 2
    near_lanes, far_lanes, all_lanes = (0, split), (split, count), (0, count)
    (south_near,) = project([south_pieces[:split]], weights)
    south_pieces[split] = after(south_pieces[split], south_near)
    (south_far,) = project([south_pieces[split:]], weights)
    (rest_near,) = project([rest_pieces[:split]], weights)

    def attend_run(blocks, layout, tags, earlier, lo, hi):
        blocks = [after(blocks[0], *earlier), *blocks[1:]]
        singles = [(i, i + 1) for i in range(lo, hi)]
        return list(attend(blocks, layout, *tags, scales, count, singles, head_width))

    blocks, layout, tags = [local_0, south_near, south_far], [all_lanes, near_lanes, far_lanes], (query_0, key_0)
    outs_0 = attend_run(blocks, layout, tags, [], 0, count)
    rest_pieces[split] = after(rest_pieces[split], *outs_0)
    (rest_far,) = project([rest_pieces[split:]], weights)
    blocks, layout, tags = [local_1, rest_near, rest_far], [all_lanes, near_lanes, far_lanes], (query_1, key_1)
    far = attend_run(blocks, layout, tags, [], split, count)
    close = attend_run(blocks, layout, tags, far, 0, split)
    outs_1 = close + far

    first = send_heads(outs_0)
    second = send_heads(outs_1)
    first[0] = after(first[0], *outs_1)
    spans = [(0, rows + row, half, WS, row, 0) for row in range(rows)]
    spans += [(1, row, 0, WS, rows + row, 0) for row in range(rows)]
    shape = (row_count, col_count, width)
    done = finish(first, out_weights, [blocked, south_0], spans, (row_count, WS, width))
    second[0] = after(second[0], done)
    base = partial(second[:split], out_weights[:split])
    spans = [(0, rows + row, half + WS, near, row, WS) for row in range(rows)]
    spans += [(1, row, 0, near, rows + row, WS) for row in range(rows)]
    spans += [(2, row, 0, half, row, WS + near) for row in range(rows)]
    spans += [(3, row, 0, half, rows + row, WS + near) for row in range(rows)]
    mixed = finish_last(second[split:], out_weights[split:], base, done, [blocked, south_1, east, corner], spans, shape)
    return mixed[None, :, None]


def solution(mesh):
    in_specs = (
        P(("member", "win"), None, "seq", None, None),
        P(("member", "win"), None, None),
        P(),
        P(),
        P(None, None, "seq"),
        P("seq"),
        P("seq", None),
    )
    out_specs = P(("member", "win"), None, "seq", None, None)

    return jax.shard_map(on_device, mesh=mesh, in_specs=in_specs, out_specs=out_specs, check_vma=False)
```

```python
import functools
import math

import jax
import jax.numpy as jnp
from jax import lax
from jax.experimental import pallas as pl
from jax.experimental.pallas import tpu as pltpu
from jax.sharding import PartitionSpec as P


CHANNEL_PER_PART = 96
WS = 32
REGIONS = 32
LANE = 128
FAR = -1e30
F32 = jnp.float32
BF16 = jnp.bfloat16


def permute_by(value, axis, move):
    count = lax.axis_size(axis)
    pairs = [(source, move(source, count)) for source in range(count)]
    return lax.ppermute(value, axis, pairs)


def exchange(value, mask, axis="seq"):
    return permute_by(value, axis, lambda source, count: source ^ mask)


def masks_of(count):
    masks = []
    while count > 1:
        count //= 2
        masks.append(count)
    return masks


def gather_pieces(piece):
    pieces = {0: piece}
    for mask in masks_of(lax.axis_size("seq")):
        for offset in list(pieces):
            pieces[offset ^ mask] = exchange(pieces[offset], mask)
    return [pieces[offset] for offset in range(len(pieces))]


def padded(width):
    return (width + LANE - 1) // LANE * LANE


VMEM = pl.BlockSpec(memory_space=pltpu.VMEM)


def after(value, *earlier):
    return lax.optimization_barrier((value, *earlier))[0]


def normalized(held, gain, bias):
    values = held.astype(F32)
    average = jnp.mean(values, axis=-1, keepdims=True)
    centred = values - average
    variance = jnp.mean(centred * centred, axis=-1, keepdims=True)
    return (centred * lax.rsqrt(variance + 1e-05) * gain + bias).astype(BF16)


HELD = pl.BlockSpec(memory_space=pltpu.HBM)


def cut_kernel(boxes, pixel_ref, *outs):
    for (row, left, size), out_ref in zip(boxes, outs, strict=True):
        out_ref[...] = pixel_ref[row : row + out_ref.shape[0], left : left + size, :]


def cut(pixels, rows, boxes):
    width = pixels.shape[2]
    return pl.pallas_call(
        functools.partial(cut_kernel, boxes),
        out_shape=[jax.ShapeDtypeStruct((rows, size, width), BF16) for _, _, size in boxes],
        in_specs=[VMEM],
        out_specs=[VMEM] * len(boxes),
        compiler_params=pltpu.CompilerParams(vmem_limit_bytes=8 << 20),
        cost_estimate=pl.CostEstimate(flops=0, bytes_accessed=2 * pixels.size, transcendentals=0),
        name="cut",
    )(pixels)


def norm_kernel(groups, *refs):
    refs, outs = refs[: -len(groups)], refs[-len(groups) :]
    *sources, gain_ref, bias_ref = refs
    gain, bias = gain_ref[...][None], bias_ref[...][None]
    for spans, out_ref in zip(groups, outs, strict=True):
        into = 0
        for which, row, left, size in spans:
            held = sources[which][row, left : left + size, :]
            out_ref[into : into + size, :] = normalized(held, gain, bias)
            into += size


def norm(sources, gain, bias, groups):
    width = sources[0].shape[-1]
    totals = [sum(span[-1] for span in spans) for spans in groups]
    return pl.pallas_call(
        functools.partial(norm_kernel, groups),
        out_shape=[jax.ShapeDtypeStruct((total, width), BF16) for total in totals],
        in_specs=[VMEM] * (len(sources) + 2),
        out_specs=[VMEM] * len(groups),
        compiler_params=pltpu.CompilerParams(vmem_limit_bytes=8 << 20),
        cost_estimate=pl.CostEstimate(
            flops=10 * sum(totals) * width, bytes_accessed=4 * sum(totals) * width, transcendentals=0
        ),
    )(*sources, gain, bias)


def tag_kernel(count, near, label_ref, weight_ref, *outs):
    del weight_ref
    query_0, key_0, query_1, key_1 = outs
    row_count, _ = label_ref.shape
    rows = row_count // (2 * count)
    device = lax.axis_index("seq")
    turned = jnp.transpose(label_ref[...].astype(F32)).astype(BF16)
    place = lax.broadcasted_iota(jnp.int32, (row_count, LANE), 0)
    lane = (lax.broadcasted_iota(jnp.int32, (1, LANE), 1) % REGIONS).astype(F32)
    group = count * rows
    for half in range(2):
        for offset in range(count):
            for row in range(rows):
                at = (half * rows + row) * count + jnp.bitwise_xor(device, offset)
                chosen = jnp.where(place == at, 1.0, 0.0).astype(BF16)
                region = jnp.dot(turned, chosen, preferred_element_type=F32)
                same = region == lane
                query = jnp.where(same, 1.0, 0.0).astype(BF16)
                key = jnp.where(same, 0.0, FAR).astype(BF16)
                slot = offset * rows + row
                apart, span = group * near, near + 2 * (WS - near)
                beside = apart + offset * rows * span
                spots = [
                    (query_0, key_0, (half * group + slot) * WS, 0, WS),
                    (query_1, key_1, beside + row * near if half else slot * near, WS, near),
                    (
                        query_1,
                        key_1,
                        beside + rows * near + (half * rows + row) * (WS - near),
                        WS + near,
                        WS - near,
                    ),
                ]
                for query_ref, key_ref, into, left, size in spots:
                    query_ref[into : into + size, :] = query[left : left + size]
                    key_ref[into : into + size, :] = key[left : left + size]


def region_tags(labels, weights, count, near):
    pixels = labels.shape[0] * WS
    return pl.pallas_call(
        functools.partial(tag_kernel, count, near),
        out_shape=[jax.ShapeDtypeStruct((pixels, LANE), BF16)] * 4,
        in_specs=[VMEM] * 2,
        out_specs=[VMEM] * 4,
        compiler_params=pltpu.CompilerParams(vmem_limit_bytes=8 << 20),
        cost_estimate=pl.CostEstimate(
            flops=8 * pixels * LANE * labels.shape[0], bytes_accessed=8 * pixels * LANE, transcendentals=0
        ),
        name="tags",
    )(labels, weights)


def project_kernel(counts, *refs):
    groups = []
    for count in counts:
        groups.append(refs[:count])
        refs = refs[count:]
    weight_ref, *outs = refs
    block = jnp.concatenate([piece[...] for group in groups for piece in group], axis=0)
    head_width = weight_ref.shape[2]
    slot = padded(head_width)
    if slot == head_width:
        weights = jnp.concatenate([weight_ref[t] for t in range(3)], axis=1)
        products = [(0, jnp.dot(block, weights, preferred_element_type=F32).astype(BF16))]
    else:
        products = [
            (t * slot, jnp.dot(block, weight_ref[t], preferred_element_type=F32).astype(BF16))
            for t in range(3)
        ]
    at = 0
    for out_ref in outs:
        for left, product in products:
            part = product[at : at + out_ref.shape[0]]
            out_ref[:, left : left + part.shape[1]] = part
        at += out_ref.shape[0]


def project(groups, weights):
    width = groups[0][0].shape[1]
    slot = padded(weights.shape[2])
    sizes = [sum(piece.shape[0] for piece in group) for group in groups]
    total = sum(sizes)
    return pl.pallas_call(
        functools.partial(project_kernel, [len(group) for group in groups]),
        out_shape=[jax.ShapeDtypeStruct((size, 3 * slot), BF16) for size in sizes],
        in_specs=[VMEM] * (sum(len(group) for group in groups) + 1),
        out_specs=[VMEM] * len(groups),
        compiler_params=pltpu.CompilerParams(vmem_limit_bytes=24 << 20),
        cost_estimate=pl.CostEstimate(
            flops=2 * total * width * 3 * slot,
            bytes_accessed=2 * (total * width + weights.size + total * 3 * slot),
            transcendentals=0,
        ),
    )(*[piece for group in groups for piece in group], weights)


def attend_kernel(layout, ranges, head_width, *refs):
    parts = len(layout)
    blocks = refs[:parts]
    query_tags, key_tags, scale_ref = refs[parts : parts + 3]
    outs = refs[parts + 3 :]
    slot = padded(head_width)
    low, high = min(lo for lo, _ in ranges), max(hi for _, hi in ranges)
    heads = head_width // CHANNEL_PER_PART
    base = math.log2(math.e) / math.sqrt(CHANNEL_PER_PART)
    tiles = [None] * (slot // LANE)
    key_rows = key_tags[...]
    runs, query_rows, at = [], [], 0
    for block, (lo, hi) in zip(blocks, layout, strict=True):
        z = block.shape[0] // (hi - lo)
        first, last = max(low, lo), min(high, hi)
        if first < last:
            runs.append((block, (first - lo) * z, (last - lo) * z, z, first, last))
            query_rows.append(query_tags[at + (first - lo) * z : at + (last - lo) * z, :])
        at += block.shape[0]
    query_rows = jnp.concatenate(query_rows, axis=0)

    def span(head):
        first = head * CHANNEL_PER_PART
        last = first + CHANNEL_PER_PART
        left, right = first // LANE * LANE, padded(last)
        lane = lax.broadcasted_iota(jnp.int32, (1, right - left), 1)
        return left, right, (lane >= first - left) & (lane < last - left)

    def scores_of(head):
        left, right, inside = span(head)
        reps = (right - left) // LANE
        queries = jnp.concatenate([run[0][run[1] : run[2], left:right] for run in runs], axis=0)
        queries = jnp.where(inside, queries, jnp.concatenate([query_rows] * reps, axis=1))
        keys = jnp.concatenate([b[:, slot + left : slot + right] for b in blocks], axis=0)
        keys = jnp.where(inside, keys, jnp.concatenate([key_rows] * reps, axis=1))
        return lax.dot_general(queries, keys, (((1,), (1,)), ((), ())), preferred_element_type=F32)

    following = scores_of(0)
    for head in range(heads):
        scores = following
        if head + 1 < heads:
            following = scores_of(head + 1)
        left, right, inside = span(head)
        row_max = jnp.max(scores, axis=-1, keepdims=True)
        numerators = jnp.exp2((scores - row_max) * (scale_ref[head] * base))
        total = jnp.sum(numerators, axis=-1, keepdims=True)
        values = jnp.concatenate([b[:, 2 * slot + left : 2 * slot + right] for b in blocks], axis=0)
        mixed = jnp.dot(numerators.astype(BF16), values, preferred_element_type=F32) / total
        for i in range((right - left) // LANE):
            tile = left // LANE + i
            own = mixed[:, i * LANE : (i + 1) * LANE]
            held = tiles[tile]
            tiles[tile] = own if held is None else jnp.where(inside[:, i * LANE : (i + 1) * LANE], own, held)
    result = jnp.concatenate(tiles, axis=1)[:, :head_width].astype(BF16)
    places = {
        offset: (out_ref, offset - lo)
        for out_ref, (lo, hi) in zip(outs, ranges, strict=True)
        for offset in range(lo, hi)
    }
    into = dict.fromkeys(places, 0)
    at = 0
    for _, _, _, z, first, last in runs:
        for offset in range(first, last):
            out_ref, index = places[offset]
            out_ref[index, into[offset] : into[offset] + z, :] = result[at : at + z]
            into[offset] += z
            at += z


def attend(blocks, layout, query_tags, key_tags, scales, count, ranges, head_width):
    pixels = sum(block.shape[0] for block in blocks)
    per_offset = pixels // count
    asked = sum(hi - lo for lo, hi in ranges) * per_offset
    heads = head_width // CHANNEL_PER_PART
    return pl.pallas_call(
        functools.partial(attend_kernel, layout, ranges, head_width),
        out_shape=[
            jax.ShapeDtypeStruct((hi - lo, per_offset, head_width), BF16) for lo, hi in ranges
        ],
        in_specs=[VMEM] * (len(blocks) + 2) + [pl.BlockSpec(memory_space=pltpu.SMEM)],
        out_specs=[VMEM] * len(ranges),
        compiler_params=pltpu.CompilerParams(vmem_limit_bytes=28 << 20),
        cost_estimate=pl.CostEstimate(
            flops=4 * heads * asked * pixels * 2 * LANE,
            bytes_accessed=2 * pixels * 3 * padded(head_width),
            transcendentals=heads * asked * pixels,
        ),
    )(*blocks, query_tags, key_tags, scales)


def product(attended, weights, columns=slice(None)):
    total = None
    for piece, weight in zip(attended, weights, strict=True):
        term = jnp.dot(piece[...], weight[:, columns], preferred_element_type=F32)
        total = term if total is None else total + term
    return total


def partial_kernel(count, *refs):
    *refs, out_ref = refs
    out_ref[...] = product(refs[:count], refs[count:])


def partial(attended, weights):
    pixels, depth = attended[0].shape
    width = weights[0].shape[1]
    return pl.pallas_call(
        functools.partial(partial_kernel, len(weights)),
        out_shape=jax.ShapeDtypeStruct((pixels, width), F32),
        in_specs=[VMEM] * (2 * len(weights)),
        out_specs=VMEM,
        compiler_params=pltpu.CompilerParams(vmem_limit_bytes=20 << 20),
        cost_estimate=pl.CostEstimate(
            flops=2 * pixels * width * depth * len(weights), bytes_accessed=2 * width * (depth + 2 * pixels), transcendentals=0
        ),
    )(*attended, *weights)


def finish_kernel(count, spans, *refs):
    attended, weights, sources, out_ref = refs[:count], refs[count : 2 * count], refs[2 * count : -1], refs[-1]
    total = product(attended, weights)
    at = 0
    for which, row, start, pixels, into, column in spans:
        held = sources[which][row, start : start + pixels, :].astype(F32)
        out_ref[into, column : column + pixels, :] = (held + total[at : at + pixels]).astype(BF16)
        at += pixels


def finish(attended, weights, sources, spans, shape):
    count = len(weights)
    pixels, width = attended[0].shape[0], shape[-1]
    return pl.pallas_call(
        functools.partial(finish_kernel, count, spans),
        out_shape=jax.ShapeDtypeStruct(shape, BF16),
        in_specs=[VMEM] * (2 * count + len(sources)),
        out_specs=VMEM,
        compiler_params=pltpu.CompilerParams(vmem_limit_bytes=20 << 20),
        cost_estimate=pl.CostEstimate(
            flops=2 * pixels * width * width, bytes_accessed=2 * width * (width + 3 * pixels), transcendentals=0
        ),
    )(*attended, *weights, *sources)


def last_kernel(count, chunks, spans, *refs):
    attended, weights = refs[:count], refs[count : 2 * count]
    base_ref, done_ref, *sources, out_ref, ready, semaphore = refs[2 * count :]
    left, size, width = done_ref.shape[1], ready.shape[1], ready.shape[2]
    wide = width // chunks
    copies = [
        pltpu.make_async_copy(done_ref, out_ref.at[:, pl.ds(0, left), :], semaphore.at[chunks])
    ]
    copies[0].start()
    for chunk in range(chunks):
        columns = slice(chunk * wide, (chunk + 1) * wide)
        total = product(attended, weights, columns) + base_ref[:, columns]
        at = 0
        for which, row, start, pixels, into, column in spans:
            held = sources[which][row, start : start + pixels, columns].astype(F32)
            ready[into, column - left : column - left + pixels, columns] = (
                held + total[at : at + pixels]
            ).astype(BF16)
            at += pixels
        place = pl.ds(chunk * wide, wide)
        copy = pltpu.make_async_copy(
            ready.at[:, :, place], out_ref.at[:, pl.ds(left, size), place], semaphore.at[chunk]
        )
        copy.start()
        copies.append(copy)
    for copy in copies:
        copy.wait()


def finish_last(attended, weights, base, done, sources, spans, shape):
    count = len(weights)
    row_count, col_count, width = shape
    pixels, depth = attended[0].shape
    chunks = 3 if width % (3 * 2 * LANE) == 0 else 1
    return pl.pallas_call(
        functools.partial(last_kernel, count, chunks, spans),
        out_shape=jax.ShapeDtypeStruct(shape, BF16),
        in_specs=[VMEM] * (2 * count + 2 + len(sources)),
        out_specs=HELD,
        scratch_shapes=[
            pltpu.VMEM((row_count, col_count - done.shape[1], width), BF16),
            pltpu.SemaphoreType.DMA((chunks + 1,)),
        ],
        compiler_params=pltpu.CompilerParams(vmem_limit_bytes=20 << 20),
        cost_estimate=pl.CostEstimate(
            flops=2 * pixels * width * depth * count, bytes_accessed=2 * width * (width + 3 * pixels), transcendentals=0
        ),
    )(*attended, *weights, base, done, *sources)


def send_heads(outs):
    own = [outs[0]]
    for offset in range(1, len(outs)):
        own.append(exchange(outs[offset], offset))
    return [piece[0] for piece in own]


def pick_kernel(place, source_ref, out_ref, semaphore):
    size = out_ref.shape[0]
    start = pl.multiple_of(place() * size, 16)
    copy = pltpu.make_async_copy(source_ref.at[pl.ds(start, size), :], out_ref, semaphore)
    copy.start()
    copy.wait()


def join_kernel(place, own_ref, other_ref, out_ref):
    size = own_ref.shape[0]
    at = place()
    out_ref[pl.ds(pl.multiple_of(at * size, 16), size), :] = own_ref[...]
    out_ref[pl.ds(pl.multiple_of((1 - at) * size, 16), size), :] = other_ref[...]


def small_call(kernel, rows, *operands, spec=VMEM, scratch=()):
    width = operands[0].shape[1]
    return pl.pallas_call(
        kernel,
        out_shape=jax.ShapeDtypeStruct((rows, width), BF16),
        in_specs=[spec] * len(operands),
        out_specs=VMEM,
        scratch_shapes=scratch,
        compiler_params=pltpu.CompilerParams(vmem_limit_bytes=8 << 20),
        cost_estimate=pl.CostEstimate(flops=0, bytes_accessed=4 * rows * width, transcendentals=0),
    )(*operands)


def gather_weights(block):
    levels = []
    rows = block.shape[0]
    for axis in ("win", "member"):
        if lax.axis_size(axis) % 2 == 0 and rows % (32 << len(levels)) == 0:
            levels.append(axis)

    def bit(axis):
        return lax.axis_index(axis) & 1

    def part_index():
        index = 0
        for axis in levels:
            index = index * 2 + bit(axis)
        return index

    pieces = {0: block}
    for mask in masks_of(lax.axis_size("seq")):
        for offset in list(pieces):
            piece = pieces[offset]
            if mask > 1 and levels:
                size = rows >> len(levels)
                part = small_call(
                    functools.partial(pick_kernel, part_index),
                    size,
                    piece,
                    spec=HELD,
                    scratch=[pltpu.SemaphoreType.DMA],
                )
                part = exchange(part, mask)
                for axis in reversed(levels):
                    other = exchange(part, 1, axis)
                    size *= 2
                    part = small_call(functools.partial(join_kernel, functools.partial(bit, axis)), size, part, other)
                pieces[offset ^ mask] = part
            else:
                pieces[offset ^ mask] = exchange(piece, mask)
    return [pieces[offset] for offset in range(len(pieces))]


def on_device(
    pixel_grid_input,
    mask_zone_labeling,
    standardize_multiplier,
    standardize_offset_vector,
    triple_projection_matrix,
    logit_scaling_per_part,
    final_projection_matrix,
):
    count = lax.axis_size("seq")
    blocked = pixel_grid_input[0, :, 0]
    row_count, col_count, width = blocked.shape
    rows = row_count // 2
    half = WS // 2
    head_width = triple_projection_matrix.shape[2]

    def west(source, count):
        return (source - 2) % count

    def west_north(source, count):
        return ((source ^ 1) - 2) % count

    near = WS - half
    gain, bias = standardize_multiplier, standardize_offset_vector
    weights = triple_projection_matrix
    scales = logit_scaling_per_part

    boxes = [(rows, half, WS), (0, half, WS), (0, half + WS, near), (rows, 0, half), (0, 0, half)]
    local_0, south_0, south_1, east, corner = cut(blocked, rows, boxes)
    spans = [(0, rows + row, half + WS, near) for row in range(rows)]
    (local_1,) = norm([blocked], gain, bias, [spans])
    south_0 = exchange(south_0, 1, "win")
    south_1 = exchange(south_1, 1, "win")
    east = permute_by(east, "win", west)
    corner = permute_by(corner, "win", west_north)
    local_0_pieces = gather_pieces(local_0)
    local_1_pieces = gather_pieces(local_1)
    query_0, key_0, query_1, key_1 = region_tags(mask_zone_labeling[0], weights, count, near)
    out_weights = gather_weights(final_projection_matrix)

    spans = [(0, row, 0, WS) for row in range(rows)]
    (south_normed,) = norm([south_0], gain, bias, [spans])
    south_pieces = gather_pieces(south_normed)
    spans = [(piece, row, 0, WS) for piece in range(count) for row in range(rows)]
    (local_0_normed,) = norm(local_0_pieces, gain, bias, [spans])
    (local_0,) = project([[local_0_normed]], weights)
    spans = [(0, row, 0, near) for row in range(rows)]
    spans += [(which, row, 0, half) for which in (1, 2) for row in range(rows)]
    (rest_normed,) = norm([south_1, east, corner], gain, bias, [spans])
    rest_pieces = gather_pieces(rest_normed)
    split = count // 2
    near_lanes, far_lanes, all_lanes = (0, split), (split, count), (0, count)
    south_near, local_1 = project([south_pieces[:split], local_1_pieces], weights)
    south_pieces[split] = after(south_pieces[split], south_near)
    (south_far,) = project([south_pieces[split:]], weights)
    (rest_near,) = project([rest_pieces[:split]], weights)

    def attend_run(blocks, layout, tags, earlier, lo, hi):
        blocks = [after(blocks[0], *earlier), *blocks[1:]]
        singles = [(i, i + 1) for i in range(lo, hi)]
        return list(attend(blocks, layout, *tags, scales, count, singles, head_width))

    blocks, layout, tags = [local_0, south_near, south_far], [all_lanes, near_lanes, far_lanes], (query_0, key_0)
    outs_0 = attend_run(blocks, layout, tags, [], 0, count)
    rest_pieces[split] = after(rest_pieces[split], *outs_0)
    (rest_far,) = project([rest_pieces[split:]], weights)
    blocks, layout, tags = [local_1, rest_near, rest_far], [all_lanes, near_lanes, far_lanes], (query_1, key_1)
    far = attend_run(blocks, layout, tags, [], split, count)
    close = attend_run(blocks, layout, tags, far, 0, split)
    outs_1 = close + far

    first = send_heads(outs_0)
    second = send_heads(outs_1)
    first[0] = after(first[0], *outs_1)
    spans = [(0, rows + row, half, WS, row, 0) for row in range(rows)]
    spans += [(1, row, 0, WS, rows + row, 0) for row in range(rows)]
    shape = (row_count, col_count, width)
    done = finish(first, out_weights, [blocked, south_0], spans, (row_count, WS, width))
    second[0] = after(second[0], done)
    base = partial(second[:split], out_weights[:split])
    spans = [(0, rows + row, half + WS, near, row, WS) for row in range(rows)]
    spans += [(1, row, 0, near, rows + row, WS) for row in range(rows)]
    spans += [(2, row, 0, half, row, WS + near) for row in range(rows)]
    spans += [(3, row, 0, half, rows + row, WS + near) for row in range(rows)]
    mixed = finish_last(second[split:], out_weights[split:], base, done, [blocked, south_1, east, corner], spans, shape)
    return mixed[None, :, None]


def solution(mesh):
    in_specs = (
        P(("member", "win"), None, "seq", None, None),
        P(("member", "win"), None, None),
        P(),
        P(),
        P(None, None, "seq"),
        P("seq"),
        P("seq", None),
    )
    out_specs = P(("member", "win"), None, "seq", None, None)

    return jax.shard_map(on_device, mesh=mesh, in_specs=in_specs, out_specs=out_specs, check_vma=False)
```

```python
import functools
import math

import jax
import jax.numpy as jnp
from jax import lax
from jax.experimental import pallas as pl
from jax.experimental.pallas import tpu as pltpu
from jax.sharding import PartitionSpec as P


CHANNEL_PER_PART = 96
WS = 32
REGIONS = 32
LANE = 128
FAR = -1e30
F32 = jnp.float32
BF16 = jnp.bfloat16


def permute_by(value, axis, move):
    count = lax.axis_size(axis)
    pairs = [(source, move(source, count)) for source in range(count)]
    return lax.ppermute(value, axis, pairs)


def exchange(value, mask, axis="seq"):
    return permute_by(value, axis, lambda source, count: source ^ mask)


def masks_of(count):
    masks = []
    while count > 1:
        count //= 2
        masks.append(count)
    return masks


def gather_pieces(piece):
    pieces = {0: piece}
    for mask in masks_of(lax.axis_size("seq")):
        for offset in list(pieces):
            pieces[offset ^ mask] = exchange(pieces[offset], mask)
    return [pieces[offset] for offset in range(len(pieces))]


def padded(width):
    return (width + LANE - 1) // LANE * LANE


VMEM = pl.BlockSpec(memory_space=pltpu.VMEM)


def after(value, *earlier):
    return lax.optimization_barrier((value, *earlier))[0]


def normalized(held, gain, bias):
    values = held.astype(F32)
    average = jnp.mean(values, axis=-1, keepdims=True)
    centred = values - average
    variance = jnp.mean(centred * centred, axis=-1, keepdims=True)
    return (centred * lax.rsqrt(variance + 1e-05) * gain + bias).astype(BF16)


HELD = pl.BlockSpec(memory_space=pltpu.HBM)


def cut_kernel(boxes, pixel_ref, *outs):
    for (row, left, size), out_ref in zip(boxes, outs, strict=True):
        out_ref[...] = pixel_ref[row : row + out_ref.shape[0], left : left + size, :]


def cut(pixels, rows, boxes):
    width = pixels.shape[2]
    return pl.pallas_call(
        functools.partial(cut_kernel, boxes),
        out_shape=[jax.ShapeDtypeStruct((rows, size, width), BF16) for _, _, size in boxes],
        in_specs=[VMEM],
        out_specs=[VMEM] * len(boxes),
        compiler_params=pltpu.CompilerParams(vmem_limit_bytes=8 << 20),
        cost_estimate=pl.CostEstimate(flops=0, bytes_accessed=2 * pixels.size, transcendentals=0),
        name="cut",
    )(pixels)


def norm_kernel(groups, *refs):
    refs, outs = refs[: -len(groups)], refs[-len(groups) :]
    *sources, gain_ref, bias_ref = refs
    gain, bias = gain_ref[...][None], bias_ref[...][None]
    for spans, out_ref in zip(groups, outs, strict=True):
        into = 0
        for which, row, left, size in spans:
            held = sources[which][row, left : left + size, :]
            out_ref[into : into + size, :] = normalized(held, gain, bias)
            into += size


def norm(sources, gain, bias, groups):
    width = sources[0].shape[-1]
    totals = [sum(span[-1] for span in spans) for spans in groups]
    return pl.pallas_call(
        functools.partial(norm_kernel, groups),
        out_shape=[jax.ShapeDtypeStruct((total, width), BF16) for total in totals],
        in_specs=[VMEM] * (len(sources) + 2),
        out_specs=[VMEM] * len(groups),
        compiler_params=pltpu.CompilerParams(vmem_limit_bytes=8 << 20),
        cost_estimate=pl.CostEstimate(
            flops=10 * sum(totals) * width, bytes_accessed=4 * sum(totals) * width, transcendentals=0
        ),
    )(*sources, gain, bias)


def tag_kernel(count, near, label_ref, weight_ref, *outs):
    del weight_ref
    query_0, key_0, query_1, key_1 = outs
    row_count, _ = label_ref.shape
    rows = row_count // (2 * count)
    device = lax.axis_index("seq")
    turned = jnp.transpose(label_ref[...].astype(F32)).astype(BF16)
    place = lax.broadcasted_iota(jnp.int32, (row_count, LANE), 0)
    lane = (lax.broadcasted_iota(jnp.int32, (1, LANE), 1) % REGIONS).astype(F32)
    group = count * rows
    for half in range(2):
        for offset in range(count):
            for row in range(rows):
                at = (half * rows + row) * count + jnp.bitwise_xor(device, offset)
                chosen = jnp.where(place == at, 1.0, 0.0).astype(BF16)
                region = jnp.dot(turned, chosen, preferred_element_type=F32)
                same = region == lane
                query = jnp.where(same, 1.0, 0.0).astype(BF16)
                key = jnp.where(same, 0.0, FAR).astype(BF16)
                slot = offset * rows + row
                apart, span = group * near, near + 2 * (WS - near)
                beside = apart + offset * rows * span
                spots = [
                    (query_0, key_0, (half * group + slot) * WS, 0, WS),
                    (query_1, key_1, beside + row * near if half else slot * near, WS, near),
                    (
                        query_1,
                        key_1,
                        beside + rows * near + (half * rows + row) * (WS - near),
                        WS + near,
                        WS - near,
                    ),
                ]
                for query_ref, key_ref, into, left, size in spots:
                    query_ref[into : into + size, :] = query[left : left + size]
                    key_ref[into : into + size, :] = key[left : left + size]


def region_tags(labels, weights, count, near):
    pixels = labels.shape[0] * WS
    return pl.pallas_call(
        functools.partial(tag_kernel, count, near),
        out_shape=[jax.ShapeDtypeStruct((pixels, LANE), BF16)] * 4,
        in_specs=[VMEM] * 2,
        out_specs=[VMEM] * 4,
        compiler_params=pltpu.CompilerParams(vmem_limit_bytes=8 << 20),
        cost_estimate=pl.CostEstimate(
            flops=8 * pixels * LANE * labels.shape[0], bytes_accessed=8 * pixels * LANE, transcendentals=0
        ),
        name="tags",
    )(labels, weights)


def project_kernel(counts, *refs):
    groups = []
    for count in counts:
        groups.append(refs[:count])
        refs = refs[count:]
    weight_ref, *outs = refs
    block = jnp.concatenate([piece[...] for group in groups for piece in group], axis=0)
    head_width = weight_ref.shape[2]
    slot = padded(head_width)
    if slot == head_width:
        weights = jnp.concatenate([weight_ref[t] for t in range(3)], axis=1)
        products = [(0, jnp.dot(block, weights, preferred_element_type=F32).astype(BF16))]
    else:
        products = [
            (t * slot, jnp.dot(block, weight_ref[t], preferred_element_type=F32).astype(BF16))
            for t in range(3)
        ]
    at = 0
    for out_ref in outs:
        for left, product in products:
            part = product[at : at + out_ref.shape[0]]
            out_ref[:, left : left + part.shape[1]] = part
        at += out_ref.shape[0]


def project(groups, weights):
    width = groups[0][0].shape[1]
    slot = padded(weights.shape[2])
    sizes = [sum(piece.shape[0] for piece in group) for group in groups]
    total = sum(sizes)
    return pl.pallas_call(
        functools.partial(project_kernel, [len(group) for group in groups]),
        out_shape=[jax.ShapeDtypeStruct((size, 3 * slot), BF16) for size in sizes],
        in_specs=[VMEM] * (sum(len(group) for group in groups) + 1),
        out_specs=[VMEM] * len(groups),
        compiler_params=pltpu.CompilerParams(vmem_limit_bytes=24 << 20),
        cost_estimate=pl.CostEstimate(
            flops=2 * total * width * 3 * slot,
            bytes_accessed=2 * (total * width + weights.size + total * 3 * slot),
            transcendentals=0,
        ),
    )(*[piece for group in groups for piece in group], weights)


def attend_kernel(layout, ranges, head_width, *refs):
    parts = len(layout)
    blocks = refs[:parts]
    query_tags, key_tags, scale_ref = refs[parts : parts + 3]
    outs = refs[parts + 3 :]
    slot = padded(head_width)
    low, high = min(lo for lo, _ in ranges), max(hi for _, hi in ranges)
    heads = head_width // CHANNEL_PER_PART
    base = math.log2(math.e) / math.sqrt(CHANNEL_PER_PART)
    tiles = [None] * (slot // LANE)
    key_rows = key_tags[...]
    runs, query_rows, at = [], [], 0
    for block, (lo, hi) in zip(blocks, layout, strict=True):
        z = block.shape[0] // (hi - lo)
        first, last = max(low, lo), min(high, hi)
        if first < last:
            runs.append((block, (first - lo) * z, (last - lo) * z, z, first, last))
            query_rows.append(query_tags[at + (first - lo) * z : at + (last - lo) * z, :])
        at += block.shape[0]
    query_rows = jnp.concatenate(query_rows, axis=0)

    def span(head):
        first = head * CHANNEL_PER_PART
        last = first + CHANNEL_PER_PART
        left, right = first // LANE * LANE, padded(last)
        lane = lax.broadcasted_iota(jnp.int32, (1, right - left), 1)
        return left, right, (lane >= first - left) & (lane < last - left)

    def scores_of(head):
        left, right, inside = span(head)
        reps = (right - left) // LANE
        queries = jnp.concatenate([run[0][run[1] : run[2], left:right] for run in runs], axis=0)
        queries = jnp.where(inside, queries, jnp.concatenate([query_rows] * reps, axis=1))
        keys = jnp.concatenate([b[:, slot + left : slot + right] for b in blocks], axis=0)
        keys = jnp.where(inside, keys, jnp.concatenate([key_rows] * reps, axis=1))
        return lax.dot_general(queries, keys, (((1,), (1,)), ((), ())), preferred_element_type=F32)

    following = scores_of(0)
    for head in range(heads):
        scores = following
        if head + 1 < heads:
            following = scores_of(head + 1)
        left, right, inside = span(head)
        row_max = jnp.max(scores, axis=-1, keepdims=True)
        numerators = jnp.exp2((scores - row_max) * (scale_ref[head] * base))
        total = jnp.sum(numerators, axis=-1, keepdims=True)
        values = jnp.concatenate([b[:, 2 * slot + left : 2 * slot + right] for b in blocks], axis=0)
        mixed = jnp.dot(numerators.astype(BF16), values, preferred_element_type=F32) / total
        for i in range((right - left) // LANE):
            tile = left // LANE + i
            own = mixed[:, i * LANE : (i + 1) * LANE]
            held = tiles[tile]
            tiles[tile] = own if held is None else jnp.where(inside[:, i * LANE : (i + 1) * LANE], own, held)
    result = jnp.concatenate(tiles, axis=1)[:, :head_width].astype(BF16)
    places = {
        offset: (out_ref, offset - lo)
        for out_ref, (lo, hi) in zip(outs, ranges, strict=True)
        for offset in range(lo, hi)
    }
    into = dict.fromkeys(places, 0)
    at = 0
    for _, _, _, z, first, last in runs:
        for offset in range(first, last):
            out_ref, index = places[offset]
            out_ref[index, into[offset] : into[offset] + z, :] = result[at : at + z]
            into[offset] += z
            at += z


def attend(blocks, layout, query_tags, key_tags, scales, count, ranges, head_width):
    pixels = sum(block.shape[0] for block in blocks)
    per_offset = pixels // count
    asked = sum(hi - lo for lo, hi in ranges) * per_offset
    heads = head_width // CHANNEL_PER_PART
    return pl.pallas_call(
        functools.partial(attend_kernel, layout, ranges, head_width),
        out_shape=[
            jax.ShapeDtypeStruct((hi - lo, per_offset, head_width), BF16) for lo, hi in ranges
        ],
        in_specs=[VMEM] * (len(blocks) + 2) + [pl.BlockSpec(memory_space=pltpu.SMEM)],
        out_specs=[VMEM] * len(ranges),
        compiler_params=pltpu.CompilerParams(vmem_limit_bytes=28 << 20),
        cost_estimate=pl.CostEstimate(
            flops=4 * heads * asked * pixels * 2 * LANE,
            bytes_accessed=2 * pixels * 3 * padded(head_width),
            transcendentals=heads * asked * pixels,
        ),
    )(*blocks, query_tags, key_tags, scales)


def product(attended, weights, columns=slice(None)):
    total = None
    for piece, weight in zip(attended, weights, strict=True):
        term = jnp.dot(piece[...], weight[:, columns], preferred_element_type=F32)
        total = term if total is None else total + term
    return total


def partial_kernel(count, *refs):
    *refs, out_ref = refs
    out_ref[...] = product(refs[:count], refs[count:])


def partial(attended, weights):
    pixels, depth = attended[0].shape
    width = weights[0].shape[1]
    return pl.pallas_call(
        functools.partial(partial_kernel, len(weights)),
        out_shape=jax.ShapeDtypeStruct((pixels, width), F32),
        in_specs=[VMEM] * (2 * len(weights)),
        out_specs=VMEM,
        compiler_params=pltpu.CompilerParams(vmem_limit_bytes=20 << 20),
        cost_estimate=pl.CostEstimate(
            flops=2 * pixels * width * depth * len(weights), bytes_accessed=2 * width * (depth + 2 * pixels), transcendentals=0
        ),
    )(*attended, *weights)


def finish_kernel(count, spans, *refs):
    attended, weights, sources, out_ref = refs[:count], refs[count : 2 * count], refs[2 * count : -1], refs[-1]
    total = product(attended, weights)
    at = 0
    for which, row, start, pixels, into, column in spans:
        held = sources[which][row, start : start + pixels, :].astype(F32)
        out_ref[into, column : column + pixels, :] = (held + total[at : at + pixels]).astype(BF16)
        at += pixels


def finish(attended, weights, sources, spans, shape):
    count = len(weights)
    pixels, width = attended[0].shape[0], shape[-1]
    return pl.pallas_call(
        functools.partial(finish_kernel, count, spans),
        out_shape=jax.ShapeDtypeStruct(shape, BF16),
        in_specs=[VMEM] * (2 * count + len(sources)),
        out_specs=VMEM,
        compiler_params=pltpu.CompilerParams(vmem_limit_bytes=20 << 20),
        cost_estimate=pl.CostEstimate(
            flops=2 * pixels * width * width, bytes_accessed=2 * width * (width + 3 * pixels), transcendentals=0
        ),
    )(*attended, *weights, *sources)


def last_kernel(count, chunks, spans, *refs):
    attended, weights = refs[:count], refs[count : 2 * count]
    base_ref, done_ref, *sources, out_ref, ready, semaphore = refs[2 * count :]
    left, size, width = done_ref.shape[1], ready.shape[1], ready.shape[2]
    wide = width // chunks
    copies = [
        pltpu.make_async_copy(done_ref, out_ref.at[:, pl.ds(0, left), :], semaphore.at[chunks])
    ]
    copies[0].start()
    for chunk in range(chunks):
        columns = slice(chunk * wide, (chunk + 1) * wide)
        total = product(attended, weights, columns) + base_ref[:, columns]
        at = 0
        for which, row, start, pixels, into, column in spans:
            held = sources[which][row, start : start + pixels, columns].astype(F32)
            ready[into, column - left : column - left + pixels, columns] = (
                held + total[at : at + pixels]
            ).astype(BF16)
            at += pixels
        place = pl.ds(chunk * wide, wide)
        copy = pltpu.make_async_copy(
            ready.at[:, :, place], out_ref.at[:, pl.ds(left, size), place], semaphore.at[chunk]
        )
        copy.start()
        copies.append(copy)
    for copy in copies:
        copy.wait()


def finish_last(attended, weights, base, done, sources, spans, shape):
    count = len(weights)
    row_count, col_count, width = shape
    pixels, depth = attended[0].shape
    chunks = 3 if width % (3 * 2 * LANE) == 0 else 1
    return pl.pallas_call(
        functools.partial(last_kernel, count, chunks, spans),
        out_shape=jax.ShapeDtypeStruct(shape, BF16),
        in_specs=[VMEM] * (2 * count + 2 + len(sources)),
        out_specs=HELD,
        scratch_shapes=[
            pltpu.VMEM((row_count, col_count - done.shape[1], width), BF16),
            pltpu.SemaphoreType.DMA((chunks + 1,)),
        ],
        compiler_params=pltpu.CompilerParams(vmem_limit_bytes=20 << 20),
        cost_estimate=pl.CostEstimate(
            flops=2 * pixels * width * depth * count, bytes_accessed=2 * width * (width + 3 * pixels), transcendentals=0
        ),
    )(*attended, *weights, base, done, *sources)


def send_heads(outs):
    own = [outs[0]]
    for offset in range(1, len(outs)):
        own.append(exchange(outs[offset], offset))
    return [piece[0] for piece in own]


def pick_kernel(place, source_ref, out_ref, semaphore):
    size = out_ref.shape[0]
    start = pl.multiple_of(place() * size, 16)
    copy = pltpu.make_async_copy(source_ref.at[pl.ds(start, size), :], out_ref, semaphore)
    copy.start()
    copy.wait()


def join_kernel(place, own_ref, other_ref, out_ref):
    size = own_ref.shape[0]
    at = place()
    out_ref[pl.ds(pl.multiple_of(at * size, 16), size), :] = own_ref[...]
    out_ref[pl.ds(pl.multiple_of((1 - at) * size, 16), size), :] = other_ref[...]


def small_call(kernel, rows, *operands, spec=VMEM, scratch=()):
    width = operands[0].shape[1]
    return pl.pallas_call(
        kernel,
        out_shape=jax.ShapeDtypeStruct((rows, width), BF16),
        in_specs=[spec] * len(operands),
        out_specs=VMEM,
        scratch_shapes=scratch,
        compiler_params=pltpu.CompilerParams(vmem_limit_bytes=8 << 20),
        cost_estimate=pl.CostEstimate(flops=0, bytes_accessed=4 * rows * width, transcendentals=0),
    )(*operands)


def gather_weights(block):
    levels = []
    rows = block.shape[0]
    for axis in ("win", "member"):
        if lax.axis_size(axis) % 2 == 0 and rows % (32 << len(levels)) == 0:
            levels.append(axis)

    def bit(axis):
        return lax.axis_index(axis) & 1

    def part_index():
        index = 0
        for axis in levels:
            index = index * 2 + bit(axis)
        return index

    pieces = {0: block}
    for mask in masks_of(lax.axis_size("seq")):
        for offset in list(pieces):
            piece = pieces[offset]
            if mask > 1 and levels:
                size = rows >> len(levels)
                part = small_call(
                    functools.partial(pick_kernel, part_index),
                    size,
                    piece,
                    spec=HELD,
                    scratch=[pltpu.SemaphoreType.DMA],
                )
                part = exchange(part, mask)
                for axis in reversed(levels):
                    other = exchange(part, 1, axis)
                    size *= 2
                    part = small_call(functools.partial(join_kernel, functools.partial(bit, axis)), size, part, other)
                pieces[offset ^ mask] = part
            else:
                pieces[offset ^ mask] = exchange(piece, mask)
    return [pieces[offset] for offset in range(len(pieces))]


def on_device(
    pixel_grid_input,
    mask_zone_labeling,
    standardize_multiplier,
    standardize_offset_vector,
    triple_projection_matrix,
    logit_scaling_per_part,
    final_projection_matrix,
):
    count = lax.axis_size("seq")
    blocked = pixel_grid_input[0, :, 0]
    row_count, col_count, width = blocked.shape
    rows = row_count // 2
    half = WS // 2
    head_width = triple_projection_matrix.shape[2]

    def west(source, count):
        return (source - 2) % count

    def west_north(source, count):
        return ((source ^ 1) - 2) % count

    near = WS - half
    gain, bias = standardize_multiplier, standardize_offset_vector
    weights = triple_projection_matrix
    scales = logit_scaling_per_part

    boxes = [
        (rows, half, WS),
        (rows, half + WS, near),
        (0, half, WS),
        (0, half + WS, near),
        (rows, 0, half),
        (0, 0, half),
    ]
    local_0, local_1, south_0, south_1, east, corner = cut(blocked, rows, boxes)
    south_0 = exchange(south_0, 1, "win")
    south_1 = exchange(south_1, 1, "win")
    east = permute_by(east, "win", west)
    corner = permute_by(corner, "win", west_north)
    local_0_pieces = gather_pieces(local_0)
    local_1_pieces = gather_pieces(local_1)
    query_0, key_0, query_1, key_1 = region_tags(mask_zone_labeling[0], weights, count, near)
    out_weights = gather_weights(final_projection_matrix)

    spans = [(0, row, 0, WS) for row in range(rows)]
    (south_normed,) = norm([south_0], gain, bias, [spans])
    south_pieces = gather_pieces(south_normed)
    spans = [(piece, row, 0, WS) for piece in range(count) for row in range(rows)]
    (local_0_normed,) = norm(local_0_pieces, gain, bias, [spans])
    (local_0,) = project([[local_0_normed]], weights)
    spans = [(0, row, 0, near) for row in range(rows)]
    spans += [(which, row, 0, half) for which in (1, 2) for row in range(rows)]
    (rest_normed,) = norm([south_1, east, corner], gain, bias, [spans])
    rest_pieces = gather_pieces(rest_normed)
    split = count // 2
    near_lanes, far_lanes, all_lanes = (0, split), (split, count), (0, count)
    spans = [(piece, row, 0, near) for piece in range(count) for row in range(rows)]
    (local_1_normed,) = norm(local_1_pieces, gain, bias, [spans])
    south_near, local_1 = project([south_pieces[:split], [local_1_normed]], weights)
    south_pieces[split] = after(south_pieces[split], south_near)
    (south_far,) = project([south_pieces[split:]], weights)
    (rest_near,) = project([rest_pieces[:split]], weights)

    def attend_run(blocks, layout, tags, earlier, lo, hi):
        blocks = [after(blocks[0], *earlier), *blocks[1:]]
        singles = [(i, i + 1) for i in range(lo, hi)]
        return list(attend(blocks, layout, *tags, scales, count, singles, head_width))

    blocks, layout, tags = [local_0, south_near, south_far], [all_lanes, near_lanes, far_lanes], (query_0, key_0)
    outs_0 = attend_run(blocks, layout, tags, [], 0, count)
    rest_pieces[split] = after(rest_pieces[split], *outs_0)
    (rest_far,) = project([rest_pieces[split:]], weights)
    blocks, layout, tags = [local_1, rest_near, rest_far], [all_lanes, near_lanes, far_lanes], (query_1, key_1)
    far = attend_run(blocks, layout, tags, [], split, count)
    close = attend_run(blocks, layout, tags, far, 0, split)
    outs_1 = close + far

    first = send_heads(outs_0)
    second = send_heads(outs_1)
    first[0] = after(first[0], *outs_1)
    spans = [(0, rows + row, half, WS, row, 0) for row in range(rows)]
    spans += [(1, row, 0, WS, rows + row, 0) for row in range(rows)]
    shape = (row_count, col_count, width)
    done = finish(first, out_weights, [blocked, south_0], spans, (row_count, WS, width))
    second[0] = after(second[0], done)
    base = partial(second[:split], out_weights[:split])
    spans = [(0, rows + row, half + WS, near, row, WS) for row in range(rows)]
    spans += [(1, row, 0, near, rows + row, WS) for row in range(rows)]
    spans += [(2, row, 0, half, row, WS + near) for row in range(rows)]
    spans += [(3, row, 0, half, rows + row, WS + near) for row in range(rows)]
    mixed = finish_last(second[split:], out_weights[split:], base, done, [blocked, south_1, east, corner], spans, shape)
    return mixed[None, :, None]


def solution(mesh):
    in_specs = (
        P(("member", "win"), None, "seq", None, None),
        P(("member", "win"), None, None),
        P(),
        P(),
        P(None, None, "seq"),
        P("seq"),
        P("seq", None),
    )
    out_specs = P(("member", "win"), None, "seq", None, None)

    return jax.shard_map(on_device, mesh=mesh, in_specs=in_specs, out_specs=out_specs, check_vma=False)
```

```python
import functools
import math

import jax
import jax.numpy as jnp
from jax import lax
from jax.experimental import pallas as pl
from jax.experimental.pallas import tpu as pltpu
from jax.sharding import PartitionSpec as P


CHANNEL_PER_PART = 96
WS = 32
REGIONS = 32
LANE = 128
FAR = -1e30
F32 = jnp.float32
BF16 = jnp.bfloat16


def permute_by(value, axis, move):
    count = lax.axis_size(axis)
    pairs = [(source, move(source, count)) for source in range(count)]
    return lax.ppermute(value, axis, pairs)


def exchange(value, mask, axis="seq"):
    return permute_by(value, axis, lambda source, count: source ^ mask)


def masks_of(count):
    masks = []
    while count > 1:
        count //= 2
        masks.append(count)
    return masks


def gather_pieces(piece):
    pieces = {0: piece}
    for mask in masks_of(lax.axis_size("seq")):
        for offset in list(pieces):
            pieces[offset ^ mask] = exchange(pieces[offset], mask)
    return [pieces[offset] for offset in range(len(pieces))]


def padded(width):
    return (width + LANE - 1) // LANE * LANE


VMEM = pl.BlockSpec(memory_space=pltpu.VMEM)


def after(value, *earlier):
    return lax.optimization_barrier((value, *earlier))[0]


def normalized(held, gain, bias):
    values = held.astype(F32)
    average = jnp.mean(values, axis=-1, keepdims=True)
    centred = values - average
    variance = jnp.mean(centred * centred, axis=-1, keepdims=True)
    return (centred * lax.rsqrt(variance + 1e-05) * gain + bias).astype(BF16)


HELD = pl.BlockSpec(memory_space=pltpu.HBM)


def cut_kernel(boxes, pixel_ref, *outs):
    for (row, left, size), out_ref in zip(boxes, outs, strict=True):
        out_ref[...] = pixel_ref[row : row + out_ref.shape[0], left : left + size, :]


def cut(pixels, rows, boxes):
    width = pixels.shape[2]
    return pl.pallas_call(
        functools.partial(cut_kernel, boxes),
        out_shape=[jax.ShapeDtypeStruct((rows, size, width), BF16) for _, _, size in boxes],
        in_specs=[VMEM],
        out_specs=[VMEM] * len(boxes),
        compiler_params=pltpu.CompilerParams(vmem_limit_bytes=8 << 20),
        cost_estimate=pl.CostEstimate(flops=0, bytes_accessed=2 * pixels.size, transcendentals=0),
        name="cut",
    )(pixels)


def norm_kernel(groups, *refs):
    refs, outs = refs[: -len(groups)], refs[-len(groups) :]
    *sources, gain_ref, bias_ref = refs
    gain, bias = gain_ref[...][None], bias_ref[...][None]
    for spans, out_ref in zip(groups, outs, strict=True):
        into = 0
        for which, row, left, size in spans:
            held = sources[which][row, left : left + size, :]
            out_ref[into : into + size, :] = normalized(held, gain, bias)
            into += size


def norm(sources, gain, bias, groups):
    width = sources[0].shape[-1]
    totals = [sum(span[-1] for span in spans) for spans in groups]
    return pl.pallas_call(
        functools.partial(norm_kernel, groups),
        out_shape=[jax.ShapeDtypeStruct((total, width), BF16) for total in totals],
        in_specs=[VMEM] * (len(sources) + 2),
        out_specs=[VMEM] * len(groups),
        compiler_params=pltpu.CompilerParams(vmem_limit_bytes=8 << 20),
        cost_estimate=pl.CostEstimate(
            flops=10 * sum(totals) * width, bytes_accessed=4 * sum(totals) * width, transcendentals=0
        ),
    )(*sources, gain, bias)


def tag_kernel(count, near, label_ref, weight_ref, *outs):
    del weight_ref
    query_0, key_0, query_1, key_1 = outs
    row_count, _ = label_ref.shape
    rows = row_count // (2 * count)
    device = lax.axis_index("seq")
    turned = jnp.transpose(label_ref[...].astype(F32)).astype(BF16)
    place = lax.broadcasted_iota(jnp.int32, (row_count, LANE), 0)
    lane = (lax.broadcasted_iota(jnp.int32, (1, LANE), 1) % REGIONS).astype(F32)
    group = count * rows
    for half in range(2):
        for offset in range(count):
            for row in range(rows):
                at = (half * rows + row) * count + jnp.bitwise_xor(device, offset)
                chosen = jnp.where(place == at, 1.0, 0.0).astype(BF16)
                region = jnp.dot(turned, chosen, preferred_element_type=F32)
                same = region == lane
                query = jnp.where(same, 1.0, 0.0).astype(BF16)
                key = jnp.where(same, 0.0, FAR).astype(BF16)
                slot = offset * rows + row
                apart, span = group * near, near + 2 * (WS - near)
                beside = apart + offset * rows * span
                spots = [
                    (query_0, key_0, (half * group + slot) * WS, 0, WS),
                    (query_1, key_1, beside + row * near if half else slot * near, WS, near),
                    (
                        query_1,
                        key_1,
                        beside + rows * near + (half * rows + row) * (WS - near),
                        WS + near,
                        WS - near,
                    ),
                ]
                for query_ref, key_ref, into, left, size in spots:
                    query_ref[into : into + size, :] = query[left : left + size]
                    key_ref[into : into + size, :] = key[left : left + size]


def region_tags(labels, weights, count, near):
    pixels = labels.shape[0] * WS
    return pl.pallas_call(
        functools.partial(tag_kernel, count, near),
        out_shape=[jax.ShapeDtypeStruct((pixels, LANE), BF16)] * 4,
        in_specs=[VMEM] * 2,
        out_specs=[VMEM] * 4,
        compiler_params=pltpu.CompilerParams(vmem_limit_bytes=8 << 20),
        cost_estimate=pl.CostEstimate(
            flops=8 * pixels * LANE * labels.shape[0], bytes_accessed=8 * pixels * LANE, transcendentals=0
        ),
        name="tags",
    )(labels, weights)


def project_kernel(counts, *refs):
    groups = []
    for count in counts:
        groups.append(refs[:count])
        refs = refs[count:]
    weight_ref, *outs = refs
    block = jnp.concatenate([piece[...] for group in groups for piece in group], axis=0)
    head_width = weight_ref.shape[2]
    slot = padded(head_width)
    if slot == head_width:
        weights = jnp.concatenate([weight_ref[t] for t in range(3)], axis=1)
        products = [(0, jnp.dot(block, weights, preferred_element_type=F32).astype(BF16))]
    else:
        products = [
            (t * slot, jnp.dot(block, weight_ref[t], preferred_element_type=F32).astype(BF16))
            for t in range(3)
        ]
    at = 0
    for out_ref in outs:
        for left, product in products:
            part = product[at : at + out_ref.shape[0]]
            out_ref[:, left : left + part.shape[1]] = part
        at += out_ref.shape[0]


def project(groups, weights):
    width = groups[0][0].shape[1]
    slot = padded(weights.shape[2])
    sizes = [sum(piece.shape[0] for piece in group) for group in groups]
    total = sum(sizes)
    return pl.pallas_call(
        functools.partial(project_kernel, [len(group) for group in groups]),
        out_shape=[jax.ShapeDtypeStruct((size, 3 * slot), BF16) for size in sizes],
        in_specs=[VMEM] * (sum(len(group) for group in groups) + 1),
        out_specs=[VMEM] * len(groups),
        compiler_params=pltpu.CompilerParams(vmem_limit_bytes=24 << 20),
        cost_estimate=pl.CostEstimate(
            flops=2 * total * width * 3 * slot,
            bytes_accessed=2 * (total * width + weights.size + total * 3 * slot),
            transcendentals=0,
        ),
    )(*[piece for group in groups for piece in group], weights)


def attend_kernel(layout, ranges, head_width, *refs):
    parts = len(layout)
    blocks = refs[:parts]
    query_tags, key_tags, scale_ref = refs[parts : parts + 3]
    outs = refs[parts + 3 :]
    slot = padded(head_width)
    low, high = min(lo for lo, _ in ranges), max(hi for _, hi in ranges)
    heads = head_width // CHANNEL_PER_PART
    base = math.log2(math.e) / math.sqrt(CHANNEL_PER_PART)
    tiles = [None] * (slot // LANE)
    key_rows = key_tags[...]
    runs, query_rows, at = [], [], 0
    for block, (lo, hi) in zip(blocks, layout, strict=True):
        z = block.shape[0] // (hi - lo)
        first, last = max(low, lo), min(high, hi)
        if first < last:
            runs.append((block, (first - lo) * z, (last - lo) * z, z, first, last))
            query_rows.append(query_tags[at + (first - lo) * z : at + (last - lo) * z, :])
        at += block.shape[0]
    query_rows = jnp.concatenate(query_rows, axis=0)

    def span(head):
        first = head * CHANNEL_PER_PART
        last = first + CHANNEL_PER_PART
        left, right = first // LANE * LANE, padded(last)
        lane = lax.broadcasted_iota(jnp.int32, (1, right - left), 1)
        return left, right, (lane >= first - left) & (lane < last - left)

    def scores_of(head):
        left, right, inside = span(head)
        reps = (right - left) // LANE
        queries = jnp.concatenate([run[0][run[1] : run[2], left:right] for run in runs], axis=0)
        queries = jnp.where(inside, queries, jnp.concatenate([query_rows] * reps, axis=1))
        keys = jnp.concatenate([b[:, slot + left : slot + right] for b in blocks], axis=0)
        keys = jnp.where(inside, keys, jnp.concatenate([key_rows] * reps, axis=1))
        return lax.dot_general(queries, keys, (((1,), (1,)), ((), ())), preferred_element_type=F32)

    following = scores_of(0)
    for head in range(heads):
        scores = following
        if head + 1 < heads:
            following = scores_of(head + 1)
        left, right, inside = span(head)
        row_max = jnp.max(scores, axis=-1, keepdims=True)
        numerators = jnp.exp2((scores - row_max) * (scale_ref[head] * base))
        total = jnp.sum(numerators, axis=-1, keepdims=True)
        values = jnp.concatenate([b[:, 2 * slot + left : 2 * slot + right] for b in blocks], axis=0)
        mixed = jnp.dot(numerators.astype(BF16), values, preferred_element_type=F32) / total
        for i in range((right - left) // LANE):
            tile = left // LANE + i
            own = mixed[:, i * LANE : (i + 1) * LANE]
            held = tiles[tile]
            tiles[tile] = own if held is None else jnp.where(inside[:, i * LANE : (i + 1) * LANE], own, held)
    result = jnp.concatenate(tiles, axis=1)[:, :head_width].astype(BF16)
    places = {
        offset: (out_ref, offset - lo)
        for out_ref, (lo, hi) in zip(outs, ranges, strict=True)
        for offset in range(lo, hi)
    }
    into = dict.fromkeys(places, 0)
    at = 0
    for _, _, _, z, first, last in runs:
        for offset in range(first, last):
            out_ref, index = places[offset]
            out_ref[index, into[offset] : into[offset] + z, :] = result[at : at + z]
            into[offset] += z
            at += z


def attend(blocks, layout, query_tags, key_tags, scales, count, ranges, head_width):
    pixels = sum(block.shape[0] for block in blocks)
    per_offset = pixels // count
    asked = sum(hi - lo for lo, hi in ranges) * per_offset
    heads = head_width // CHANNEL_PER_PART
    return pl.pallas_call(
        functools.partial(attend_kernel, layout, ranges, head_width),
        out_shape=[
            jax.ShapeDtypeStruct((hi - lo, per_offset, head_width), BF16) for lo, hi in ranges
        ],
        in_specs=[VMEM] * (len(blocks) + 2) + [pl.BlockSpec(memory_space=pltpu.SMEM)],
        out_specs=[VMEM] * len(ranges),
        compiler_params=pltpu.CompilerParams(vmem_limit_bytes=28 << 20),
        cost_estimate=pl.CostEstimate(
            flops=4 * heads * asked * pixels * 2 * LANE,
            bytes_accessed=2 * pixels * 3 * padded(head_width),
            transcendentals=heads * asked * pixels,
        ),
    )(*blocks, query_tags, key_tags, scales)


def product(attended, weights, columns=slice(None)):
    rows = jnp.concatenate([piece[...] for piece in attended], axis=1)
    depth = jnp.concatenate([weight[:, columns] for weight in weights], axis=0)
    return jnp.dot(rows, depth, preferred_element_type=F32)


def partial_kernel(count, *refs):
    *refs, out_ref = refs
    out_ref[...] = product(refs[:count], refs[count:])


def partial(attended, weights):
    pixels, depth = attended[0].shape
    width = weights[0].shape[1]
    return pl.pallas_call(
        functools.partial(partial_kernel, len(weights)),
        out_shape=jax.ShapeDtypeStruct((pixels, width), F32),
        in_specs=[VMEM] * (2 * len(weights)),
        out_specs=VMEM,
        compiler_params=pltpu.CompilerParams(vmem_limit_bytes=20 << 20),
        cost_estimate=pl.CostEstimate(
            flops=2 * pixels * width * depth * len(weights), bytes_accessed=2 * width * (depth + 2 * pixels), transcendentals=0
        ),
    )(*attended, *weights)


def finish_kernel(count, spans, *refs):
    attended, weights, sources, out_ref = refs[:count], refs[count : 2 * count], refs[2 * count : -1], refs[-1]
    total = product(attended, weights)
    at = 0
    for which, row, start, pixels, into, column in spans:
        held = sources[which][row, start : start + pixels, :].astype(F32)
        out_ref[into, column : column + pixels, :] = (held + total[at : at + pixels]).astype(BF16)
        at += pixels


def finish(attended, weights, sources, spans, shape):
    count = len(weights)
    pixels, width = attended[0].shape[0], shape[-1]
    return pl.pallas_call(
        functools.partial(finish_kernel, count, spans),
        out_shape=jax.ShapeDtypeStruct(shape, BF16),
        in_specs=[VMEM] * (2 * count + len(sources)),
        out_specs=VMEM,
        compiler_params=pltpu.CompilerParams(vmem_limit_bytes=20 << 20),
        cost_estimate=pl.CostEstimate(
            flops=2 * pixels * width * width, bytes_accessed=2 * width * (width + 3 * pixels), transcendentals=0
        ),
    )(*attended, *weights, *sources)


def last_kernel(count, chunks, spans, *refs):
    attended, weights = refs[:count], refs[count : 2 * count]
    base_ref, done_ref, *sources, out_ref, ready, semaphore = refs[2 * count :]
    left, size, width = done_ref.shape[1], ready.shape[1], ready.shape[2]
    wide = width // chunks
    copies = [
        pltpu.make_async_copy(done_ref, out_ref.at[:, pl.ds(0, left), :], semaphore.at[chunks])
    ]
    copies[0].start()
    for chunk in range(chunks):
        columns = slice(chunk * wide, (chunk + 1) * wide)
        total = product(attended, weights, columns) + base_ref[:, columns]
        at = 0
        for which, row, start, pixels, into, column in spans:
            held = sources[which][row, start : start + pixels, columns].astype(F32)
            ready[into, column - left : column - left + pixels, columns] = (
                held + total[at : at + pixels]
            ).astype(BF16)
            at += pixels
        place = pl.ds(chunk * wide, wide)
        copy = pltpu.make_async_copy(
            ready.at[:, :, place], out_ref.at[:, pl.ds(left, size), place], semaphore.at[chunk]
        )
        copy.start()
        copies.append(copy)
    for copy in copies:
        copy.wait()


def finish_last(attended, weights, base, done, sources, spans, shape):
    count = len(weights)
    row_count, col_count, width = shape
    pixels, depth = attended[0].shape
    chunks = 3 if width % (3 * 2 * LANE) == 0 else 1
    return pl.pallas_call(
        functools.partial(last_kernel, count, chunks, spans),
        out_shape=jax.ShapeDtypeStruct(shape, BF16),
        in_specs=[VMEM] * (2 * count + 2 + len(sources)),
        out_specs=HELD,
        scratch_shapes=[
            pltpu.VMEM((row_count, col_count - done.shape[1], width), BF16),
            pltpu.SemaphoreType.DMA((chunks + 1,)),
        ],
        compiler_params=pltpu.CompilerParams(vmem_limit_bytes=20 << 20),
        cost_estimate=pl.CostEstimate(
            flops=2 * pixels * width * depth * count, bytes_accessed=2 * width * (width + 3 * pixels), transcendentals=0
        ),
    )(*attended, *weights, base, done, *sources)


def send_heads(outs):
    own = [outs[0]]
    for offset in range(1, len(outs)):
        own.append(exchange(outs[offset], offset))
    return [piece[0] for piece in own]


def pick_kernel(place, source_ref, out_ref, semaphore):
    size = out_ref.shape[0]
    start = pl.multiple_of(place() * size, 16)
    copy = pltpu.make_async_copy(source_ref.at[pl.ds(start, size), :], out_ref, semaphore)
    copy.start()
    copy.wait()


def join_kernel(place, own_ref, other_ref, out_ref):
    size = own_ref.shape[0]
    at = place()
    out_ref[pl.ds(pl.multiple_of(at * size, 16), size), :] = own_ref[...]
    out_ref[pl.ds(pl.multiple_of((1 - at) * size, 16), size), :] = other_ref[...]


def small_call(kernel, rows, *operands, spec=VMEM, scratch=()):
    width = operands[0].shape[1]
    return pl.pallas_call(
        kernel,
        out_shape=jax.ShapeDtypeStruct((rows, width), BF16),
        in_specs=[spec] * len(operands),
        out_specs=VMEM,
        scratch_shapes=scratch,
        compiler_params=pltpu.CompilerParams(vmem_limit_bytes=8 << 20),
        cost_estimate=pl.CostEstimate(flops=0, bytes_accessed=4 * rows * width, transcendentals=0),
    )(*operands)


def gather_weights(block):
    levels = []
    rows = block.shape[0]
    for axis in ("win", "member"):
        if lax.axis_size(axis) % 2 == 0 and rows % (32 << len(levels)) == 0:
            levels.append(axis)

    def bit(axis):
        return lax.axis_index(axis) & 1

    def part_index():
        index = 0
        for axis in levels:
            index = index * 2 + bit(axis)
        return index

    pieces = {0: block}
    for mask in masks_of(lax.axis_size("seq")):
        for offset in list(pieces):
            piece = pieces[offset]
            if mask > 1 and levels:
                size = rows >> len(levels)
                part = small_call(
                    functools.partial(pick_kernel, part_index),
                    size,
                    piece,
                    spec=HELD,
                    scratch=[pltpu.SemaphoreType.DMA],
                )
                part = exchange(part, mask)
                for axis in reversed(levels):
                    other = exchange(part, 1, axis)
                    size *= 2
                    part = small_call(functools.partial(join_kernel, functools.partial(bit, axis)), size, part, other)
                pieces[offset ^ mask] = part
            else:
                pieces[offset ^ mask] = exchange(piece, mask)
    return [pieces[offset] for offset in range(len(pieces))]


def on_device(
    pixel_grid_input,
    mask_zone_labeling,
    standardize_multiplier,
    standardize_offset_vector,
    triple_projection_matrix,
    logit_scaling_per_part,
    final_projection_matrix,
):
    count = lax.axis_size("seq")
    blocked = pixel_grid_input[0, :, 0]
    row_count, col_count, width = blocked.shape
    rows = row_count // 2
    half = WS // 2
    head_width = triple_projection_matrix.shape[2]

    def west(source, count):
        return (source - 2) % count

    def west_north(source, count):
        return ((source ^ 1) - 2) % count

    near = WS - half
    gain, bias = standardize_multiplier, standardize_offset_vector
    weights = triple_projection_matrix
    scales = logit_scaling_per_part

    boxes = [
        (rows, half, WS),
        (rows, half + WS, near),
        (0, half, WS),
        (0, half + WS, near),
        (rows, 0, half),
        (0, 0, half),
    ]
    local_0, local_1, south_0, south_1, east, corner = cut(blocked, rows, boxes)
    south_0 = exchange(south_0, 1, "win")
    south_1 = exchange(south_1, 1, "win")
    east = permute_by(east, "win", west)
    corner = permute_by(corner, "win", west_north)
    local_0_pieces = gather_pieces(local_0)
    local_1_pieces = gather_pieces(local_1)
    query_0, key_0, query_1, key_1 = region_tags(mask_zone_labeling[0], weights, count, near)
    out_weights = gather_weights(final_projection_matrix)

    spans = [(0, row, 0, WS) for row in range(rows)]
    (south_normed,) = norm([south_0], gain, bias, [spans])
    south_pieces = gather_pieces(south_normed)
    spans = [(piece, row, 0, WS) for piece in range(count) for row in range(rows)]
    (local_0_normed,) = norm(local_0_pieces, gain, bias, [spans])
    (local_0,) = project([[local_0_normed]], weights)
    spans = [(0, row, 0, near) for row in range(rows)]
    spans += [(which, row, 0, half) for which in (1, 2) for row in range(rows)]
    (rest_normed,) = norm([south_1, east, corner], gain, bias, [spans])
    rest_pieces = gather_pieces(rest_normed)
    split = count // 2
    near_lanes, far_lanes, all_lanes = (0, split), (split, count), (0, count)
    spans = [(piece, row, 0, near) for piece in range(count) for row in range(rows)]
    (local_1_normed,) = norm(local_1_pieces, gain, bias, [spans])
    south_near, local_1 = project([south_pieces[:split], [local_1_normed]], weights)
    south_pieces[split] = after(south_pieces[split], south_near)
    (south_far,) = project([south_pieces[split:]], weights)
    (rest_near,) = project([rest_pieces[:split]], weights)

    def attend_run(blocks, layout, tags, earlier, lo, hi):
        blocks = [after(blocks[0], *earlier), *blocks[1:]]
        singles = [(i, i + 1) for i in range(lo, hi)]
        return list(attend(blocks, layout, *tags, scales, count, singles, head_width))

    blocks, layout, tags = [local_0, south_near, south_far], [all_lanes, near_lanes, far_lanes], (query_0, key_0)
    outs_0 = attend_run(blocks, layout, tags, [], 0, count)
    rest_pieces[split] = after(rest_pieces[split], *outs_0)
    (rest_far,) = project([rest_pieces[split:]], weights)
    blocks, layout, tags = [local_1, rest_near, rest_far], [all_lanes, near_lanes, far_lanes], (query_1, key_1)
    far = attend_run(blocks, layout, tags, [], split, count)
    close = attend_run(blocks, layout, tags, far, 0, split)
    outs_1 = close + far

    first = send_heads(outs_0)
    second = send_heads(outs_1)
    first[0] = after(first[0], *outs_1)
    spans = [(0, rows + row, half, WS, row, 0) for row in range(rows)]
    spans += [(1, row, 0, WS, rows + row, 0) for row in range(rows)]
    shape = (row_count, col_count, width)
    done = finish(first, out_weights, [blocked, south_0], spans, (row_count, WS, width))
    second[0] = after(second[0], done)
    base = partial(second[:-1], out_weights[:-1])
    spans = [(0, rows + row, half + WS, near, row, WS) for row in range(rows)]
    spans += [(1, row, 0, near, rows + row, WS) for row in range(rows)]
    spans += [(2, row, 0, half, row, WS + near) for row in range(rows)]
    spans += [(3, row, 0, half, rows + row, WS + near) for row in range(rows)]
    mixed = finish_last(second[-1:], out_weights[-1:], base, done, [blocked, south_1, east, corner], spans, shape)
    return mixed[None, :, None]


def solution(mesh):
    in_specs = (
        P(("member", "win"), None, "seq", None, None),
        P(("member", "win"), None, None),
        P(),
        P(),
        P(None, None, "seq"),
        P("seq"),
        P("seq", None),
    )
    out_specs = P(("member", "win"), None, "seq", None, None)

    return jax.shard_map(on_device, mesh=mesh, in_specs=in_specs, out_specs=out_specs, check_vma=False)
```

```python
import functools
import math

import jax
import jax.numpy as jnp
from jax import lax
from jax.experimental import pallas as pl
from jax.experimental.pallas import tpu as pltpu
from jax.sharding import PartitionSpec as P


CHANNEL_PER_PART = 96
WS = 32
REGIONS = 32
LANE = 128
FAR = -1e30
F32 = jnp.float32
BF16 = jnp.bfloat16


def permute_by(value, axis, move):
    count = lax.axis_size(axis)
    pairs = [(source, move(source, count)) for source in range(count)]
    return lax.ppermute(value, axis, pairs)


def exchange(value, mask, axis="seq"):
    return permute_by(value, axis, lambda source, count: source ^ mask)


def masks_of(count):
    masks = []
    while count > 1:
        count //= 2
        masks.append(count)
    return masks


def gather_pieces(piece):
    pieces = {0: piece}
    for mask in masks_of(lax.axis_size("seq")):
        for offset in list(pieces):
            pieces[offset ^ mask] = exchange(pieces[offset], mask)
    return [pieces[offset] for offset in range(len(pieces))]


def padded(width):
    return (width + LANE - 1) // LANE * LANE


VMEM = pl.BlockSpec(memory_space=pltpu.VMEM)


def after(value, *earlier):
    return lax.optimization_barrier((value, *earlier))[0]


def normalized(held, gain, bias):
    values = held.astype(F32)
    average = jnp.mean(values, axis=-1, keepdims=True)
    centred = values - average
    variance = jnp.mean(centred * centred, axis=-1, keepdims=True)
    return (centred * lax.rsqrt(variance + 1e-05) * gain + bias).astype(BF16)


HELD = pl.BlockSpec(memory_space=pltpu.HBM)


def cut_kernel(boxes, pixel_ref, *outs):
    for (row, left, size), out_ref in zip(boxes, outs, strict=True):
        out_ref[...] = pixel_ref[row : row + out_ref.shape[0], left : left + size, :]


def cut(pixels, rows, boxes):
    width = pixels.shape[2]
    return pl.pallas_call(
        functools.partial(cut_kernel, boxes),
        out_shape=[jax.ShapeDtypeStruct((rows, size, width), BF16) for _, _, size in boxes],
        in_specs=[VMEM],
        out_specs=[VMEM] * len(boxes),
        compiler_params=pltpu.CompilerParams(vmem_limit_bytes=8 << 20),
        cost_estimate=pl.CostEstimate(flops=0, bytes_accessed=2 * pixels.size, transcendentals=0),
        name="cut",
    )(pixels)


def norm_kernel(groups, *refs):
    refs, outs = refs[: -len(groups)], refs[-len(groups) :]
    *sources, gain_ref, bias_ref = refs
    gain, bias = gain_ref[...][None], bias_ref[...][None]
    for spans, out_ref in zip(groups, outs, strict=True):
        into = 0
        for which, row, left, size in spans:
            held = sources[which][row, left : left + size, :]
            out_ref[into : into + size, :] = normalized(held, gain, bias)
            into += size


def norm(sources, gain, bias, groups):
    width = sources[0].shape[-1]
    totals = [sum(span[-1] for span in spans) for spans in groups]
    return pl.pallas_call(
        functools.partial(norm_kernel, groups),
        out_shape=[jax.ShapeDtypeStruct((total, width), BF16) for total in totals],
        in_specs=[VMEM] * (len(sources) + 2),
        out_specs=[VMEM] * len(groups),
        compiler_params=pltpu.CompilerParams(vmem_limit_bytes=8 << 20),
        cost_estimate=pl.CostEstimate(
            flops=10 * sum(totals) * width, bytes_accessed=4 * sum(totals) * width, transcendentals=0
        ),
    )(*sources, gain, bias)


def tag_kernel(count, near, label_ref, weight_ref, *outs):
    del weight_ref
    query_0, key_0, query_1, key_1 = outs
    row_count, _ = label_ref.shape
    rows = row_count // (2 * count)
    device = lax.axis_index("seq")
    turned = jnp.transpose(label_ref[...].astype(F32)).astype(BF16)
    place = lax.broadcasted_iota(jnp.int32, (row_count, LANE), 0)
    lane = (lax.broadcasted_iota(jnp.int32, (1, LANE), 1) % REGIONS).astype(F32)
    group = count * rows
    for half in range(2):
        for offset in range(count):
            for row in range(rows):
                at = (half * rows + row) * count + jnp.bitwise_xor(device, offset)
                chosen = jnp.where(place == at, 1.0, 0.0).astype(BF16)
                region = jnp.dot(turned, chosen, preferred_element_type=F32)
                same = region == lane
                query = jnp.where(same, 1.0, 0.0).astype(BF16)
                key = jnp.where(same, 0.0, FAR).astype(BF16)
                slot = offset * rows + row
                apart, span = group * near, near + 2 * (WS - near)
                beside = apart + offset * rows * span
                spots = [
                    (query_0, key_0, (half * group + slot) * WS, 0, WS),
                    (query_1, key_1, beside + row * near if half else slot * near, WS, near),
                    (
                        query_1,
                        key_1,
                        beside + rows * near + (half * rows + row) * (WS - near),
                        WS + near,
                        WS - near,
                    ),
                ]
                for query_ref, key_ref, into, left, size in spots:
                    query_ref[into : into + size, :] = query[left : left + size]
                    key_ref[into : into + size, :] = key[left : left + size]


def region_tags(labels, weights, count, near):
    pixels = labels.shape[0] * WS
    return pl.pallas_call(
        functools.partial(tag_kernel, count, near),
        out_shape=[jax.ShapeDtypeStruct((pixels, LANE), BF16)] * 4,
        in_specs=[VMEM] * 2,
        out_specs=[VMEM] * 4,
        compiler_params=pltpu.CompilerParams(vmem_limit_bytes=8 << 20),
        cost_estimate=pl.CostEstimate(
            flops=8 * pixels * LANE * labels.shape[0], bytes_accessed=8 * pixels * LANE, transcendentals=0
        ),
        name="tags",
    )(labels, weights)


def project_kernel(counts, *refs):
    groups = []
    for count in counts:
        groups.append(refs[:count])
        refs = refs[count:]
    weight_ref, *outs = refs
    block = jnp.concatenate([piece[...] for group in groups for piece in group], axis=0)
    head_width = weight_ref.shape[2]
    slot = padded(head_width)
    if slot == head_width:
        weights = jnp.concatenate([weight_ref[t] for t in range(3)], axis=1)
        products = [(0, jnp.dot(block, weights, preferred_element_type=F32).astype(BF16))]
    else:
        products = [
            (t * slot, jnp.dot(block, weight_ref[t], preferred_element_type=F32).astype(BF16))
            for t in range(3)
        ]
    at = 0
    for out_ref in outs:
        for left, product in products:
            part = product[at : at + out_ref.shape[0]]
            out_ref[:, left : left + part.shape[1]] = part
        at += out_ref.shape[0]


def project(groups, weights):
    width = groups[0][0].shape[1]
    slot = padded(weights.shape[2])
    sizes = [sum(piece.shape[0] for piece in group) for group in groups]
    total = sum(sizes)
    return pl.pallas_call(
        functools.partial(project_kernel, [len(group) for group in groups]),
        out_shape=[jax.ShapeDtypeStruct((size, 3 * slot), BF16) for size in sizes],
        in_specs=[VMEM] * (sum(len(group) for group in groups) + 1),
        out_specs=[VMEM] * len(groups),
        compiler_params=pltpu.CompilerParams(vmem_limit_bytes=24 << 20),
        cost_estimate=pl.CostEstimate(
            flops=2 * total * width * 3 * slot,
            bytes_accessed=2 * (total * width + weights.size + total * 3 * slot),
            transcendentals=0,
        ),
    )(*[piece for group in groups for piece in group], weights)


def attend_kernel(layout, ranges, head_width, *refs):
    parts = len(layout)
    blocks = refs[:parts]
    query_tags, key_tags, scale_ref = refs[parts : parts + 3]
    outs = refs[parts + 3 :]
    slot = padded(head_width)
    low, high = min(lo for lo, _ in ranges), max(hi for _, hi in ranges)
    heads = head_width // CHANNEL_PER_PART
    base = math.log2(math.e) / math.sqrt(CHANNEL_PER_PART)
    tiles = [None] * (slot // LANE)
    key_rows = key_tags[...]
    runs, query_rows, at = [], [], 0
    for block, (lo, hi) in zip(blocks, layout, strict=True):
        z = block.shape[0] // (hi - lo)
        first, last = max(low, lo), min(high, hi)
        if first < last:
            runs.append((block, (first - lo) * z, (last - lo) * z, z, first, last))
            query_rows.append(query_tags[at + (first - lo) * z : at + (last - lo) * z, :])
        at += block.shape[0]
    query_rows = jnp.concatenate(query_rows, axis=0)

    def span(head):
        first = head * CHANNEL_PER_PART
        last = first + CHANNEL_PER_PART
        left, right = first // LANE * LANE, padded(last)
        lane = lax.broadcasted_iota(jnp.int32, (1, right - left), 1)
        return left, right, (lane >= first - left) & (lane < last - left)

    def scores_of(head):
        left, right, inside = span(head)
        reps = (right - left) // LANE
        queries = jnp.concatenate([run[0][run[1] : run[2], left:right] for run in runs], axis=0)
        queries = jnp.where(inside, queries, jnp.concatenate([query_rows] * reps, axis=1))
        keys = jnp.concatenate([b[:, slot + left : slot + right] for b in blocks], axis=0)
        keys = jnp.where(inside, keys, jnp.concatenate([key_rows] * reps, axis=1))
        return lax.dot_general(queries, keys, (((1,), (1,)), ((), ())), preferred_element_type=F32)

    following = scores_of(0)
    for head in range(heads):
        scores = following
        if head + 1 < heads:
            following = scores_of(head + 1)
        left, right, inside = span(head)
        row_max = jnp.max(scores, axis=-1, keepdims=True)
        numerators = jnp.exp2((scores - row_max) * (scale_ref[head] * base))
        total = jnp.sum(numerators, axis=-1, keepdims=True)
        values = jnp.concatenate([b[:, 2 * slot + left : 2 * slot + right] for b in blocks], axis=0)
        mixed = jnp.dot(numerators.astype(BF16), values, preferred_element_type=F32) / total
        for i in range((right - left) // LANE):
            tile = left // LANE + i
            own = mixed[:, i * LANE : (i + 1) * LANE]
            held = tiles[tile]
            tiles[tile] = own if held is None else jnp.where(inside[:, i * LANE : (i + 1) * LANE], own, held)
    result = jnp.concatenate(tiles, axis=1)[:, :head_width].astype(BF16)
    places = {
        offset: (out_ref, offset - lo)
        for out_ref, (lo, hi) in zip(outs, ranges, strict=True)
        for offset in range(lo, hi)
    }
    into = dict.fromkeys(places, 0)
    at = 0
    for _, _, _, z, first, last in runs:
        for offset in range(first, last):
            out_ref, index = places[offset]
            out_ref[index, into[offset] : into[offset] + z, :] = result[at : at + z]
            into[offset] += z
            at += z


def attend(blocks, layout, query_tags, key_tags, scales, count, ranges, head_width):
    pixels = sum(block.shape[0] for block in blocks)
    per_offset = pixels // count
    asked = sum(hi - lo for lo, hi in ranges) * per_offset
    heads = head_width // CHANNEL_PER_PART
    return pl.pallas_call(
        functools.partial(attend_kernel, layout, ranges, head_width),
        out_shape=[
            jax.ShapeDtypeStruct((hi - lo, per_offset, head_width), BF16) for lo, hi in ranges
        ],
        in_specs=[VMEM] * (len(blocks) + 2) + [pl.BlockSpec(memory_space=pltpu.SMEM)],
        out_specs=[VMEM] * len(ranges),
        compiler_params=pltpu.CompilerParams(vmem_limit_bytes=28 << 20),
        cost_estimate=pl.CostEstimate(
            flops=4 * heads * asked * pixels * 2 * LANE,
            bytes_accessed=2 * pixels * 3 * padded(head_width),
            transcendentals=heads * asked * pixels,
        ),
    )(*blocks, query_tags, key_tags, scales)


def product(attended, weights, columns=slice(None)):
    rows = jnp.concatenate([piece[...] for piece in attended], axis=1)
    depth = jnp.concatenate([weight[:, columns] for weight in weights], axis=0)
    return jnp.dot(rows, depth, preferred_element_type=F32)


def partial_kernel(count, spans, *refs):
    attended, weights = refs[:count], refs[count : 2 * count]
    done_ref, *sources, out_ref, mixed_ref, semaphore = refs[2 * count :]
    copy = pltpu.make_async_copy(
        done_ref, mixed_ref.at[:, pl.ds(0, done_ref.shape[1]), :], semaphore.at[0]
    )
    copy.start()
    total = product(attended, weights)
    at = 0
    for which, row, start, pixels in spans:
        held = sources[which][row, start : start + pixels, :].astype(F32)
        out_ref[at : at + pixels, :] = held + total[at : at + pixels]
        at += pixels
    copy.wait()


def partial(attended, weights, done, sources, spans, shape):
    pixels, depth = attended[0].shape
    width = weights[0].shape[1]
    return pl.pallas_call(
        functools.partial(partial_kernel, len(weights), spans),
        out_shape=[jax.ShapeDtypeStruct((pixels, width), F32), jax.ShapeDtypeStruct(shape, BF16)],
        in_specs=[VMEM] * (2 * len(weights) + 1 + len(sources)),
        out_specs=[VMEM, HELD],
        scratch_shapes=[pltpu.SemaphoreType.DMA((1,))],
        compiler_params=pltpu.CompilerParams(vmem_limit_bytes=20 << 20),
        cost_estimate=pl.CostEstimate(
            flops=2 * pixels * width * depth * len(weights), bytes_accessed=2 * width * (depth + 2 * pixels), transcendentals=0
        ),
    )(*attended, *weights, done, *sources)


def finish_kernel(count, spans, *refs):
    attended, weights, sources, out_ref = refs[:count], refs[count : 2 * count], refs[2 * count : -1], refs[-1]
    total = product(attended, weights)
    at = 0
    for which, row, start, pixels, into, column in spans:
        held = sources[which][row, start : start + pixels, :].astype(F32)
        out_ref[into, column : column + pixels, :] = (held + total[at : at + pixels]).astype(BF16)
        at += pixels


def finish(attended, weights, sources, spans, shape):
    count = len(weights)
    pixels, width = attended[0].shape[0], shape[-1]
    return pl.pallas_call(
        functools.partial(finish_kernel, count, spans),
        out_shape=jax.ShapeDtypeStruct(shape, BF16),
        in_specs=[VMEM] * (2 * count + len(sources)),
        out_specs=VMEM,
        compiler_params=pltpu.CompilerParams(vmem_limit_bytes=20 << 20),
        cost_estimate=pl.CostEstimate(
            flops=2 * pixels * width * width, bytes_accessed=2 * width * (width + 3 * pixels), transcendentals=0
        ),
    )(*attended, *weights, *sources)


def last_kernel(count, chunks, spans, *refs):
    attended, weights = refs[:count], refs[count : 2 * count]
    base_ref, _, out_ref, ready, semaphore = refs[2 * count :]
    size, width = ready.shape[1], ready.shape[2]
    left = out_ref.shape[1] - size
    wide = width // chunks
    copies = []
    for chunk in range(chunks):
        columns = slice(chunk * wide, (chunk + 1) * wide)
        total = (product(attended, weights, columns) + base_ref[:, columns]).astype(BF16)
        at = 0
        for pixels, into, column in spans:
            ready[into, column - left : column - left + pixels, columns] = total[at : at + pixels]
            at += pixels
        place = pl.ds(chunk * wide, wide)
        copy = pltpu.make_async_copy(
            ready.at[:, :, place], out_ref.at[:, pl.ds(left, size), place], semaphore.at[chunk]
        )
        copy.start()
        copies.append(copy)
    for copy in copies:
        copy.wait()


def finish_last(attended, weights, base, mixed, done_columns, spans):
    count = len(weights)
    row_count, col_count, width = mixed.shape
    pixels, depth = attended[0].shape
    chunks = 3 if width % (3 * 2 * LANE) == 0 else 1
    return pl.pallas_call(
        functools.partial(last_kernel, count, chunks, spans),
        out_shape=jax.ShapeDtypeStruct(mixed.shape, BF16),
        in_specs=[VMEM] * (2 * count + 1) + [HELD],
        out_specs=HELD,
        input_output_aliases={2 * count + 1: 0},
        scratch_shapes=[
            pltpu.VMEM((row_count, col_count - done_columns, width), BF16),
            pltpu.SemaphoreType.DMA((chunks,)),
        ],
        compiler_params=pltpu.CompilerParams(vmem_limit_bytes=20 << 20),
        cost_estimate=pl.CostEstimate(
            flops=2 * pixels * width * depth * count, bytes_accessed=2 * width * (width + 3 * pixels), transcendentals=0
        ),
    )(*attended, *weights, base, mixed)


def send_heads(outs):
    own = [outs[0]]
    for offset in range(1, len(outs)):
        own.append(exchange(outs[offset], offset))
    return [piece[0] for piece in own]


def pick_kernel(place, source_ref, out_ref, semaphore):
    size = out_ref.shape[0]
    start = pl.multiple_of(place() * size, 16)
    copy = pltpu.make_async_copy(source_ref.at[pl.ds(start, size), :], out_ref, semaphore)
    copy.start()
    copy.wait()


def join_kernel(place, own_ref, other_ref, out_ref):
    size = own_ref.shape[0]
    at = place()
    out_ref[pl.ds(pl.multiple_of(at * size, 16), size), :] = own_ref[...]
    out_ref[pl.ds(pl.multiple_of((1 - at) * size, 16), size), :] = other_ref[...]


def small_call(kernel, rows, *operands, spec=VMEM, scratch=()):
    width = operands[0].shape[1]
    return pl.pallas_call(
        kernel,
        out_shape=jax.ShapeDtypeStruct((rows, width), BF16),
        in_specs=[spec] * len(operands),
        out_specs=VMEM,
        scratch_shapes=scratch,
        compiler_params=pltpu.CompilerParams(vmem_limit_bytes=8 << 20),
        cost_estimate=pl.CostEstimate(flops=0, bytes_accessed=4 * rows * width, transcendentals=0),
    )(*operands)


def gather_weights(block):
    levels = []
    rows = block.shape[0]
    for axis in ("win", "member"):
        if lax.axis_size(axis) % 2 == 0 and rows % (32 << len(levels)) == 0:
            levels.append(axis)

    def bit(axis):
        return lax.axis_index(axis) & 1

    def part_index():
        index = 0
        for axis in levels:
            index = index * 2 + bit(axis)
        return index

    pieces = {0: block}
    for mask in masks_of(lax.axis_size("seq")):
        for offset in list(pieces):
            piece = pieces[offset]
            if mask > 1 and levels:
                size = rows >> len(levels)
                part = small_call(
                    functools.partial(pick_kernel, part_index),
                    size,
                    piece,
                    spec=HELD,
                    scratch=[pltpu.SemaphoreType.DMA],
                )
                part = exchange(part, mask)
                for axis in reversed(levels):
                    other = exchange(part, 1, axis)
                    size *= 2
                    part = small_call(functools.partial(join_kernel, functools.partial(bit, axis)), size, part, other)
                pieces[offset ^ mask] = part
            else:
                pieces[offset ^ mask] = exchange(piece, mask)
    return [pieces[offset] for offset in range(len(pieces))]


def on_device(
    pixel_grid_input,
    mask_zone_labeling,
    standardize_multiplier,
    standardize_offset_vector,
    triple_projection_matrix,
    logit_scaling_per_part,
    final_projection_matrix,
):
    count = lax.axis_size("seq")
    blocked = pixel_grid_input[0, :, 0]
    row_count, col_count, width = blocked.shape
    rows = row_count // 2
    half = WS // 2
    head_width = triple_projection_matrix.shape[2]

    def west(source, count):
        return (source - 2) % count

    def west_north(source, count):
        return ((source ^ 1) - 2) % count

    near = WS - half
    gain, bias = standardize_multiplier, standardize_offset_vector
    weights = triple_projection_matrix
    scales = logit_scaling_per_part

    local_0 = blocked[rows:, half : half + WS]
    boxes = [
        (rows, half + WS, near),
        (0, half, WS),
        (0, half + WS, near),
        (rows, 0, half),
        (0, 0, half),
    ]
    local_1, south_0, south_1, east, corner = cut(blocked, rows, boxes)
    south_0 = exchange(south_0, 1, "win")
    south_1 = exchange(south_1, 1, "win")
    east = permute_by(east, "win", west)
    corner = permute_by(corner, "win", west_north)
    local_0_pieces = gather_pieces(local_0)
    local_1_pieces = gather_pieces(local_1)
    query_0, key_0, query_1, key_1 = region_tags(mask_zone_labeling[0], weights, count, near)
    out_weights = gather_weights(final_projection_matrix)

    spans = [(0, row, 0, WS) for row in range(rows)]
    (south_normed,) = norm([south_0], gain, bias, [spans])
    south_pieces = gather_pieces(south_normed)
    spans = [(piece, row, 0, WS) for piece in range(count) for row in range(rows)]
    (local_0_normed,) = norm(local_0_pieces, gain, bias, [spans])
    (local_0,) = project([[local_0_normed]], weights)
    spans = [(0, row, 0, near) for row in range(rows)]
    spans += [(which, row, 0, half) for which in (1, 2) for row in range(rows)]
    (rest_normed,) = norm([south_1, east, corner], gain, bias, [spans])
    rest_pieces = gather_pieces(rest_normed)
    split = count // 2
    near_lanes, far_lanes, all_lanes = (0, split), (split, count), (0, count)
    spans = [(piece, row, 0, near) for piece in range(count) for row in range(rows)]
    (local_1_normed,) = norm(local_1_pieces, gain, bias, [spans])
    south_near, local_1 = project([south_pieces[:split], [local_1_normed]], weights)
    south_pieces[split] = after(south_pieces[split], south_near)
    (south_far,) = project([south_pieces[split:]], weights)
    (rest_near,) = project([rest_pieces[:split]], weights)

    def attend_run(blocks, layout, tags, earlier, lo, hi):
        blocks = [after(blocks[0], *earlier), *blocks[1:]]
        singles = [(i, i + 1) for i in range(lo, hi)]
        return list(attend(blocks, layout, *tags, scales, count, singles, head_width))

    blocks, layout, tags = [local_0, south_near, south_far], [all_lanes, near_lanes, far_lanes], (query_0, key_0)
    outs_0 = attend_run(blocks, layout, tags, [], 0, count)
    rest_pieces[split] = after(rest_pieces[split], *outs_0)
    (rest_far,) = project([rest_pieces[split:]], weights)
    blocks, layout, tags = [local_1, rest_near, rest_far], [all_lanes, near_lanes, far_lanes], (query_1, key_1)
    far = attend_run(blocks, layout, tags, [], split, count)
    close = attend_run(blocks, layout, tags, far, 0, split)
    outs_1 = close + far

    first = send_heads(outs_0)
    second = send_heads(outs_1)
    first[0] = after(first[0], *outs_1)
    spans = [(0, rows + row, half, WS, row, 0) for row in range(rows)]
    spans += [(1, row, 0, WS, rows + row, 0) for row in range(rows)]
    shape = (row_count, col_count, width)
    done = finish(first, out_weights, [blocked, south_0], spans, (row_count, WS, width))
    second[0] = after(second[0], done)
    spans = [(0, rows + row, half + WS, near, row, WS) for row in range(rows)]
    spans += [(1, row, 0, near, rows + row, WS) for row in range(rows)]
    spans += [(2, row, 0, half, row, WS + near) for row in range(rows)]
    spans += [(3, row, 0, half, rows + row, WS + near) for row in range(rows)]
    sources = [blocked, south_1, east, corner]
    base, mixed = partial(second[:-1], out_weights[:-1], done, sources, [span[:4] for span in spans], shape)
    spans = [span[3:] for span in spans]
    mixed = finish_last(second[-1:], out_weights[-1:], base, mixed, WS, spans)
    return mixed[None, :, None]


def solution(mesh):
    in_specs = (
        P(("member", "win"), None, "seq", None, None),
        P(("member", "win"), None, None),
        P(),
        P(),
        P(None, None, "seq"),
        P("seq"),
        P("seq", None),
    )
    out_specs = P(("member", "win"), None, "seq", None, None)

    return jax.shard_map(on_device, mesh=mesh, in_specs=in_specs, out_specs=out_specs, check_vma=False)
```

```python
import functools
import math

import jax
import jax.numpy as jnp
from jax import lax
from jax.experimental import pallas as pl
from jax.experimental.pallas import tpu as pltpu
from jax.sharding import PartitionSpec as P


CHANNEL_PER_PART = 96
WS = 32
REGIONS = 32
LANE = 128
FAR = -1e30
F32 = jnp.float32
BF16 = jnp.bfloat16


def permute_by(value, axis, move):
    count = lax.axis_size(axis)
    pairs = [(source, move(source, count)) for source in range(count)]
    return lax.ppermute(value, axis, pairs)


def exchange(value, mask, axis="seq"):
    return permute_by(value, axis, lambda source, count: source ^ mask)


def masks_of(count):
    masks = []
    while count > 1:
        count //= 2
        masks.append(count)
    return masks


def gather_pieces(piece):
    pieces = {0: piece}
    for mask in masks_of(lax.axis_size("seq")):
        for offset in list(pieces):
            pieces[offset ^ mask] = exchange(pieces[offset], mask)
    return [pieces[offset] for offset in range(len(pieces))]


def padded(width):
    return (width + LANE - 1) // LANE * LANE


VMEM = pl.BlockSpec(memory_space=pltpu.VMEM)


def after(value, *earlier):
    return lax.optimization_barrier((value, *earlier))[0]


def normalized(held, gain, bias):
    values = held.astype(F32)
    average = jnp.mean(values, axis=-1, keepdims=True)
    centred = values - average
    variance = jnp.mean(centred * centred, axis=-1, keepdims=True)
    return (centred * lax.rsqrt(variance + 1e-05) * gain + bias).astype(BF16)


HELD = pl.BlockSpec(memory_space=pltpu.HBM)


def cut_kernel(boxes, pixel_ref, *outs):
    for (row, left, size), out_ref in zip(boxes, outs, strict=True):
        out_ref[...] = pixel_ref[row : row + out_ref.shape[0], left : left + size, :]


def cut(pixels, rows, boxes):
    width = pixels.shape[2]
    return pl.pallas_call(
        functools.partial(cut_kernel, boxes),
        out_shape=[jax.ShapeDtypeStruct((rows, size, width), BF16) for _, _, size in boxes],
        in_specs=[VMEM],
        out_specs=[VMEM] * len(boxes),
        compiler_params=pltpu.CompilerParams(vmem_limit_bytes=8 << 20),
        cost_estimate=pl.CostEstimate(flops=0, bytes_accessed=2 * pixels.size, transcendentals=0),
        name="cut",
    )(pixels)


def norm_kernel(groups, *refs):
    refs, outs = refs[: -len(groups)], refs[-len(groups) :]
    *sources, gain_ref, bias_ref = refs
    gain, bias = gain_ref[...][None], bias_ref[...][None]
    for spans, out_ref in zip(groups, outs, strict=True):
        into = 0
        for which, row, left, size in spans:
            held = sources[which][row, left : left + size, :]
            out_ref[into : into + size, :] = normalized(held, gain, bias)
            into += size


def norm(sources, gain, bias, groups):
    width = sources[0].shape[-1]
    totals = [sum(span[-1] for span in spans) for spans in groups]
    return pl.pallas_call(
        functools.partial(norm_kernel, groups),
        out_shape=[jax.ShapeDtypeStruct((total, width), BF16) for total in totals],
        in_specs=[VMEM] * (len(sources) + 2),
        out_specs=[VMEM] * len(groups),
        compiler_params=pltpu.CompilerParams(vmem_limit_bytes=8 << 20),
        cost_estimate=pl.CostEstimate(
            flops=10 * sum(totals) * width, bytes_accessed=4 * sum(totals) * width, transcendentals=0
        ),
    )(*sources, gain, bias)


def tag_kernel(count, near, label_ref, weight_ref, *outs):
    del weight_ref
    query_0, key_0, query_1, key_1 = outs
    row_count, _ = label_ref.shape
    rows = row_count // (2 * count)
    device = lax.axis_index("seq")
    turned = jnp.transpose(label_ref[...].astype(F32)).astype(BF16)
    place = lax.broadcasted_iota(jnp.int32, (row_count, LANE), 0)
    lane = (lax.broadcasted_iota(jnp.int32, (1, LANE), 1) % REGIONS).astype(F32)
    group = count * rows
    for half in range(2):
        for offset in range(count):
            for row in range(rows):
                at = (half * rows + row) * count + jnp.bitwise_xor(device, offset)
                chosen = jnp.where(place == at, 1.0, 0.0).astype(BF16)
                region = jnp.dot(turned, chosen, preferred_element_type=F32)
                same = region == lane
                query = jnp.where(same, 1.0, 0.0).astype(BF16)
                key = jnp.where(same, 0.0, FAR).astype(BF16)
                slot = offset * rows + row
                apart, span = group * near, near + 2 * (WS - near)
                beside = apart + offset * rows * span
                spots = [
                    (query_0, key_0, (half * group + slot) * WS, 0, WS),
                    (query_1, key_1, beside + row * near if half else slot * near, WS, near),
                    (
                        query_1,
                        key_1,
                        beside + rows * near + (half * rows + row) * (WS - near),
                        WS + near,
                        WS - near,
                    ),
                ]
                for query_ref, key_ref, into, left, size in spots:
                    query_ref[into : into + size, :] = query[left : left + size]
                    key_ref[into : into + size, :] = key[left : left + size]


def region_tags(labels, weights, count, near):
    pixels = labels.shape[0] * WS
    return pl.pallas_call(
        functools.partial(tag_kernel, count, near),
        out_shape=[jax.ShapeDtypeStruct((pixels, LANE), BF16)] * 4,
        in_specs=[VMEM] * 2,
        out_specs=[VMEM] * 4,
        compiler_params=pltpu.CompilerParams(vmem_limit_bytes=8 << 20),
        cost_estimate=pl.CostEstimate(
            flops=8 * pixels * LANE * labels.shape[0], bytes_accessed=8 * pixels * LANE, transcendentals=0
        ),
        name="tags",
    )(labels, weights)


def project_kernel(counts, *refs):
    groups = []
    for count in counts:
        groups.append(refs[:count])
        refs = refs[count:]
    weight_ref, *outs = refs
    block = jnp.concatenate([piece[...] for group in groups for piece in group], axis=0)
    head_width = weight_ref.shape[2]
    slot = padded(head_width)
    if slot == head_width:
        weights = jnp.concatenate([weight_ref[t] for t in range(3)], axis=1)
        products = [(0, jnp.dot(block, weights, preferred_element_type=F32).astype(BF16))]
    else:
        products = [
            (t * slot, jnp.dot(block, weight_ref[t], preferred_element_type=F32).astype(BF16))
            for t in range(3)
        ]
    at = 0
    for out_ref in outs:
        for left, product in products:
            part = product[at : at + out_ref.shape[0]]
            out_ref[:, left : left + part.shape[1]] = part
        at += out_ref.shape[0]


def project(groups, weights):
    width = groups[0][0].shape[1]
    slot = padded(weights.shape[2])
    sizes = [sum(piece.shape[0] for piece in group) for group in groups]
    total = sum(sizes)
    return pl.pallas_call(
        functools.partial(project_kernel, [len(group) for group in groups]),
        out_shape=[jax.ShapeDtypeStruct((size, 3 * slot), BF16) for size in sizes],
        in_specs=[VMEM] * (sum(len(group) for group in groups) + 1),
        out_specs=[VMEM] * len(groups),
        compiler_params=pltpu.CompilerParams(vmem_limit_bytes=24 << 20),
        cost_estimate=pl.CostEstimate(
            flops=2 * total * width * 3 * slot,
            bytes_accessed=2 * (total * width + weights.size + total * 3 * slot),
            transcendentals=0,
        ),
    )(*[piece for group in groups for piece in group], weights)


def attend_kernel(layout, ranges, head_width, *refs):
    parts = len(layout)
    blocks = refs[:parts]
    query_tags, key_tags, scale_ref = refs[parts : parts + 3]
    outs = refs[parts + 3 :]
    slot = padded(head_width)
    low, high = min(lo for lo, _ in ranges), max(hi for _, hi in ranges)
    heads = head_width // CHANNEL_PER_PART
    base = math.log2(math.e) / math.sqrt(CHANNEL_PER_PART)
    tiles = [None] * (slot // LANE)
    key_rows = key_tags[...]
    runs, query_rows, at = [], [], 0
    for block, (lo, hi) in zip(blocks, layout, strict=True):
        z = block.shape[0] // (hi - lo)
        first, last = max(low, lo), min(high, hi)
        if first < last:
            runs.append((block, (first - lo) * z, (last - lo) * z, z, first, last))
            query_rows.append(query_tags[at + (first - lo) * z : at + (last - lo) * z, :])
        at += block.shape[0]
    query_rows = jnp.concatenate(query_rows, axis=0)

    def span(head):
        first = head * CHANNEL_PER_PART
        last = first + CHANNEL_PER_PART
        left, right = first // LANE * LANE, padded(last)
        lane = lax.broadcasted_iota(jnp.int32, (1, right - left), 1)
        return left, right, (lane >= first - left) & (lane < last - left)

    def scores_of(head):
        left, right, inside = span(head)
        reps = (right - left) // LANE
        queries = jnp.concatenate([run[0][run[1] : run[2], left:right] for run in runs], axis=0)
        queries = jnp.where(inside, queries, jnp.concatenate([query_rows] * reps, axis=1))
        keys = jnp.concatenate([b[:, slot + left : slot + right] for b in blocks], axis=0)
        keys = jnp.where(inside, keys, jnp.concatenate([key_rows] * reps, axis=1))
        return lax.dot_general(queries, keys, (((1,), (1,)), ((), ())), preferred_element_type=F32)

    following = scores_of(0)
    for head in range(heads):
        scores = following
        if head + 1 < heads:
            following = scores_of(head + 1)
        left, right, inside = span(head)
        row_max = jnp.max(scores, axis=-1, keepdims=True)
        numerators = jnp.exp2((scores - row_max) * (scale_ref[head] * base))
        total = jnp.sum(numerators, axis=-1, keepdims=True)
        values = jnp.concatenate([b[:, 2 * slot + left : 2 * slot + right] for b in blocks], axis=0)
        mixed = jnp.dot(numerators.astype(BF16), values, preferred_element_type=F32) / total
        for i in range((right - left) // LANE):
            tile = left // LANE + i
            own = mixed[:, i * LANE : (i + 1) * LANE]
            held = tiles[tile]
            tiles[tile] = own if held is None else jnp.where(inside[:, i * LANE : (i + 1) * LANE], own, held)
    result = jnp.concatenate(tiles, axis=1)[:, :head_width].astype(BF16)
    places = {
        offset: (out_ref, offset - lo)
        for out_ref, (lo, hi) in zip(outs, ranges, strict=True)
        for offset in range(lo, hi)
    }
    into = dict.fromkeys(places, 0)
    at = 0
    for _, _, _, z, first, last in runs:
        for offset in range(first, last):
            out_ref, index = places[offset]
            out_ref[index, into[offset] : into[offset] + z, :] = result[at : at + z]
            into[offset] += z
            at += z


def attend(blocks, layout, query_tags, key_tags, scales, count, ranges, head_width):
    pixels = sum(block.shape[0] for block in blocks)
    per_offset = pixels // count
    asked = sum(hi - lo for lo, hi in ranges) * per_offset
    heads = head_width // CHANNEL_PER_PART
    return pl.pallas_call(
        functools.partial(attend_kernel, layout, ranges, head_width),
        out_shape=[
            jax.ShapeDtypeStruct((hi - lo, per_offset, head_width), BF16) for lo, hi in ranges
        ],
        in_specs=[VMEM] * (len(blocks) + 2) + [pl.BlockSpec(memory_space=pltpu.SMEM)],
        out_specs=[VMEM] * len(ranges),
        compiler_params=pltpu.CompilerParams(vmem_limit_bytes=28 << 20),
        cost_estimate=pl.CostEstimate(
            flops=4 * heads * asked * pixels * 2 * LANE,
            bytes_accessed=2 * pixels * 3 * padded(head_width),
            transcendentals=heads * asked * pixels,
        ),
    )(*blocks, query_tags, key_tags, scales)


def product(attended, weights, columns=slice(None)):
    rows = jnp.concatenate([piece[...] for piece in attended], axis=1)
    depth = jnp.concatenate([weight[:, columns] for weight in weights], axis=0)
    return jnp.dot(rows, depth, preferred_element_type=F32)


def partial_kernel(count, spans, *refs):
    attended, weights, sources, out_ref = refs[:count], refs[count : 2 * count], refs[2 * count : -1], refs[-1]
    total = product(attended, weights)
    at = 0
    for which, row, start, pixels in spans:
        held = sources[which][row, start : start + pixels, :].astype(F32)
        out_ref[at : at + pixels, :] = held + total[at : at + pixels]
        at += pixels


def partial(attended, weights, sources, spans):
    pixels, depth = attended[0].shape
    width = weights[0].shape[1]
    return pl.pallas_call(
        functools.partial(partial_kernel, len(weights), spans),
        out_shape=jax.ShapeDtypeStruct((pixels, width), F32),
        in_specs=[VMEM] * (2 * len(weights) + len(sources)),
        out_specs=VMEM,
        compiler_params=pltpu.CompilerParams(vmem_limit_bytes=20 << 20),
        cost_estimate=pl.CostEstimate(
            flops=2 * pixels * width * depth * len(weights), bytes_accessed=2 * width * (depth + 2 * pixels), transcendentals=0
        ),
    )(*attended, *weights, *sources)


def finish_kernel(count, spans, *refs):
    attended, weights, sources, out_ref = refs[:count], refs[count : 2 * count], refs[2 * count : -1], refs[-1]
    total = product(attended, weights)
    at = 0
    for which, row, start, pixels, into, column in spans:
        held = sources[which][row, start : start + pixels, :].astype(F32)
        out_ref[into, column : column + pixels, :] = (held + total[at : at + pixels]).astype(BF16)
        at += pixels


def finish(attended, weights, sources, spans, shape):
    count = len(weights)
    pixels, width = attended[0].shape[0], shape[-1]
    return pl.pallas_call(
        functools.partial(finish_kernel, count, spans),
        out_shape=jax.ShapeDtypeStruct(shape, BF16),
        in_specs=[VMEM] * (2 * count + len(sources)),
        out_specs=VMEM,
        compiler_params=pltpu.CompilerParams(vmem_limit_bytes=20 << 20),
        cost_estimate=pl.CostEstimate(
            flops=2 * pixels * width * width, bytes_accessed=2 * width * (width + 3 * pixels), transcendentals=0
        ),
    )(*attended, *weights, *sources)


def last_kernel(count, chunks, spans, *refs):
    attended, weights = refs[:count], refs[count : 2 * count]
    base_ref, done_ref, out_ref, ready, semaphore = refs[2 * count :]
    left, size, width = done_ref.shape[1], ready.shape[1], ready.shape[2]
    wide = width // chunks
    copies = [
        pltpu.make_async_copy(done_ref, out_ref.at[:, pl.ds(0, left), :], semaphore.at[chunks])
    ]
    copies[0].start()
    for chunk in range(chunks):
        columns = slice(chunk * wide, (chunk + 1) * wide)
        total = (product(attended, weights, columns) + base_ref[:, columns]).astype(BF16)
        at = 0
        for pixels, into, column in spans:
            ready[into, column - left : column - left + pixels, columns] = total[at : at + pixels]
            at += pixels
        place = pl.ds(chunk * wide, wide)
        copy = pltpu.make_async_copy(
            ready.at[:, :, place], out_ref.at[:, pl.ds(left, size), place], semaphore.at[chunk]
        )
        copy.start()
        copies.append(copy)
    for copy in copies:
        copy.wait()


def finish_last(attended, weights, base, done, spans, shape):
    count = len(weights)
    row_count, col_count, width = shape
    pixels, depth = attended[0].shape
    chunks = 1
    return pl.pallas_call(
        functools.partial(last_kernel, count, chunks, spans),
        out_shape=jax.ShapeDtypeStruct(shape, BF16),
        in_specs=[VMEM] * (2 * count + 2),
        out_specs=HELD,
        scratch_shapes=[
            pltpu.VMEM((row_count, col_count - done.shape[1], width), BF16),
            pltpu.SemaphoreType.DMA((chunks + 1,)),
        ],
        compiler_params=pltpu.CompilerParams(vmem_limit_bytes=20 << 20),
        cost_estimate=pl.CostEstimate(
            flops=2 * pixels * width * depth * count, bytes_accessed=2 * width * (width + 3 * pixels), transcendentals=0
        ),
    )(*attended, *weights, base, done)


def send_heads(outs):
    own = [outs[0]]
    for offset in range(1, len(outs)):
        own.append(exchange(outs[offset], offset))
    return [piece[0] for piece in own]


def pick_kernel(place, source_ref, out_ref, semaphore):
    size = out_ref.shape[0]
    start = pl.multiple_of(place() * size, 16)
    copy = pltpu.make_async_copy(source_ref.at[pl.ds(start, size), :], out_ref, semaphore)
    copy.start()
    copy.wait()


def join_kernel(place, own_ref, other_ref, out_ref):
    size = own_ref.shape[0]
    at = place()
    out_ref[pl.ds(pl.multiple_of(at * size, 16), size), :] = own_ref[...]
    out_ref[pl.ds(pl.multiple_of((1 - at) * size, 16), size), :] = other_ref[...]


def small_call(kernel, rows, *operands, spec=VMEM, scratch=()):
    width = operands[0].shape[1]
    return pl.pallas_call(
        kernel,
        out_shape=jax.ShapeDtypeStruct((rows, width), BF16),
        in_specs=[spec] * len(operands),
        out_specs=VMEM,
        scratch_shapes=scratch,
        compiler_params=pltpu.CompilerParams(vmem_limit_bytes=8 << 20),
        cost_estimate=pl.CostEstimate(flops=0, bytes_accessed=4 * rows * width, transcendentals=0),
    )(*operands)


def gather_weights(block):
    levels = []
    rows = block.shape[0]
    for axis in ("win", "member"):
        if lax.axis_size(axis) % 2 == 0 and rows % (32 << len(levels)) == 0:
            levels.append(axis)

    def bit(axis):
        return lax.axis_index(axis) & 1

    def part_index():
        index = 0
        for axis in levels:
            index = index * 2 + bit(axis)
        return index

    pieces = {0: block}
    for mask in masks_of(lax.axis_size("seq")):
        for offset in list(pieces):
            piece = pieces[offset]
            if mask > 1 and levels:
                size = rows >> len(levels)
                part = small_call(
                    functools.partial(pick_kernel, part_index),
                    size,
                    piece,
                    spec=HELD,
                    scratch=[pltpu.SemaphoreType.DMA],
                )
                part = exchange(part, mask)
                for axis in reversed(levels):
                    other = exchange(part, 1, axis)
                    size *= 2
                    part = small_call(functools.partial(join_kernel, functools.partial(bit, axis)), size, part, other)
                pieces[offset ^ mask] = part
            else:
                pieces[offset ^ mask] = exchange(piece, mask)
    return [pieces[offset] for offset in range(len(pieces))]


def on_device(
    pixel_grid_input,
    mask_zone_labeling,
    standardize_multiplier,
    standardize_offset_vector,
    triple_projection_matrix,
    logit_scaling_per_part,
    final_projection_matrix,
):
    count = lax.axis_size("seq")
    blocked = pixel_grid_input[0, :, 0]
    row_count, col_count, width = blocked.shape
    rows = row_count // 2
    half = WS // 2
    head_width = triple_projection_matrix.shape[2]

    def west(source, count):
        return (source - 2) % count

    def west_north(source, count):
        return ((source ^ 1) - 2) % count

    near = WS - half
    gain, bias = standardize_multiplier, standardize_offset_vector
    weights = triple_projection_matrix
    scales = logit_scaling_per_part

    local_0 = blocked[rows:, half : half + WS]
    boxes = [
        (rows, half + WS, near),
        (0, half, WS),
        (0, half + WS, near),
        (rows, 0, half),
        (0, 0, half),
    ]
    local_1, south_0, south_1, east, corner = cut(blocked, rows, boxes)
    south_0 = exchange(south_0, 1, "win")
    south_1 = exchange(south_1, 1, "win")
    east = permute_by(east, "win", west)
    corner = permute_by(corner, "win", west_north)
    local_0_pieces = gather_pieces(local_0)
    local_1_pieces = gather_pieces(local_1)
    query_0, key_0, query_1, key_1 = region_tags(mask_zone_labeling[0], weights, count, near)
    out_weights = gather_weights(final_projection_matrix)

    spans = [(0, row, 0, WS) for row in range(rows)]
    (south_normed,) = norm([south_0], gain, bias, [spans])
    south_pieces = gather_pieces(south_normed)
    spans = [(piece, row, 0, WS) for piece in range(count) for row in range(rows)]
    (local_0_normed,) = norm(local_0_pieces, gain, bias, [spans])
    (local_0,) = project([[local_0_normed]], weights)
    spans = [(0, row, 0, near) for row in range(rows)]
    spans += [(which, row, 0, half) for which in (1, 2) for row in range(rows)]
    (rest_normed,) = norm([south_1, east, corner], gain, bias, [spans])
    rest_pieces = gather_pieces(rest_normed)
    split = count // 2
    near_lanes, far_lanes, all_lanes = (0, split), (split, count), (0, count)
    spans = [(piece, row, 0, near) for piece in range(count) for row in range(rows)]
    (local_1_normed,) = norm(local_1_pieces, gain, bias, [spans])
    south_near, local_1 = project([south_pieces[:split], [local_1_normed]], weights)
    south_pieces[split] = after(south_pieces[split], south_near)
    (south_far,) = project([south_pieces[split:]], weights)
    (rest_near,) = project([rest_pieces[:split]], weights)

    def attend_run(blocks, layout, tags, earlier, lo, hi):
        blocks = [after(blocks[0], *earlier), *blocks[1:]]
        singles = [(i, i + 1) for i in range(lo, hi)]
        return list(attend(blocks, layout, *tags, scales, count, singles, head_width))

    blocks, layout, tags = [local_0, south_near, south_far], [all_lanes, near_lanes, far_lanes], (query_0, key_0)
    outs_0 = attend_run(blocks, layout, tags, [], 0, count)
    rest_pieces[split] = after(rest_pieces[split], *outs_0)
    (rest_far,) = project([rest_pieces[split:]], weights)
    blocks, layout, tags = [local_1, rest_near, rest_far], [all_lanes, near_lanes, far_lanes], (query_1, key_1)
    far = attend_run(blocks, layout, tags, [], split, count)
    close = attend_run(blocks, layout, tags, far, 0, split)
    outs_1 = close + far

    first = send_heads(outs_0)
    second = send_heads(outs_1)
    first[0] = after(first[0], *outs_1)
    spans = [(0, rows + row, half, WS, row, 0) for row in range(rows)]
    spans += [(1, row, 0, WS, rows + row, 0) for row in range(rows)]
    shape = (row_count, col_count, width)
    done = finish(first, out_weights, [blocked, south_0], spans, (row_count, WS, width))
    second[0] = after(second[0], done)
    spans = [(0, rows + row, half + WS, near, row, WS) for row in range(rows)]
    spans += [(1, row, 0, near, rows + row, WS) for row in range(rows)]
    spans += [(2, row, 0, half, row, WS + near) for row in range(rows)]
    spans += [(3, row, 0, half, rows + row, WS + near) for row in range(rows)]
    sources = [blocked, south_1, east, corner]
    base = partial(second[:-1], out_weights[:-1], sources, [span[:4] for span in spans])
    spans = [span[3:] for span in spans]
    mixed = finish_last(second[-1:], out_weights[-1:], base, done, spans, shape)
    return mixed[None, :, None]


def solution(mesh):
    in_specs = (
        P(("member", "win"), None, "seq", None, None),
        P(("member", "win"), None, None),
        P(),
        P(),
        P(None, None, "seq"),
        P("seq"),
        P("seq", None),
    )
    out_specs = P(("member", "win"), None, "seq", None, None)

    return jax.shard_map(on_device, mesh=mesh, in_specs=in_specs, out_specs=out_specs, check_vma=False)
```
